128 devices in a mesh: seq: 8 (over z, core), tp: 16 (over x, y).
Axes of the slice: x: 4, y: 4, z: 4, core: 2. Of those that a mesh axis runs over, the one named last changes fastest.
Arguments:
- sequence_in: bfloat16 [1536, 4096], P('tp', 'seq')
- conv_weight: bfloat16 [3, 1536, 3, 1536], P(None, 'tp')
- norm_gain: float32 [3, 1536], P(None, 'tp'), may hold values from 0.1 to 1.9
- tissue_scale: float32 [367, 1536], replicated, may hold values from 0.3 to 3
- donor_offset: int32 [2048], P('seq'), may hold values from 0 to 511
- acceptor_owner: int32 [2048, 1], P('seq'), may hold values from 0 to 7; in each aligned block of 256 rows (0 to 255, 256 to 511, ...) at most 128 rows name the same one
- acceptor_offset: int32 [2048], P('seq'), may hold values from 0 to 511
- tissue: int32 [2048], P('seq'), may hold values from 0 to 366
- tower_grad: float32 [1536, 4096], P('tp', 'seq'), may hold values from -6 to 6
- score_grad: float32 [2048], P('seq'), may hold values from -24 to 24
Outputs:
- scores: float32 [2048], P('seq')
- input_grad: float32 [1536, 4096], P('tp', 'seq')
- weight_grad: float32 [3, 1536, 3, 1536], P(None, 'tp')
- gain_grad: float32 [3, 1536], P(None, 'tp')
The draws below stay inside these ranges and needn't reach their ends.
Inputs may be any that keep to these rules, and one draw needn't show every extreme that they name: `acceptor_owner`: among the 256 junctions of one index of seq, at most 128 have their acceptor on one index of seq.
All inputs are finite; a program needn't handle non-finite values.
Results may differ from the reference program's by a relative error of at most 0.025.
Values may be sent and summed in bfloat16 or wider, within the bound.
A program may use at most 128 MiB of HBM per device.

```python
import math
import jax
import jax.numpy as jnp
import numpy as np
from jax import lax

CHANNELS = 1536
TISSUES = 367
LAYERS = 3
POS_DEV = 512
J_DEV = 256
POSITIONS = 4096
JUNCTIONS = 2048
CAP = 128
N_SEQ = 8


def draw_sequence_in(key, part):
    key_base, key_chan, key_pos = jax.random.split(key, 3)
    ramp = jnp.arange(CHANNELS, dtype=jnp.float32)[:, None] / CHANNELS
    chan_scale = jnp.exp(jnp.log(3.0) * ramp) * 10.0 ** (0.5 * jax.random.uniform(key_chan, (CHANNELS, 1), jnp.float32))
    pos_scale = 10.0 ** (0.5 * jax.random.uniform(key_pos, (1, POSITIONS), jnp.float32))
    base = jax.random.normal(key_base, (CHANNELS, POSITIONS), jnp.float32)
    return (0.25 * base * chan_scale * pos_scale).astype(jnp.bfloat16)


def draw_conv_weight(key, part):
    key_noise, key_left, key_right = jax.random.split(jax.random.fold_in(key, 17), 3)
    spread = (3.0 * CHANNELS) ** (-0.5)
    common = 1.5 * spread
    left = (2 * jax.random.randint(key_left, (LAYERS, CHANNELS, 1, 1), 0, 2) - 1).astype(jnp.float32)
    right = (2 * jax.random.randint(key_right, (LAYERS, 1, 3, CHANNELS), 0, 2) - 1).astype(jnp.float32)
    noise = jnp.clip(jax.random.normal(key_noise, (LAYERS, CHANNELS, 3, CHANNELS), jnp.float32), -4.0, 4.0)
    return (common * left * right + spread * noise).astype(jnp.bfloat16)


def plant(values, key, smallest, high):
    longest = values.shape.index(max(values.shape))
    spots = []
    for shift in (0, 1):
        where = [jax.random.randint(jax.random.fold_in(key, axis), (), 0, length) for axis, length in enumerate(values.shape)]
        where[longest] = (where[longest] + shift) % values.shape[longest]
        spots.append(tuple(where))
    return values.at[spots[0]].set(smallest).at[spots[1]].set(high)


def level_of(rng, dims, cuts, low, largest):
    level = 1.0
    for dim, parts in cuts:
        draws = jax.random.uniform(jax.random.fold_in(jax.random.fold_in(rng, 6), dim), (parts,), jnp.float32, low / len(cuts), largest / len(cuts))
        level = level * jnp.repeat(jnp.exp(draws), dims[dim] // parts).reshape((-1,) + (1,) * (len(dims) - 1 - dim))
    return level


def assign_block(key, own, number, rows, count, top, limit, skew):
    sequence = jax.random.permutation(key, count)
    packed, usual = load_shares(count, rows * top, limit, skew, True), load_shares(count, rows * top, limit, skew, False)
    places = jnp.arange(count)

    def named(sizes, offset_by):
        used = int((sizes > 0).sum())
        fixed = max(1, used // 4)
        moved = fixed + (places - fixed + offset_by * (used - fixed)) % max(1, count - fixed)
        return jnp.zeros((count,), jnp.int32).at[sequence[jnp.where(places < fixed, places, moved)]].set(jnp.asarray(sizes, jnp.int32))

    sizes = jnp.where(number % 4 == 0, named(packed, number // 4), named(usual, number - number // 4 - 1))
    mixed = jax.random.permutation(jax.random.fold_in(own, 3), count)
    giver, sink = mixed[0:count // 2 * 2:2], mixed[1:count // 2 * 2:2]
    slack = jnp.minimum(sizes[giver] - 1, limit - sizes[sink]) // 2
    slack = jnp.where((giver == sequence[0]) | (sink == sequence[0]) | (sizes[sink] == 0), 0, jnp.maximum(slack, 0))
    moved = jax.random.randint(jax.random.fold_in(own, 4), (count // 2,), 0, 1 << 20) % (slack + 1)
    sizes = sizes.at[giver].add(-moved).at[sink].add(moved)
    items = jnp.searchsorted(jnp.cumsum(sizes), jnp.arange(rows * top), side="right").astype(jnp.int32)
    grid = items.reshape(top, rows).T
    grid = grid[jax.random.permutation(jax.random.fold_in(own, 1), rows)]
    offset_by = jax.random.randint(jax.random.fold_in(own, 2), (rows, 1), 0, top)
    return jnp.take_along_axis(grid, (jnp.arange(top)[None, :] + offset_by) % top, axis=1)


def load_shares(amount, total, limit, lean, full):
    portions = [(1 << 20) // math.isqrt(standing ** lean) + 1 for standing in range(1, amount + 1)]
    largest = limit if full else min(limit, max(-(-total // amount), total * portions[0] // sum(portions)))
    least = 1 if total - largest >= amount - 1 else 0
    holding, surplus = [largest] + [least] * (amount - 1), total - largest - least * (amount - 1)
    while surplus > 0:
        free = [i for i in range(1, amount) if holding[i] < largest] or [i for i in range(1, amount) if holding[i] < limit]
        whole, budget = sum([portions[i] for i in free]), surplus
        for i in free:
            more = min(limit - holding[i], max(1, budget * portions[i] // whole), surplus)
            holding[i] = holding[i] + more
            surplus = surplus - more
    return np.array(holding)


def bell_draw(own_key, dims, scale, bound, shards=(), held_as=jnp.bfloat16):
    array = scale * jax.random.normal(own_key, dims, jnp.float32)
    if shards:
        array = array * level_of(own_key, dims, shards, -0.22, 0.18)
    return jnp.clip(array, -bound, bound).astype(held_as)


def setup_inputs(seed: int = 0) -> dict:
    keys = jax.random.split(jax.random.key(seed), 11)
    sequence_in = draw_sequence_in(jax.random.fold_in(keys[10], 71), 0)
    conv_weight = draw_conv_weight(jax.random.fold_in(keys[10], 71), 0)
    norm_gain = jnp.clip(1.0 + 0.18 * jax.random.normal(keys[2], (LAYERS, CHANNELS), jnp.float32), 0.1, 1.9)
    tissue_scale = jnp.clip(jnp.exp(jax.random.uniform(keys[3], (TISSUES, CHANNELS), jnp.float32, math.log(0.3), math.log(3.0))), 0.3, 3.0)
    donor_offset = plant(jax.random.randint(keys[4], (JUNCTIONS,), 0, POS_DEV), jax.random.fold_in(keys[4], 1), 0, POS_DEV - 1).astype(jnp.int32)
    acceptor_owner_keys = jax.random.split(jax.random.fold_in(keys[5], 1), JUNCTIONS // J_DEV)
    acceptor_owner_turns = jax.random.permutation(jax.random.fold_in(keys[5], 3), JUNCTIONS // J_DEV)
    acceptor_owner = jax.vmap(lambda own, number: assign_block(jax.random.fold_in(keys[5], 2), own, number, J_DEV, N_SEQ, 1, CAP, 2))(acceptor_owner_keys, acceptor_owner_turns).reshape((JUNCTIONS, 1))
    acceptor_offset = plant(jax.random.randint(keys[6], (JUNCTIONS,), 0, POS_DEV), jax.random.fold_in(keys[6], 1), 0, POS_DEV - 1).astype(jnp.int32)
    tissue = plant(jax.random.randint(keys[7], (JUNCTIONS,), 0, TISSUES), jax.random.fold_in(keys[7], 1), 0, TISSUES - 1).astype(jnp.int32)
    tower_grad = bell_draw(keys[8], (CHANNELS, POSITIONS), 1.0, 6.0, ((0, 16), (1, 8)), jnp.float32)
    score_grad = bell_draw(keys[9], (JUNCTIONS,), 4.0, 24.0, ((0, 8),), jnp.float32)
    return dict(sequence_in=sequence_in, conv_weight=conv_weight, norm_gain=norm_gain, tissue_scale=tissue_scale, donor_offset=donor_offset, acceptor_owner=acceptor_owner, acceptor_offset=acceptor_offset, tissue=tissue, tower_grad=tower_grad, score_grad=score_grad)


EPSILON = 1e-06

def gelu_fn(value):
    return jax.nn.gelu(value, approximate=True)

def forward_taps(weights, padded, reach, length):
    total = jnp.zeros((weights.shape[0], length), jnp.float32)
    for tap in range(3):
        total = total + jnp.dot(weights[:, tap, :], padded[:, tap * reach:tap * reach + length], preferred_element_type=jnp.float32)
    return total

def backward_taps(weights, grad_pad, reach, length):
    total = jnp.zeros((weights.shape[2], length), jnp.float32)
    for tap in range(3):
        total = total + lax.dot_general(weights[:, tap, :], grad_pad[:, (2 - tap) * reach:(2 - tap) * reach + length], (((0,), (0,)), ((), ())), preferred_element_type=jnp.float32)
    return total

def weight_taps(padded, grad_bf, reach, length):
    blocks = []
    for tap in range(3):
        blocks.append(lax.dot_general(grad_bf, padded[:, tap * reach:tap * reach + length], (((1,), (1,)), ((), ())), preferred_element_type=jnp.float32))
    return jnp.stack(blocks, axis=1)

def reference(sequence_in, conv_weight, norm_gain, tissue_scale, donor_offset, acceptor_owner, acceptor_offset, tissue, tower_grad, score_grad):
    length = POSITIONS
    state = sequence_in
    stored = []
    for layer in range(LAYERS):
        reach = 2 ** (layer + 3)
        stream = state.astype(jnp.float32)
        power = lax.optimization_barrier(jnp.sum(stream * stream, axis=0)) / CHANNELS
        inverse = 1.0 / jnp.sqrt(power + EPSILON)
        pre_act = stream * inverse[None, :] * norm_gain[layer][:, None]
        hidden = gelu_fn(pre_act).astype(jnp.bfloat16)
        padded = jnp.pad(hidden, ((0, 0), (reach, reach)))
        mixed = forward_taps(conv_weight[layer], padded, reach, length)
        stored.append((state, inverse, pre_act, padded))
        state = (stream + mixed).astype(jnp.bfloat16)
    final = state.astype(jnp.float32)
    owner = acceptor_owner[:, 0]
    donor_pos = jnp.arange(JUNCTIONS, dtype=jnp.int32) // J_DEV * POS_DEV + donor_offset
    accept_pos = owner * POS_DEV + acceptor_offset
    donor_cols = final[:, donor_pos].T
    accept_cols = final[:, accept_pos].T
    member = (tissue[:, None] == jnp.arange(TISSUES, dtype=jnp.int32)[None, :]).astype(jnp.float32)
    tissue_rows = jnp.dot(member, tissue_scale, precision=lax.Precision.HIGHEST)
    root = math.sqrt(CHANNELS)
    scores = lax.optimization_barrier(jnp.sum(donor_cols * accept_cols * tissue_rows, axis=1)) / root
    weight_j = score_grad / root
    donor_back = weight_j[:, None] * accept_cols * tissue_rows
    accept_back = weight_j[:, None] * donor_cols * tissue_rows
    upstream = tower_grad.at[:, donor_pos].add(donor_back.T)
    upstream = upstream.at[:, accept_pos].add(accept_back.T)
    weight_list = [None] * LAYERS
    gain_list = [None] * LAYERS
    for layer in reversed(range(LAYERS)):
        reach = 2 ** (layer + 3)
        old_state, inverse, pre_act, padded = stored[layer]
        stream = old_state.astype(jnp.float32)
        grad_bf = upstream.astype(jnp.bfloat16)
        grad_pad = jnp.pad(grad_bf, ((0, 0), (reach, reach)))
        weight_list[layer] = weight_taps(padded, grad_bf, reach, length)
        back_hidden = backward_taps(conv_weight[layer], grad_pad, reach, length)
        _, gelu_back = jax.vjp(gelu_fn, pre_act)
        back_pre = gelu_back(back_hidden)[0]
        gain_list[layer] = lax.optimization_barrier(jnp.sum(back_pre * stream * inverse[None, :], axis=1))
        back_norm = back_pre * norm_gain[layer][:, None]
        inner = lax.optimization_barrier(jnp.sum(back_norm * stream, axis=0))
        upstream = upstream + inverse[None, :] * back_norm - stream * (inverse ** 3)[None, :] * inner[None, :] / CHANNELS
    return (scores, upstream, jnp.stack(weight_list), jnp.stack(gain_list))
```

```python
import math
import functools

import jax
import jax.numpy as jnp
from jax import lax
from jax.experimental import pallas as pl
from jax.experimental.pallas import tpu as pltpu
from jax.sharding import PartitionSpec as P

CHANNELS = 1536
LAYERS = 3
CAP = 128
WIN = 640
SIDE = 4
MESH = pl.DeviceIdType.MESH


EPSILON = 1e-06


def remote(src, dst, send_sem, recv_sem, device):
    return pltpu.make_async_remote_copy(
        src_ref=src,
        dst_ref=dst,
        send_sem=send_sem,
        recv_sem=recv_sem,
        device_id=device,
        device_id_type=MESH,
    )


def forward_kernel(
    seq_ref,
    w_ref,
    gain_ref,
    hid_ref,
    states_ref,
    inv_ref,
    gst,
    halo_rx,
    halo_send,
    halo_recv,
    send_sems,
    recv_sems,
):
    seq_count = lax.axis_size("seq")
    s = lax.axis_index("seq")
    me = lax.axis_index("tp")
    mx = me // SIDE
    my = lax.rem(me, SIDE)

    def xpeer(d):
        return lax.rem(mx + d, SIDE) * SIDE + my

    def ypeer(d):
        return mx * SIDE + lax.rem(my + d, SIDE)

    barrier = pltpu.get_barrier_semaphore()
    for d in range(1, SIDE):
        pl.semaphore_signal(barrier, inc=1, device_id={"tp": xpeer(d)}, device_id_type=MESH)
        pl.semaphore_signal(barrier, inc=1, device_id={"tp": ypeer(d)}, device_id_type=MESH)

    @pl.when(s > 0)
    def _():
        pl.semaphore_signal(barrier, inc=1, device_id={"seq": s - 1}, device_id_type=MESH)

    @pl.when(s < seq_count - 1)
    def _():
        pl.semaphore_signal(barrier, inc=1, device_id={"seq": s + 1}, device_id_type=MESH)

    sides = jnp.where(s > 0, 1, 0) + jnp.where(s < seq_count - 1, 1, 0)
    pl.semaphore_wait(barrier, 2 * (SIDE - 1) + sides)

    def to_left():
        return remote(
            seq_ref.at[:, 0:128], halo_rx.at[0], halo_send.at[0], halo_recv.at[0], {"seq": s - 1}
        )

    def to_right():
        return remote(
            seq_ref.at[:, 384:512], halo_rx.at[1], halo_send.at[1], halo_recv.at[1], {"seq": s + 1}
        )

    @pl.when(s > 0)
    def _():
        to_left().start()

    @pl.when(s < seq_count - 1)
    def _():
        to_right().start()

    @pl.when(s == 0)
    def _():
        halo_rx[1] = jnp.zeros((96, 128), jnp.bfloat16)

    @pl.when(s == seq_count - 1)
    def _():
        halo_rx[0] = jnp.zeros((96, 128), jnp.bfloat16)

    lane = lax.broadcasted_iota(jnp.int32, (96, 128), 1)
    gain = gain_ref[...]
    high = gain.astype(jnp.bfloat16).astype(jnp.float32)
    rest = gain - high
    mid = rest.astype(jnp.bfloat16).astype(jnp.float32)
    low = rest - mid
    packed = jnp.where(lane < 59, high, jnp.where(lane < 62, mid, low))
    in_gain = (lane >= 56) & (lane < 65)

    for h in range(2):
        gst[0, me, h, :, 0:512] = seq_ref[48 * h : 48 * h + 48, :]

    @pl.when(s > 0)
    def _():
        to_left().wait_send()
        remote(
            seq_ref.at[:, 384:512], halo_rx.at[1], halo_send.at[1], halo_recv.at[1], {"seq": s - 1}
        ).wait_recv()

    @pl.when(s < seq_count - 1)
    def _():
        to_right().wait_send()
        remote(
            seq_ref.at[:, 0:128], halo_rx.at[0], halo_send.at[0], halo_recv.at[0], {"seq": s + 1}
        ).wait_recv()

    halo = jnp.where(
        lane < 64, halo_rx[0].astype(jnp.float32), halo_rx[1].astype(jnp.float32)
    )
    tile = jnp.where(in_gain, packed, halo).astype(jnp.bfloat16)
    for h in range(2):
        gst[0, me, h, :, 512:640] = tile[48 * h : 48 * h + 48, :]

    col = lax.broadcasted_iota(jnp.int32, (96, WIN), 1)
    outside = ((s == seq_count - 1) & (col >= 512) & (col < 576)) | ((s == 0) & (col >= 576))

    for layer in range(LAYERS):
        reach = 2 ** (layer + 3)

        def send(slot, block, h, peer, layer=layer):
            return remote(
                gst.at[layer, block, h],
                gst.at[layer, block, h],
                send_sems.at[slot],
                recv_sems.at[layer, block, h],
                {"tp": peer},
            )

        def arrived(block, h, layer=layer):
            remote(
                gst.at[layer, block, h],
                gst.at[layer, block, h],
                send_sems.at[0],
                recv_sems.at[layer, block, h],
                {"tp": xpeer(1)},
            ).wait_recv()

        sent = []

        def go(block, h, peer):
            copy = send(len(sent), block, h, peer)
            copy.start()
            sent.append(copy)

        for d in (1, 3, 2):
            go(me, 0, xpeer(d))
            go(me, 1, ypeer(d))
        for d in (1, 3, 2):
            go(me, 0, ypeer(d))
            go(me, 1, xpeer(d))

        def square(block, h, layer=layer):
            x = gst[layer, block, h].astype(jnp.float32)
            return jnp.sum((x * x).reshape(6, 8, WIN), axis=0)

        total = square(me, 0) + square(me, 1)
        for d in (1, 3, 2):
            arrived(xpeer(d), 0)
            for e in (1, 3, 2):
                go(xpeer(d), 0, ypeer(e))
            arrived(ypeer(d), 1)
            for e in (1, 3, 2):
                go(ypeer(d), 1, xpeer(e))
            total = total + square(xpeer(d), 0) + square(ypeer(d), 1)
        for d in (1, 3, 2):
            arrived(xpeer(d), 1)
            arrived(ypeer(d), 0)
            total = total + square(xpeer(d), 1) + square(ypeer(d), 0)
        for d in (1, 3, 2):
            for e in (1, 3, 2):
                block = lax.rem(mx + d, SIDE) * SIDE + lax.rem(my + e, SIDE)
                arrived(block, 0)
                arrived(block, 1)
                total = total + square(block, 0) + square(block, 1)
        power = jnp.sum(total, axis=0, keepdims=True) / CHANNELS
        inverse = 1.0 / jnp.sqrt(power + EPSILON)
        inv_ref[layer] = jnp.broadcast_to(inverse, (8, WIN))

        def hide(block, carry, layer=layer):
            inv = inv_ref[layer, 0:1, :]
            for h in range(2):
                head = gst[0, block, h, :, 512:640].astype(jnp.float32)
                g = (
                    head[:, 56 + layer : 57 + layer]
                    + head[:, 59 + layer : 60 + layer]
                    + head[:, 62 + layer : 63 + layer]
                )
                x = gst[layer, block, h].astype(jnp.float32) * inv * g
                inner = x + 0.044715 * (x * x * x)
                y = 0.5 * x * (1.0 + jnp.tanh(math.sqrt(2.0 / math.pi) * inner))
                rows = pl.ds(pl.multiple_of(block * 96 + 48 * h, 16), 48)
                hid_ref[layer, rows, :] = y.astype(jnp.bfloat16)
            return carry

        lax.fori_loop(0, SIDE * SIDE, hide, 0)

        parts = []
        for start, width in ((0, 256), (256, 256), (512, 128)):
            parts.append(
                jnp.dot(
                    w_ref[layer],
                    hid_ref[layer, :, start : start + width],
                    preferred_element_type=jnp.float32,
                )
            )
        y = jnp.concatenate(parts, axis=1)
        mixed = (
            pltpu.roll(y[0:96], reach, 1) + y[96:192] + pltpu.roll(y[192:288], WIN - reach, 1)
        )
        own = jnp.concatenate([gst[layer, me, 0], gst[layer, me, 1]], axis=0)
        state = own.astype(jnp.float32) + mixed
        if layer < LAYERS - 1:
            state = jnp.where(outside, 0.0, state).astype(jnp.bfloat16)
            for h in range(2):
                gst[layer + 1, me, h] = state[48 * h : 48 * h + 48, :]
        else:
            state = state.astype(jnp.bfloat16)
        states_ref[layer] = state[:, 0:512]
        for copy in sent:
            copy.wait_send()


def forward(sequence_in, weights, gain_tile):
    return pl.pallas_call(
        forward_kernel,
        out_shape=(
            jax.ShapeDtypeStruct((LAYERS, CHANNELS, WIN), jnp.bfloat16),
            jax.ShapeDtypeStruct((LAYERS, 96, 512), jnp.bfloat16),
            jax.ShapeDtypeStruct((LAYERS, 8, WIN), jnp.float32),
        ),
        in_specs=[pl.BlockSpec(memory_space=pltpu.VMEM)] * 3,
        out_specs=(pl.BlockSpec(memory_space=pltpu.VMEM),) * 3,
        scratch_shapes=[
            pltpu.VMEM((LAYERS, 16, 2, 48, WIN), jnp.bfloat16),
            pltpu.VMEM((2, 96, 128), jnp.bfloat16),
            pltpu.SemaphoreType.DMA((2,)),
            pltpu.SemaphoreType.DMA((2,)),
            pltpu.SemaphoreType.DMA((30,)),
            pltpu.SemaphoreType.DMA((LAYERS, 16, 2)),
        ],
        compiler_params=pltpu.CompilerParams(
            collective_id=0, has_side_effects=True, vmem_limit_bytes=56 * 1024 * 1024
        ),
        name="forward_section",
    )(sequence_in, weights, gain_tile)


def with_halo(x, sides, width):
    for axis, dim in sides:
        count, length = (lax.axis_size(axis), x.shape[dim])
        up = [(i, (i + 1) % count) for i in range(count - 1)]
        down = [(j, i) for i, j in up]
        last = lax.slice_in_dim(x, length - width, length, axis=dim)
        initial = lax.slice_in_dim(x, 0, width, axis=dim)
        before = lax.ppermute(last, axis, up)
        after = lax.ppermute(initial, axis, down)
        x = jnp.concatenate([before, x, after], axis=dim)
    return x


def gelu_fn(value):
    return jax.nn.gelu(value, approximate=True)


def widen(block, width):
    return with_halo(block, (("seq", 1),), width)


def forward_taps(weights, padded, reach, length):
    total = jnp.zeros((weights.shape[0], length), jnp.float32)
    for tap in range(3):
        total = total + jnp.dot(
            weights[:, tap, :],
            padded[:, tap * reach : tap * reach + length],
            preferred_element_type=jnp.float32,
        )
    return total


def backward_taps(weights, grad_pad, reach, length):
    total = jnp.zeros((weights.shape[2], length), jnp.float32)
    for tap in range(3):
        total = total + lax.dot_general(
            weights[:, tap, :],
            grad_pad[:, (2 - tap) * reach : (2 - tap) * reach + length],
            (((0,), (0,)), ((), ())),
            preferred_element_type=jnp.float32,
        )
    return total


def weight_taps(padded, grad_bf, reach, length):
    blocks = []
    for tap in range(3):
        blocks.append(
            lax.dot_general(
                grad_bf,
                padded[:, tap * reach : tap * reach + length],
                (((1,), (1,)), ((), ())),
                preferred_element_type=jnp.float32,
            )
        )
    return jnp.stack(blocks, axis=1)


def local(
    sequence_in,
    conv_weight,
    norm_gain,
    tissue_scale,
    donor_offset,
    acceptor_owner,
    acceptor_offset,
    tissue,
    tower_grad,
    score_grad,
):
    local_ch = sequence_in.shape[0]
    length = sequence_in.shape[1]
    seq_count = lax.axis_size("seq")
    gain_tile = jnp.pad(jnp.tile(norm_gain.T, (1, 3)), ((0, 0), (56, 63)))
    stacked = conv_weight.transpose(0, 2, 1, 3).reshape(LAYERS, 3 * local_ch, CHANNELS)
    hidden_all, states, inverses = forward(sequence_in, stacked, gain_tile)
    stored = []
    for layer in range(LAYERS):
        reach = 2 ** (layer + 3)
        state = sequence_in if layer == 0 else states[layer - 1]
        inverse = inverses[layer, 0, :length]
        pre_act = state.astype(jnp.float32) * inverse[None, :] * norm_gain[layer][:, None]
        window = hidden_all[layer]
        gathered = jnp.concatenate([window[:, WIN - reach :], window[:, : length + reach]], axis=1)
        stored.append((state, inverse, pre_act, gathered))
    state = states[LAYERS - 1]
    owner = acceptor_owner[:, 0]
    member = (owner[:, None] == jnp.arange(seq_count, dtype=jnp.int32)[None, :]).astype(jnp.int32)
    slot = jnp.sum(jnp.cumsum(member, axis=0) * member, axis=1) - 1
    requests = jnp.zeros((seq_count, CAP), jnp.int32).at[owner, slot].set(acceptor_offset)
    rows_view = state.T
    offsets = lax.all_to_all(requests, "seq", split_axis=0, concat_axis=0, tiled=True)
    picked = rows_view[offsets]
    returned = lax.all_to_all(picked, "seq", split_axis=0, concat_axis=0, tiled=True)
    accept_cols = returned[owner, slot].astype(jnp.float32)
    donor_cols = rows_view[donor_offset].astype(jnp.float32)
    chan_start = lax.axis_index("tp") * local_ch
    local_table = lax.dynamic_slice_in_dim(tissue_scale, chan_start, local_ch, 1)
    tissue_hit = (
        tissue[:, None] == jnp.arange(tissue_scale.shape[0], dtype=jnp.int32)[None, :]
    ).astype(jnp.float32)
    tissue_rows = jnp.dot(tissue_hit, local_table, precision=lax.Precision.HIGHEST)
    root = math.sqrt(CHANNELS)
    partial_scores = jnp.sum(donor_cols * accept_cols * tissue_rows, axis=1) / root
    scores = lax.psum(partial_scores, "tp")
    weight_j = score_grad / root
    donor_back = weight_j[:, None] * accept_cols * tissue_rows
    accept_back = weight_j[:, None] * donor_cols * tissue_rows
    outgoing = jnp.zeros((seq_count, CAP, local_ch), jnp.float32).at[owner, slot].set(accept_back)
    incoming = lax.all_to_all(
        outgoing.astype(jnp.bfloat16), "seq", split_axis=0, concat_axis=0, tiled=True
    ).astype(outgoing.dtype)
    upstream = tower_grad.at[:, donor_offset].add(donor_back.T)
    upstream = upstream.at[:, offsets.reshape(-1)].add(incoming.reshape(-1, local_ch).T)
    weight_list = [None] * LAYERS
    gain_list = [None] * LAYERS
    for layer in reversed(range(LAYERS)):
        reach = 2 ** (layer + 3)
        old_state, inverse, pre_act, gathered = stored[layer]
        stream = old_state.astype(jnp.float32)
        grad_bf = upstream.astype(jnp.bfloat16)
        grad_pad = widen(grad_bf, reach)
        weights = conv_weight[layer]

        def term_rows(start, count, weights=weights, grad_pad=grad_pad, reach=reach):
            return backward_taps(weights, grad_pad, reach, length)

        back_hidden = lax.psum_scatter(
            term_rows(jnp.int32(0), local_ch * lax.axis_size("tp")).astype(jnp.bfloat16),
            "tp",
            scatter_dimension=0,
            tiled=True,
        ).astype(jnp.float32)

        def fold_weights(total, piece, start, grad_bf=grad_bf, reach=reach):
            return weight_taps(piece, grad_bf, reach, length)

        weight_term = fold_weights(
            jnp.zeros((local_ch, 3, CHANNELS), jnp.float32),
            gathered,
            jnp.int32(0),
        )
        weight_list[layer] = lax.psum(weight_term.astype(jnp.bfloat16), "seq").astype(jnp.float32)
        _, gelu_back = jax.vjp(gelu_fn, pre_act)
        back_pre = gelu_back(back_hidden)[0]
        gain_list[layer] = jnp.sum(back_pre * stream * inverse[None, :], axis=1)
        back_norm = back_pre * norm_gain[layer][:, None]
        inner = lax.psum(jnp.sum(back_norm * stream, axis=0), "tp")
        upstream = (
            upstream
            + inverse[None, :] * back_norm
            - stream * (inverse**3)[None, :] * inner[None, :] / CHANNELS
        )
    gain_grad = lax.psum(jnp.stack(gain_list), "seq")
    return (scores, upstream, jnp.stack(weight_list), gain_grad)


def solution(mesh):
    return jax.shard_map(
        local,
        mesh=mesh,
        in_specs=(
            P("tp", "seq"),
            P(None, "tp", None, None),
            P(None, "tp"),
            P(),
            P("seq"),
            P("seq", None),
            P("seq"),
            P("seq"),
            P("tp", "seq"),
            P("seq"),
        ),
        out_specs=(P("seq"), P("tp", "seq"), P(None, "tp", None, None), P(None, "tp")),
        check_vma=False,
    )
```

```python
import math

import jax
import jax.numpy as jnp
from jax import lax
from jax.experimental import pallas as pl
from jax.experimental.pallas import tpu as pltpu
from jax.sharding import PartitionSpec as P

CHANNELS = 1536
LAYERS = 3
LOCAL = 96
HALF = 48
LENGTH = 512
WIN = 640
SIDE = 4
SEQ = 8
JUNC = 256
MESH = pl.DeviceIdType.MESH
EPSILON = 1e-06
ROOT = math.sqrt(CHANNELS)
GELU_C = math.sqrt(2.0 / math.pi)
GELU_A = 0.044715
F32 = jnp.float32
BF16 = jnp.bfloat16
NEAR = (1, 3, 2)


def remote(src, dst, send_sem, recv_sem, device):
    return pltpu.make_async_remote_copy(
        src_ref=src,
        dst_ref=dst,
        send_sem=send_sem,
        recv_sem=recv_sem,
        device_id=device,
        device_id_type=MESH,
    )


def dot(a, b):
    return jnp.dot(a, b, preferred_element_type=F32)


def dot_rows(a, b):
    return lax.dot_general(a, b, (((1,), (1,)), ((), ())), preferred_element_type=F32)


def section_kernel(
    seq_ref,
    w_ref,
    gain_ref,
    tower_ref,
    table_ref,
    meta_ref,
    donor_ref,
    tissue_ref,
    sgrad_ref,
    scores_ref,
    grad_ref,
    wgrad_ref,
    gains_ref,
    gst,
    hid,
    inv,
    wt,
    meta_all,
    pick,
    donor_hot,
    tissue_rows,
    state3,
    acc_tx,
    acc_rx,
    ab_tx,
    ab_rx,
    sc_all,
    up,
    gbuf,
    halo_rx,
    halo_b,
    pab,
    rx,
    sf,
    sab,
    ry,
    inn,
    wg,
    wrx,
    wz_tx,
    wz_rx,
    wres,
    gg,
    gg_all,
    halo_send,
    halo_recv,
    gather_send,
    gather_recv,
    meta_send,
    meta_recv,
    acc_send,
    acc_recv,
    ab_send,
    ab_recv,
    sc_send,
    sc_recv,
    rs_send,
    rs_recv,
    inn_send,
    inn_recv,
    w_send,
    w_recv,
    gg_send,
    gg_recv,
):
    s = lax.axis_index("seq")
    me = lax.axis_index("tp")
    mx = me // SIDE
    my = lax.rem(me, SIDE)
    mz = s // 2
    core = lax.rem(s, 2)

    def xpeer(d):
        return lax.rem(mx + d, SIDE) * SIDE + my

    def ypeer(d):
        return mx * SIDE + lax.rem(my + d, SIDE)

    def tpeer(d):
        return lax.rem(me + d, SIDE * SIDE)

    def speer(d):
        return lax.rem(s + d, SEQ)

    def zpeer(d):
        return lax.rem(mz + d, SIDE) * 2 + core

    partner = mz * 2 + 1 - core

    barrier = pltpu.get_barrier_semaphore()
    for d in range(1, SIDE * SIDE):
        pl.semaphore_signal(barrier, inc=1, device_id={"tp": tpeer(d)}, device_id_type=MESH)
    for d in range(1, SEQ):
        pl.semaphore_signal(barrier, inc=1, device_id={"seq": speer(d)}, device_id_type=MESH)
    pl.semaphore_wait(barrier, SIDE * SIDE - 1 + SEQ - 1)

    pending = []

    def begin(copy):
        copy.start()
        pending.append(copy)

    def halo_left(src, dst, k):
        return remote(src.at[:, 0:128], dst.at[0], halo_send.at[k, 0], halo_recv.at[k, 0], {"seq": s - 1})

    def halo_right(src, dst, k):
        return remote(src.at[:, 384:512], dst.at[1], halo_send.at[k, 1], halo_recv.at[k, 1], {"seq": s + 1})

    def halo_start(src, dst, k):
        @pl.when(s > 0)
        def _():
            halo_left(src, dst, k).start()

        @pl.when(s < SEQ - 1)
        def _():
            halo_right(src, dst, k).start()

        @pl.when(s == 0)
        def _():
            dst[1] = jnp.zeros((LOCAL, 128), BF16)

        @pl.when(s == SEQ - 1)
        def _():
            dst[0] = jnp.zeros((LOCAL, 128), BF16)

    def halo_wait(src, dst, k):
        @pl.when(s > 0)
        def _():
            halo_left(src, dst, k).wait_send()
            remote(
                src.at[:, 384:512], dst.at[1], halo_send.at[k, 1], halo_recv.at[k, 1], {"seq": s - 1}
            ).wait_recv()

        @pl.when(s < SEQ - 1)
        def _():
            halo_right(src, dst, k).wait_send()
            remote(
                src.at[:, 0:128], dst.at[0], halo_send.at[k, 0], halo_recv.at[k, 0], {"seq": s + 1}
            ).wait_recv()

    lane = lax.broadcasted_iota(jnp.int32, (LOCAL, 128), 1)

    def halo_tile(dst):
        return jnp.where(lane < 64, dst[0].astype(F32), dst[1].astype(F32))

    halo_start(seq_ref, halo_rx, 0)

    meta_all[s] = meta_ref[...]
    for d in range(1, SEQ):
        begin(
            remote(
                meta_all.at[s], meta_all.at[s], meta_send.at[d - 1], meta_recv.at[d - 1], {"seq": speer(d)}
            )
        )

    gain = gain_ref[...]
    high = gain.astype(BF16).astype(F32)
    rest = gain - high
    mid = rest.astype(BF16).astype(F32)
    low = rest - mid
    packed = jnp.where(lane < 59, high, jnp.where(lane < 62, mid, low))
    in_gain = (lane >= 56) & (lane < 65)

    for h in range(2):
        gst[0, me, h, :, 0:512] = seq_ref[HALF * h : HALF * h + HALF, :]
    halo_wait(seq_ref, halo_rx, 0)
    tile = jnp.where(in_gain, packed, halo_tile(halo_rx)).astype(BF16)
    for h in range(2):
        gst[0, me, h, :, 512:640] = tile[HALF * h : HALF * h + HALF, :]

    col = lax.broadcasted_iota(jnp.int32, (LOCAL, WIN), 1)
    outside = ((s == SEQ - 1) & (col >= 512) & (col < 576)) | ((s == 0) & (col >= 576))

    def transpose_weights(layer):
        for x in range(SIDE):
            block = w_ref[layer, :, 384 * x : 384 * x + 384].astype(F32).T.astype(BF16)
            for y in range(SIDE):
                a = 192 * x + HALF * y
                b = 768 + 192 * y + HALF * x
                wt[layer, a : a + HALF, :] = block[96 * y : 96 * y + HALF]
                wt[layer, b : b + HALF, :] = block[96 * y + HALF : 96 * y + 96]

    def one_hot(rows, row_ids, base):
        ids = lax.broadcasted_iota(jnp.int32, (rows, JUNC), 0) + base
        return jnp.where(ids == row_ids, 1.0, 0.0).astype(BF16)

    def prepare_tissues():
        table = table_ref[...]
        t_high = table.astype(BF16)
        t_rest = table - t_high.astype(F32)
        t_mid = t_rest.astype(BF16)
        t_low = (t_rest - t_mid.astype(F32)).astype(BF16)
        hot = one_hot(384, tissue_ref[...], 0)
        tissue_rows[...] = dot(t_high, hot) + dot(t_mid, hot) + dot(t_low, hot)
        donor_hot[...] = one_hot(LENGTH, donor_ref[...], 0)

    def prepare_picks():
        for d in range(1, SEQ):
            src = speer(SEQ - d)
            remote(
                meta_all.at[src], meta_all.at[src], meta_send.at[d - 1], meta_recv.at[d - 1], {"seq": src}
            ).wait_recv()
        for d in range(SEQ):
            pick[d] = one_hot(LENGTH, meta_all[speer(d)], s * LENGTH)

    for layer in range(LAYERS):
        reach = 2 ** (layer + 3)
        count = [0]

        def go(block, h, peer, layer=layer, count=count):
            begin(
                remote(
                    gst.at[layer, block, h],
                    gst.at[layer, block, h],
                    gather_send.at[layer, count[0]],
                    gather_recv.at[layer, block, h],
                    {"tp": peer},
                )
            )
            count[0] += 1

        def arrived(block, h, layer=layer):
            remote(
                gst.at[layer, block, h],
                gst.at[layer, block, h],
                gather_send.at[layer, 0],
                gather_recv.at[layer, block, h],
                {"tp": xpeer(1)},
            ).wait_recv()

        for d in NEAR:
            go(me, 0, xpeer(d))
            go(me, 1, ypeer(d))
        for d in NEAR:
            go(me, 0, ypeer(d))
            go(me, 1, xpeer(d))

        def square(block, h, layer=layer):
            x = gst[layer, block, h].astype(F32)
            return jnp.sum((x * x).reshape(6, 8, WIN), axis=0)

        total = square(me, 0) + square(me, 1)
        for d in NEAR:
            arrived(xpeer(d), 0)
            for e in NEAR:
                go(xpeer(d), 0, ypeer(e))
            arrived(ypeer(d), 1)
            for e in NEAR:
                go(ypeer(d), 1, xpeer(e))
            total = total + square(xpeer(d), 0) + square(ypeer(d), 1)

        transpose_weights(layer)
        if layer == 0:
            prepare_tissues()
        if layer == 1:
            prepare_picks()

        for d in NEAR:
            arrived(xpeer(d), 1)
            arrived(ypeer(d), 0)
            total = total + square(xpeer(d), 1) + square(ypeer(d), 0)
        for d in NEAR:
            for e in NEAR:
                block = lax.rem(mx + d, SIDE) * SIDE + lax.rem(my + e, SIDE)
                arrived(block, 0)
                arrived(block, 1)
                total = total + square(block, 0) + square(block, 1)
        power = jnp.sum(total, axis=0, keepdims=True) / CHANNELS
        inverse = 1.0 / jnp.sqrt(power + EPSILON)
        inv[layer] = jnp.broadcast_to(inverse, (8, WIN))

        def hide(block, carry, layer=layer):
            scale = inv[layer, 0:1, :]
            for h in range(2):
                head = gst[0, block, h, :, 512:640].astype(F32)
                g = (
                    head[:, 56 + layer : 57 + layer]
                    + head[:, 59 + layer : 60 + layer]
                    + head[:, 62 + layer : 63 + layer]
                )
                x = gst[layer, block, h].astype(F32) * scale * g
                t = jnp.tanh(GELU_C * (x + GELU_A * (x * x * x)))
                rows = pl.ds(pl.multiple_of(block * LOCAL + HALF * h, 16), HALF)
                hid[layer, rows, :] = (0.5 * x * (1.0 + t)).astype(BF16)
            return carry

        lax.fori_loop(0, SIDE * SIDE, hide, 0)

        parts = []
        for start, width in ((0, 256), (256, 256), (512, 128)):
            parts.append(dot(w_ref[layer], hid[layer, :, start : start + width]))
        y = jnp.concatenate(parts, axis=1)
        mixed = pltpu.roll(y[0:96], reach, 1) + y[96:192] + pltpu.roll(y[192:288], WIN - reach, 1)
        own = jnp.concatenate([gst[layer, me, 0], gst[layer, me, 1]], axis=0)
        state = own.astype(F32) + mixed
        if layer < LAYERS - 1:
            state = jnp.where(outside, 0.0, state).astype(BF16)
            for h in range(2):
                gst[layer + 1, me, h] = state[HALF * h : HALF * h + HALF, :]
        else:
            state3[...] = state[:, 0:LENGTH].astype(BF16)

    for d in range(1, SEQ):
        acc_tx[d - 1] = dot(state3[...], pick[d]).astype(BF16)
        begin(
            remote(
                acc_tx.at[d - 1], acc_rx.at[d - 1], acc_send.at[d - 1], acc_recv.at[d - 1], {"seq": speer(d)}
            )
        )
    accept = dot(state3[...], pick[0])
    donor = dot(state3[...], donor_hot[...])
    for d in range(1, SEQ):
        remote(
            acc_tx.at[d - 1], acc_rx.at[d - 1], acc_send.at[d - 1], acc_recv.at[d - 1], {"seq": speer(d)}
        ).wait_recv()
        accept = accept + acc_rx[d - 1].astype(F32)
    weight_j = sgrad_ref[...] / ROOT
    rows_q = tissue_rows[...]
    accept_back = (weight_j * donor * rows_q).astype(BF16)
    ab_tx[...] = accept_back
    for d in range(1, SEQ):
        begin(
            remote(ab_tx, ab_rx.at[d - 1], ab_send.at[d - 1], ab_recv.at[d - 1], {"seq": speer(d)})
        )
    sc_all[me] = jnp.sum(donor * accept * rows_q, axis=0, keepdims=True) / ROOT
    for d in range(1, SIDE * SIDE):
        begin(
            remote(sc_all.at[me], sc_all.at[me], sc_send.at[d - 1], sc_recv.at[d - 1], {"tp": tpeer(d)})
        )
    donor_back = weight_j * accept * rows_q
    d_high = donor_back.astype(BF16)
    d_low = (donor_back - d_high.astype(F32)).astype(BF16)
    added = (
        dot_rows(d_high, donor_hot[...])
        + dot_rows(d_low, donor_hot[...])
        + dot_rows(accept_back, pick[0])
    )
    up[...] = tower_ref[...] + added
    for d in range(1, SEQ):
        remote(
            ab_tx, ab_rx.at[d - 1], ab_send.at[d - 1], ab_recv.at[d - 1], {"seq": speer(d)}
        ).wait_recv()
        up[...] += dot_rows(ab_rx[d - 1], pick[SEQ - d])

    def w_cores(layer):
        return remote(
            wg.at[layer, 1 - core], wrx.at[layer], w_send.at[layer, 0], w_recv.at[layer, 0], {"seq": partner}
        )

    def w_slices(layer, d):
        return remote(
            wz_tx.at[layer, lax.rem(mz + d, SIDE)],
            wz_rx.at[layer, d - 1],
            w_send.at[layer, d],
            w_recv.at[layer, d],
            {"seq": zpeer(d)},
        )

    def w_result(layer, d):
        return remote(
            wres.at[layer, core, mz],
            wres.at[layer, core, mz],
            w_send.at[layer, 3 + d],
            w_recv.at[layer, 3 + d],
            {"seq": zpeer(d)},
        )

    def w_share(layer, d):
        part = wres.at[layer, core, lax.rem(mz + SIDE - d, SIDE)]
        return remote(part, part, w_send.at[layer, 7 + d], w_recv.at[layer, 7 + d], {"seq": partner})

    def w_step2(layer):
        w_cores(layer).wait_recv()
        summed = wg[layer, core].astype(F32) + wrx[layer].astype(F32)
        for q in range(SIDE):
            wz_tx[layer, q] = summed[:, 384 * q : 384 * q + 384].astype(BF16)
        for d in NEAR:
            begin(w_slices(layer, d))

    def w_step3(layer):
        result = wz_tx[layer, mz].astype(F32)
        for d in NEAR:
            w_slices(layer, d).wait_recv()
            result = result + wz_rx[layer, d - 1].astype(F32)
        wres[layer, core, mz] = result.astype(BF16)
        for d in NEAR:
            begin(w_result(layer, d))
        begin(w_share(layer, 0))

    def w_step4(layer):
        for d in NEAR:
            src = wres.at[layer, core, lax.rem(mz + SIDE - d, SIDE)]
            remote(
                src, src, w_send.at[layer, 3 + d], w_recv.at[layer, 3 + d], {"seq": zpeer(d)}
            ).wait_recv()
            begin(w_share(layer, d))

    def w_step5(layer):
        for d in range(SIDE):
            part = wres.at[layer, 1 - core, lax.rem(mz + SIDE - d, SIDE)]
            remote(
                part, part, w_send.at[layer, 7 + d], w_recv.at[layer, 7 + d], {"seq": partner}
            ).wait_recv()
        for h in range(2):
            for q in range(SIDE):
                wgrad_ref[layer, 144 * h : 144 * h + 144, 384 * q : 384 * q + 384] = wres[layer, h, q]

    gg[...] = jnp.zeros((128, 128), F32)
    for layer in reversed(range(LAYERS)):
        reach = 2 ** (layer + 3)
        shifts = (WIN - reach, 0, reach)
        gbuf[layer] = up[...].astype(BF16)
        halo_start(gbuf.at[layer], halo_b.at[layer], layer + 1)
        g = gbuf[layer].astype(F32)

        def shifted(window, shifts=shifts):
            rolled = [pltpu.roll(window, k, 1) if k else window for k in shifts]
            return jnp.concatenate(rolled, axis=0)

        inner_g = shifted(jnp.concatenate([g, jnp.zeros((LOCAL, 128), F32)], axis=1)).astype(BF16)
        for q in range(3):
            part = dot_rows(inner_g, hid[layer, 512 * q : 512 * q + 512, :]).astype(BF16)
            for h in range(2):
                wg[layer, h, :, 512 * q : 512 * q + 512] = part[144 * h : 144 * h + 144]
        begin(w_cores(layer))
        if layer < LAYERS - 1:
            w_step4(layer + 1)
        halo_wait(gbuf.at[layer], halo_b.at[layer], layer + 1)
        full_g = shifted(jnp.concatenate([g, halo_tile(halo_b.at[layer])], axis=1))
        full_g = full_g[:, 0:LENGTH].astype(BF16)

        def chunk(h, index, full_g=full_g, layer=layer):
            rows = pl.ds(pl.multiple_of(768 * h + 192 * index, 16), 192)
            return dot(wt[layer, rows, :], full_g)

        def rs_one(h, d, layer=layer):
            return remote(
                pab.at[layer, h, d - 1],
                rx.at[layer, h, d - 1],
                rs_send.at[layer, h, d - 1],
                rs_recv.at[layer, h, d - 1],
                {"tp": xpeer(d) if h == 0 else ypeer(d)},
            )

        def rs_two(h, d, layer=layer):
            index = lax.rem((my if h == 0 else mx) + d, SIDE)
            return remote(
                sab.at[layer, h, index],
                ry.at[layer, h, d - 1],
                rs_send.at[layer, h, 2 + d],
                rs_recv.at[layer, h, 2 + d],
                {"tp": ypeer(d) if h == 0 else xpeer(d)},
            )

        for d in NEAR:
            for h in range(2):
                base = mx if h == 0 else my
                pab[layer, h, d - 1] = chunk(h, lax.rem(base + d, SIDE)).astype(BF16)
                begin(rs_one(h, d))
        for h in range(2):
            sf[h] = chunk(h, mx if h == 0 else my).reshape(SIDE, HALF, LENGTH)
        w_step2(layer)
        for h in range(2):
            for d in NEAR:
                rs_one(h, d).wait_recv()
                sf[h] += rx[layer, h, d - 1].astype(F32).reshape(SIDE, HALF, LENGTH)
            sab[layer, h] = sf[h].astype(BF16)
            for d in NEAR:
                begin(rs_two(h, d))
        w_step3(layer)

        x = (seq_ref[...] if layer == 0 else jnp.concatenate(
            [gst[layer, me, 0, :, 0:LENGTH], gst[layer, me, 1, :, 0:LENGTH]], axis=0
        )).astype(F32)
        scale = inv[layer, 0:1, 0:LENGTH]
        g_col = gain_ref[:, 56 + layer : 57 + layer]
        norm = x * scale
        pre = norm * g_col
        t = jnp.tanh(GELU_C * (pre + GELU_A * (pre * pre * pre)))
        slope = 0.5 * (1.0 + t) + 0.5 * pre * (1.0 - t * t) * (
            GELU_C * (1.0 + 3.0 * GELU_A * (pre * pre))
        )
        halves = []
        for h in range(2):
            back = sf[h, my if h == 0 else mx]
            for d in NEAR:
                rs_two(h, d).wait_recv()
                back = back + ry[layer, h, d - 1].astype(F32)
            halves.append(back)
        back_pre = jnp.concatenate(halves, axis=0) * slope
        back_norm = back_pre * g_col
        inn[layer, me] = jnp.sum(back_norm * x, axis=0, keepdims=True)
        for d in range(1, SIDE * SIDE):
            begin(
                remote(
                    inn.at[layer, me],
                    inn.at[layer, me],
                    inn_send.at[layer, d - 1],
                    inn_recv.at[layer, d - 1],
                    {"tp": tpeer(d)},
                )
            )
        gain_col = jnp.sum(back_pre * norm, axis=1, keepdims=True)
        gg[0:LOCAL, :] = jnp.where(lane == layer, gain_col, gg[0:LOCAL, :])
        if layer == 0:
            gg_all[s] = gg[...].T[0:8]
            for d in range(1, SEQ):
                begin(
                    remote(
                        gg_all.at[s], gg_all.at[s], gg_send.at[d - 1], gg_recv.at[d - 1], {"seq": speer(d)}
                    )
                )
        for d in range(1, SIDE * SIDE):
            src = inn.at[layer, tpeer(SIDE * SIDE - d)]
            remote(
                src, src, inn_send.at[layer, d - 1], inn_recv.at[layer, d - 1], {"tp": tpeer(d)}
            ).wait_recv()
        inner = jnp.sum(inn[layer], axis=0)
        up[...] = up[...] + scale * back_norm - x * (scale * scale * scale) * (inner / CHANNELS)

    grad_ref[...] = up[...]
    w_step4(0)
    for d in range(1, SIDE * SIDE):
        src = sc_all.at[tpeer(SIDE * SIDE - d)]
        remote(src, src, sc_send.at[d - 1], sc_recv.at[d - 1], {"tp": tpeer(d)}).wait_recv()
    scores_ref[...] = jnp.sum(sc_all[...], axis=0)
    for d in range(1, SEQ):
        src = gg_all.at[speer(SEQ - d)]
        remote(src, src, gg_send.at[d - 1], gg_recv.at[d - 1], {"seq": speer(d)}).wait_recv()
    gains_ref[...] = jnp.sum(gg_all[...], axis=0)
    for layer in reversed(range(LAYERS)):
        w_step5(layer)
    for copy in pending:
        copy.wait_send()


def dma(*shape):
    return pltpu.SemaphoreType.DMA(shape)


def section(*operands):
    vmem = pl.BlockSpec(memory_space=pltpu.VMEM)
    return pl.pallas_call(
        section_kernel,
        out_shape=(
            jax.ShapeDtypeStruct((1, JUNC), F32),
            jax.ShapeDtypeStruct((LOCAL, LENGTH), F32),
            jax.ShapeDtypeStruct((LAYERS, 3 * LOCAL, CHANNELS), BF16),
            jax.ShapeDtypeStruct((8, 128), F32),
        ),
        in_specs=[vmem] * 9,
        out_specs=(vmem,) * 4,
        scratch_shapes=[
            pltpu.VMEM((LAYERS, 16, 2, HALF, WIN), BF16),
            pltpu.VMEM((LAYERS, CHANNELS, WIN), BF16),
            pltpu.VMEM((LAYERS, 8, WIN), F32),
            pltpu.VMEM((LAYERS, CHANNELS, 3 * LOCAL), BF16),
            pltpu.VMEM((SEQ, 1, JUNC), jnp.int32),
            pltpu.VMEM((SEQ, LENGTH, JUNC), BF16),
            pltpu.VMEM((LENGTH, JUNC), BF16),
            pltpu.VMEM((LOCAL, JUNC), F32),
            pltpu.VMEM((LOCAL, LENGTH), BF16),
            pltpu.VMEM((SEQ - 1, LOCAL, JUNC), BF16),
            pltpu.VMEM((SEQ - 1, LOCAL, JUNC), BF16),
            pltpu.VMEM((LOCAL, JUNC), BF16),
            pltpu.VMEM((SEQ - 1, LOCAL, JUNC), BF16),
            pltpu.VMEM((16, 1, JUNC), F32),
            pltpu.VMEM((LOCAL, LENGTH), F32),
            pltpu.VMEM((LAYERS, LOCAL, LENGTH), BF16),
            pltpu.VMEM((2, LOCAL, 128), BF16),
            pltpu.VMEM((LAYERS, 2, LOCAL, 128), BF16),
            pltpu.VMEM((LAYERS, 2, 3, 192, LENGTH), BF16),
            pltpu.VMEM((LAYERS, 2, 3, 192, LENGTH), BF16),
            pltpu.VMEM((2, SIDE, HALF, LENGTH), F32),
            pltpu.VMEM((LAYERS, 2, SIDE, HALF, LENGTH), BF16),
            pltpu.VMEM((LAYERS, 2, 3, HALF, LENGTH), BF16),
            pltpu.VMEM((LAYERS, 16, 1, LENGTH), F32),
            pltpu.VMEM((LAYERS, 2, 144, CHANNELS), BF16),
            pltpu.VMEM((LAYERS, 144, CHANNELS), BF16),
            pltpu.VMEM((LAYERS, SIDE, 144, 384), BF16),
            pltpu.VMEM((LAYERS, 3, 144, 384), BF16),
            pltpu.VMEM((LAYERS, 2, SIDE, 144, 384), BF16),
            pltpu.VMEM((128, 128), F32),
            pltpu.VMEM((SEQ, 8, 128), F32),
            dma(4, 2),
            dma(4, 2),
            dma(LAYERS, 30),
            dma(LAYERS, 16, 2),
            dma(7),
            dma(7),
            dma(7),
            dma(7),
            dma(7),
            dma(7),
            dma(15),
            dma(15),
            dma(LAYERS, 2, 6),
            dma(LAYERS, 2, 6),
            dma(LAYERS, 15),
            dma(LAYERS, 15),
            dma(LAYERS, 11),
            dma(LAYERS, 11),
            dma(7),
            dma(7),
        ],
        compiler_params=pltpu.CompilerParams(
            collective_id=0, has_side_effects=True, vmem_limit_bytes=62 * 1024 * 1024
        ),
        name="conv_section",
    )(*operands)


def local(
    sequence_in,
    conv_weight,
    norm_gain,
    tissue_scale,
    donor_offset,
    acceptor_owner,
    acceptor_offset,
    tissue,
    tower_grad,
    score_grad,
):
    gain_tile = jnp.pad(jnp.tile(norm_gain.T, (1, 3)), ((0, 0), (56, 63)))
    stacked = conv_weight.transpose(0, 2, 1, 3).reshape(LAYERS, 3 * LOCAL, CHANNELS)
    table = lax.dynamic_slice_in_dim(tissue_scale, lax.axis_index("tp") * LOCAL, LOCAL, 1).T
    table = jnp.pad(table, ((0, 0), (0, 384 - table.shape[1])))
    meta = (acceptor_owner[:, 0] * LENGTH + acceptor_offset)[None, :]
    scores, grad, weights, gains = section(
        sequence_in,
        stacked,
        gain_tile,
        tower_grad,
        table,
        meta,
        donor_offset[None, :],
        tissue[None, :],
        score_grad[None, :],
    )
    weights = weights.reshape(LAYERS, 3, LOCAL, CHANNELS).transpose(0, 2, 1, 3).astype(F32)
    return (scores[0], grad, weights, gains[:LAYERS, :LOCAL])


def solution(mesh):
    return jax.shard_map(
        local,
        mesh=mesh,
        in_specs=(
            P("tp", "seq"),
            P(None, "tp", None, None),
            P(None, "tp"),
            P(),
            P("seq"),
            P("seq", None),
            P("seq"),
            P("seq"),
            P("tp", "seq"),
            P("seq"),
        ),
        out_specs=(P("seq"), P("tp", "seq"), P(None, "tp", None, None), P(None, "tp")),
        check_vma=False,
    )
```

```python
import math

import jax
import jax.numpy as jnp
from jax import lax
from jax.experimental import pallas as pl
from jax.experimental.pallas import tpu as pltpu
from jax.sharding import PartitionSpec as P

CHANNELS = 1536
LAYERS = 3
LOCAL = 96
HALF = 48
LENGTH = 512
WIN = 640
SIDE = 4
SEQ = 8
JUNC = 256
MESH = pl.DeviceIdType.MESH
EPSILON = 1e-06
ROOT = math.sqrt(CHANNELS)
GELU_C = math.sqrt(2.0 / math.pi)
GELU_A = 0.044715
F32 = jnp.float32
BF16 = jnp.bfloat16
NEAR = (1, 3, 2)


def remote(src, dst, send_sem, recv_sem, device):
    return pltpu.make_async_remote_copy(
        src_ref=src,
        dst_ref=dst,
        send_sem=send_sem,
        recv_sem=recv_sem,
        device_id=device,
        device_id_type=MESH,
    )


def dot(a, b):
    return jnp.dot(a, b, preferred_element_type=F32)


def dot_rows(a, b):
    return lax.dot_general(a, b, (((1,), (1,)), ((), ())), preferred_element_type=F32)


def section_kernel(
    seq_ref,
    w_hbm,
    gain_in,
    tower_hbm,
    table_ref,
    owner_ref,
    offset_ref,
    donor_ref,
    tissue_ref,
    sgrad_ref,
    scores_ref,
    grad_ref,
    wgrad_ref,
    gains_ref,
    w_ref,
    tower_ref,
    gain_ref,
    turn,
    tab,
    gst,
    hid,
    mm,
    vv,
    ysum,
    pw,
    inv,
    wt,
    meta_all,
    pick,
    donor_hot,
    tissue_rows,
    state3,
    acc_tx,
    acc_rx,
    ab_tx,
    ab_rx,
    sc_all,
    up,
    gbuf,
    halo_rx,
    halo_b,
    pab,
    rx,
    sf,
    sab,
    ry,
    inn,
    wg,
    wrx,
    wz_tx,
    wz_rx,
    wres,
    gg,
    gg_all,
    halo_send,
    halo_recv,
    gather_send,
    gather_recv,
    meta_send,
    meta_recv,
    acc_send,
    acc_recv,
    ab_send,
    ab_recv,
    sc_send,
    sc_recv,
    rs_send,
    rs_recv,
    inn_send,
    inn_recv,
    w_send,
    w_recv,
    gg_send,
    gg_recv,
    pw_send,
    pw_recv,
    load_sem,
):
    s = lax.axis_index("seq")
    me = lax.axis_index("tp")
    mx = me // SIDE
    my = lax.rem(me, SIDE)
    mz = s // 2
    core = lax.rem(s, 2)

    def xpeer(d):
        return lax.rem(mx + d, SIDE) * SIDE + my

    def ypeer(d):
        return mx * SIDE + lax.rem(my + d, SIDE)

    def tpeer(d):
        return lax.rem(me + d, SIDE * SIDE)

    def speer(d):
        return lax.rem(s + d, SEQ)

    def zpeer(d):
        return lax.rem(mz + d, SIDE) * 2 + core

    partner = mz * 2 + 1 - core

    load_w = pltpu.make_async_copy(w_hbm, w_ref, load_sem.at[0])
    load_tower = pltpu.make_async_copy(tower_hbm, tower_ref, load_sem.at[1])
    load_w.start()
    load_tower.start()

    barrier = pltpu.get_barrier_semaphore()
    for d in range(1, SIDE * SIDE):
        pl.semaphore_signal(barrier, inc=1, device_id={"tp": tpeer(d)}, device_id_type=MESH)
    for d in range(1, SEQ):
        pl.semaphore_signal(barrier, inc=1, device_id={"seq": speer(d)}, device_id_type=MESH)
    turn[...] = jnp.zeros((128, 128), F32)
    for k in range(3):
        turn[56 + 3 * k : 59 + 3 * k, 0:LOCAL] = gain_in[...]
    gain_ref[...] = turn[...].T[0:LOCAL]
    pl.semaphore_wait(barrier, SIDE * SIDE - 1 + SEQ - 1)

    pending = []

    def begin(copy):
        copy.start()
        pending.append(copy)

    def halo_left(src, dst, k):
        return remote(src.at[:, 0:128], dst.at[0], halo_send.at[k, 0], halo_recv.at[k, 0], {"seq": s - 1})

    def halo_right(src, dst, k):
        return remote(src.at[:, 384:512], dst.at[1], halo_send.at[k, 1], halo_recv.at[k, 1], {"seq": s + 1})

    def halo_start(src, dst, k):
        @pl.when(s > 0)
        def _():
            halo_left(src, dst, k).start()

        @pl.when(s < SEQ - 1)
        def _():
            halo_right(src, dst, k).start()

        @pl.when(s == 0)
        def _():
            dst[1] = jnp.zeros((LOCAL, 128), BF16)

        @pl.when(s == SEQ - 1)
        def _():
            dst[0] = jnp.zeros((LOCAL, 128), BF16)

    def halo_wait(src, dst, k):
        @pl.when(s > 0)
        def _():
            halo_left(src, dst, k).wait_send()
            remote(
                src.at[:, 384:512], dst.at[1], halo_send.at[k, 1], halo_recv.at[k, 1], {"seq": s - 1}
            ).wait_recv()

        @pl.when(s < SEQ - 1)
        def _():
            halo_right(src, dst, k).wait_send()
            remote(
                src.at[:, 0:128], dst.at[0], halo_send.at[k, 0], halo_recv.at[k, 0], {"seq": s + 1}
            ).wait_recv()

    lane = lax.broadcasted_iota(jnp.int32, (LOCAL, 128), 1)

    def halo_tile(dst):
        return jnp.where(lane < 64, dst[0].astype(F32), dst[1].astype(F32))

    halo_start(seq_ref, halo_rx, 0)

    meta_all[s] = owner_ref[...] * LENGTH + offset_ref[...]
    for d in range(1, SEQ):
        begin(
            remote(
                meta_all.at[s], meta_all.at[s], meta_send.at[d - 1], meta_recv.at[d - 1], {"seq": speer(d)}
            )
        )

    gain = gain_ref[...]
    high = gain.astype(BF16).astype(F32)
    rest = gain - high
    mid = rest.astype(BF16).astype(F32)
    low = rest - mid
    packed = jnp.where(lane < 59, high, jnp.where(lane < 62, mid, low))
    in_gain = (lane >= 56) & (lane < 65)

    for h in range(2):
        gst[0, me, h, :, 0:512] = seq_ref[HALF * h : HALF * h + HALF, :]
    halo_wait(seq_ref, halo_rx, 0)
    tile = jnp.where(in_gain, packed, halo_tile(halo_rx)).astype(BF16)
    for h in range(2):
        gst[0, me, h, :, 512:640] = tile[HALF * h : HALF * h + HALF, :]

    col = lax.broadcasted_iota(jnp.int32, (LOCAL, WIN), 1)
    outside = ((s == SEQ - 1) & (col >= 512) & (col < 576)) | ((s == 0) & (col >= 576))

    def transpose_weights(layer):
        for x in range(SIDE):
            block = w_ref[layer, :, 384 * x : 384 * x + 384].astype(F32).T.astype(BF16)
            for y in range(SIDE):
                a = 192 * x + HALF * y
                b = 768 + 192 * y + HALF * x
                wt[layer, a : a + HALF, :] = block[96 * y : 96 * y + HALF]
                wt[layer, b : b + HALF, :] = block[96 * y + HALF : 96 * y + 96]

    def one_hot(rows, row_ids, base):
        ids = lax.broadcasted_iota(jnp.int32, (rows, JUNC), 0) + base
        return jnp.where(ids == row_ids, 1.0, 0.0).astype(BF16)

    def prepare_tissues():
        tab[...] = jnp.zeros((384, 128), F32)
        tab[0 : table_ref.shape[0], 0:LOCAL] = table_ref[...]
        table = tab[...].T[0:LOCAL]
        t_high = table.astype(BF16)
        t_rest = table - t_high.astype(F32)
        t_mid = t_rest.astype(BF16)
        t_low = (t_rest - t_mid.astype(F32)).astype(BF16)
        hot = one_hot(384, tissue_ref[...], 0)
        tissue_rows[...] = dot(t_high, hot) + dot(t_mid, hot) + dot(t_low, hot)
        donor_hot[...] = one_hot(LENGTH, donor_ref[...], 0)

    def prepare_picks():
        for d in range(1, SEQ):
            src = speer(SEQ - d)
            remote(
                meta_all.at[src], meta_all.at[src], meta_send.at[d - 1], meta_recv.at[d - 1], {"seq": src}
            ).wait_recv()
        for d in range(SEQ):
            pick[d] = one_hot(LENGTH, meta_all[speer(d)], s * LENGTH)

    for layer in range(LAYERS):
        reach = 2 ** (layer + 3)
        count = [0]

        def go(block, h, peer, layer=layer, count=count):
            begin(
                remote(
                    gst.at[layer, block, h],
                    gst.at[layer, block, h],
                    gather_send.at[layer, count[0]],
                    gather_recv.at[layer, block, h],
                    {"tp": peer},
                )
            )
            count[0] += 1

        def arrived(block, h, layer=layer):
            remote(
                gst.at[layer, block, h],
                gst.at[layer, block, h],
                gather_send.at[layer, 0],
                gather_recv.at[layer, block, h],
                {"tp": xpeer(1)},
            ).wait_recv()

        squares = jnp.concatenate([gst[layer, me, 0], gst[layer, me, 1]], axis=0).astype(F32)
        pw[layer, me] = jnp.sum(squares * squares, axis=0, keepdims=True)
        for d in range(1, SIDE * SIDE):
            begin(
                remote(
                    pw.at[layer, me],
                    pw.at[layer, me],
                    pw_send.at[layer, d - 1],
                    pw_recv.at[layer, d - 1],
                    {"tp": tpeer(d)},
                )
            )
        for d in NEAR:
            go(me, 0, xpeer(d))
            go(me, 1, ypeer(d))
        for d in NEAR:
            go(me, 0, ypeer(d))
            go(me, 1, xpeer(d))

        if layer == 0:
            prepare_tissues()
            load_w.wait()
        if layer > 0:
            vv[layer - 1] = dot(w_ref[layer - 1], mm[layer - 1])

        for d in NEAR:
            arrived(xpeer(d), 0)
            for e in NEAR:
                go(xpeer(d), 0, ypeer(e))
            arrived(ypeer(d), 1)
            for e in NEAR:
                go(ypeer(d), 1, xpeer(e))

        for d in range(1, SIDE * SIDE):
            src = pw.at[layer, tpeer(SIDE * SIDE - d)]
            remote(
                src, src, pw_send.at[layer, d - 1], pw_recv.at[layer, d - 1], {"tp": tpeer(d)}
            ).wait_recv()
        power = jnp.sum(pw[layer], axis=0) / CHANNELS
        inverse = 1.0 / jnp.sqrt(power + EPSILON)
        inv[layer] = jnp.broadcast_to(inverse, (8, WIN))

        def hide(block, carry, layer=layer):
            scale = inv[layer, 0:1, :]
            for h in range(2):
                head = gst[0, block, h, :, 512:640].astype(F32)
                g = (
                    head[:, 56 + layer : 57 + layer]
                    + head[:, 59 + layer : 60 + layer]
                    + head[:, 62 + layer : 63 + layer]
                )
                rows = pl.ds(pl.multiple_of(block * LOCAL + HALF * h, 16), HALF)
                raw = gst[layer, block, h, :, 0:LENGTH].astype(F32) * g
                x = raw * scale[:, 0:LENGTH]
                xx = x * x
                t = jnp.tanh(GELU_C * (x + GELU_A * (xx * x)))
                upper = 0.5 * (1.0 + t)
                hid[layer, rows, 0:LENGTH] = (x * upper).astype(BF16)
                slope = upper + (0.5 * x) * (1.0 - t * t) * (GELU_C + (3.0 * GELU_A * GELU_C) * xx)
                mm[layer, rows, :] = (raw * slope).astype(BF16)
                x = gst[layer, block, h, :, LENGTH:WIN].astype(F32) * scale[:, LENGTH:WIN] * g
                t = jnp.tanh(GELU_C * (x + GELU_A * (x * x * x)))
                hid[layer, rows, LENGTH:WIN] = (0.5 * x * (1.0 + t)).astype(BF16)
            return carry

        for d in (0,) + NEAR:
            group = lax.rem(mx + d, SIDE)
            if d == 0:
                for e in NEAR:
                    arrived(ypeer(e), 0)
            else:
                arrived(xpeer(d), 1)
                for e in NEAR:
                    block = group * SIDE + lax.rem(my + e, SIDE)
                    arrived(block, 0)
                    arrived(block, 1)
            lax.fori_loop(group * SIDE, group * SIDE + SIDE, hide, 0)
            span = pl.ds(pl.multiple_of(group * 384, 128), 384)
            part = dot(w_ref[layer, :, span], hid[layer, span, :])
            if d == 0:
                ysum[...] = part
                transpose_weights(layer)
                if layer == 1:
                    prepare_picks()
            elif d != NEAR[-1]:
                ysum[...] += part
            else:
                y = ysum[...] + part

        mixed = pltpu.roll(y[0:96], reach, 1) + y[96:192] + pltpu.roll(y[192:288], WIN - reach, 1)
        own = jnp.concatenate([gst[layer, me, 0], gst[layer, me, 1]], axis=0)
        state = own.astype(F32) + mixed
        if layer < LAYERS - 1:
            state = jnp.where(outside, 0.0, state).astype(BF16)
            for h in range(2):
                gst[layer + 1, me, h] = state[HALF * h : HALF * h + HALF, :]
        else:
            state3[...] = state[:, 0:LENGTH].astype(BF16)

    for d in range(1, SEQ):
        acc_tx[d - 1] = dot(state3[...], pick[d]).astype(BF16)
        begin(
            remote(
                acc_tx.at[d - 1], acc_rx.at[d - 1], acc_send.at[d - 1], acc_recv.at[d - 1], {"seq": speer(d)}
            )
        )
    vv[LAYERS - 1] = dot(w_ref[LAYERS - 1], mm[LAYERS - 1])
    load_tower.wait()
    accept = dot(state3[...], pick[0])
    donor = dot(state3[...], donor_hot[...])
    for d in range(1, SEQ):
        remote(
            acc_tx.at[d - 1], acc_rx.at[d - 1], acc_send.at[d - 1], acc_recv.at[d - 1], {"seq": speer(d)}
        ).wait_recv()
        accept = accept + acc_rx[d - 1].astype(F32)
    weight_j = sgrad_ref[...] / ROOT
    rows_q = tissue_rows[...]
    accept_back = (weight_j * donor * rows_q).astype(BF16)
    ab_tx[...] = accept_back
    for d in range(1, SEQ):
        begin(
            remote(ab_tx, ab_rx.at[d - 1], ab_send.at[d - 1], ab_recv.at[d - 1], {"seq": speer(d)})
        )
    sc_all[me] = jnp.sum(donor * accept * rows_q, axis=0, keepdims=True) / ROOT
    for d in range(1, SIDE * SIDE):
        begin(
            remote(sc_all.at[me], sc_all.at[me], sc_send.at[d - 1], sc_recv.at[d - 1], {"tp": tpeer(d)})
        )
    donor_back = weight_j * accept * rows_q
    d_high = donor_back.astype(BF16)
    d_low = (donor_back - d_high.astype(F32)).astype(BF16)
    added = (
        dot_rows(d_high, donor_hot[...])
        + dot_rows(d_low, donor_hot[...])
        + dot_rows(accept_back, pick[0])
    )
    up[...] = tower_ref[...] + added
    for d in range(1, SEQ):
        remote(
            ab_tx, ab_rx.at[d - 1], ab_send.at[d - 1], ab_recv.at[d - 1], {"seq": speer(d)}
        ).wait_recv()
        up[...] += dot_rows(ab_rx[d - 1], pick[SEQ - d])

    def w_cores(layer):
        return remote(
            wg.at[layer, 1 - core], wrx.at[layer], w_send.at[layer, 0], w_recv.at[layer, 0], {"seq": partner}
        )

    def w_slices(layer, d):
        return remote(
            wz_tx.at[layer, lax.rem(mz + d, SIDE)],
            wz_rx.at[layer, d - 1],
            w_send.at[layer, d],
            w_recv.at[layer, d],
            {"seq": zpeer(d)},
        )

    def w_result(layer, d):
        return remote(
            wres.at[layer, core, mz],
            wres.at[layer, core, mz],
            w_send.at[layer, 3 + d],
            w_recv.at[layer, 3 + d],
            {"seq": zpeer(d)},
        )

    def w_share(layer, d):
        part = wres.at[layer, core, lax.rem(mz + SIDE - d, SIDE)]
        return remote(part, part, w_send.at[layer, 7 + d], w_recv.at[layer, 7 + d], {"seq": partner})

    def w_step2(layer):
        w_cores(layer).wait_recv()
        summed = wg[layer, core].astype(F32) + wrx[layer].astype(F32)
        for q in range(SIDE):
            wz_tx[layer, q] = summed[:, 384 * q : 384 * q + 384].astype(BF16)
        for d in NEAR:
            begin(w_slices(layer, d))

    def w_step3(layer):
        result = wz_tx[layer, mz].astype(F32)
        for d in NEAR:
            w_slices(layer, d).wait_recv()
            result = result + wz_rx[layer, d - 1].astype(F32)
        wres[layer, core, mz] = result.astype(BF16)
        for d in NEAR:
            begin(w_result(layer, d))
        begin(w_share(layer, 0))

    def w_step4(layer):
        for d in NEAR:
            src = wres.at[layer, core, lax.rem(mz + SIDE - d, SIDE)]
            remote(
                src, src, w_send.at[layer, 3 + d], w_recv.at[layer, 3 + d], {"seq": zpeer(d)}
            ).wait_recv()
            begin(w_share(layer, d))

    def w_step5(layer):
        for d in range(SIDE):
            part = wres.at[layer, 1 - core, lax.rem(mz + SIDE - d, SIDE)]
            remote(
                part, part, w_send.at[layer, 7 + d], w_recv.at[layer, 7 + d], {"seq": partner}
            ).wait_recv()
        for h in range(2):
            for q in range(SIDE):
                wgrad_ref[layer, 144 * h : 144 * h + 144, 384 * q : 384 * q + 384] = wres[layer, h, q]

    gg[...] = jnp.zeros((128, 128), F32)
    for layer in reversed(range(LAYERS)):
        reach = 2 ** (layer + 3)
        shifts = (WIN - reach, 0, reach)
        gbuf[layer] = up[...].astype(BF16)
        halo_start(gbuf.at[layer], halo_b.at[layer], layer + 1)
        g = gbuf[layer].astype(F32)

        def shifted(window, shifts=shifts):
            rolled = [pltpu.roll(window, k, 1) if k else window for k in shifts]
            return jnp.concatenate(rolled, axis=0)

        inner_g = shifted(jnp.concatenate([g, jnp.zeros((LOCAL, 128), F32)], axis=1)).astype(BF16)
        for q in range(3):
            part = dot_rows(inner_g, hid[layer, 512 * q : 512 * q + 512, :]).astype(BF16)
            for h in range(2):
                wg[layer, h, :, 512 * q : 512 * q + 512] = part[144 * h : 144 * h + 144]
        begin(w_cores(layer))
        if layer < LAYERS - 1:
            w_step4(layer + 1)
        halo_wait(gbuf.at[layer], halo_b.at[layer], layer + 1)
        full_g = shifted(jnp.concatenate([g, halo_tile(halo_b.at[layer])], axis=1))
        full_g = full_g[:, 0:LENGTH]
        inn[layer, me] = jnp.sum(full_g * vv[layer], axis=0, keepdims=True)
        for d in range(1, SIDE * SIDE):
            begin(
                remote(
                    inn.at[layer, me],
                    inn.at[layer, me],
                    inn_send.at[layer, d - 1],
                    inn_recv.at[layer, d - 1],
                    {"tp": tpeer(d)},
                )
            )
        full_g = full_g.astype(BF16)

        def chunk(h, index, full_g=full_g, layer=layer):
            rows = pl.ds(pl.multiple_of(768 * h + 192 * index, 16), 192)
            return dot(wt[layer, rows, :], full_g)

        def rs_one(h, d, layer=layer):
            return remote(
                pab.at[layer, h, d - 1],
                rx.at[layer, h, d - 1],
                rs_send.at[layer, h, d - 1],
                rs_recv.at[layer, h, d - 1],
                {"tp": xpeer(d) if h == 0 else ypeer(d)},
            )

        def rs_two(h, d, layer=layer):
            index = lax.rem((my if h == 0 else mx) + d, SIDE)
            return remote(
                sab.at[layer, h, index],
                ry.at[layer, h, d - 1],
                rs_send.at[layer, h, 2 + d],
                rs_recv.at[layer, h, 2 + d],
                {"tp": ypeer(d) if h == 0 else xpeer(d)},
            )

        for d in NEAR:
            for h in range(2):
                base = mx if h == 0 else my
                pab[layer, h, d - 1] = chunk(h, lax.rem(base + d, SIDE)).astype(BF16)
                begin(rs_one(h, d))
        for h in range(2):
            sf[h] = chunk(h, mx if h == 0 else my).reshape(SIDE, HALF, LENGTH)
        w_step2(layer)
        for h in range(2):
            for d in NEAR:
                rs_one(h, d).wait_recv()
                sf[h] += rx[layer, h, d - 1].astype(F32).reshape(SIDE, HALF, LENGTH)
            sab[layer, h] = sf[h].astype(BF16)
            for d in NEAR:
                begin(rs_two(h, d))
            if h == 0 and layer == 0:
                w_step3(layer)
        if layer > 0:
            w_step3(layer)

        x = (seq_ref[...] if layer == 0 else jnp.concatenate(
            [gst[layer, me, 0, :, 0:LENGTH], gst[layer, me, 1, :, 0:LENGTH]], axis=0
        )).astype(F32)
        scale = inv[layer, 0:1, 0:LENGTH]
        g_col = gain_ref[:, 56 + layer : 57 + layer]
        norm = x * scale
        pre = norm * g_col
        t = jnp.tanh(GELU_C * (pre + GELU_A * (pre * pre * pre)))
        slope = 0.5 * (1.0 + t) + 0.5 * pre * (1.0 - t * t) * (
            GELU_C * (1.0 + 3.0 * GELU_A * (pre * pre))
        )
        halves = []
        for h in range(2):
            back = sf[h, my if h == 0 else mx]
            for d in NEAR:
                rs_two(h, d).wait_recv()
                back = back + ry[layer, h, d - 1].astype(F32)
            halves.append(back)
        back_pre = jnp.concatenate(halves, axis=0) * slope
        back_norm = back_pre * g_col
        gain_col = jnp.sum(back_pre * norm, axis=1, keepdims=True)
        gg[0:LOCAL, :] = jnp.where(lane == layer, gain_col, gg[0:LOCAL, :])
        if layer == 0:
            gg_all[s] = gg[...].T[0:8]
            for d in range(1, SEQ):
                begin(
                    remote(
                        gg_all.at[s], gg_all.at[s], gg_send.at[d - 1], gg_recv.at[d - 1], {"seq": speer(d)}
                    )
                )
        for d in range(1, SIDE * SIDE):
            src = inn.at[layer, tpeer(SIDE * SIDE - d)]
            remote(
                src, src, inn_send.at[layer, d - 1], inn_recv.at[layer, d - 1], {"tp": tpeer(d)}
            ).wait_recv()
        inner = jnp.sum(inn[layer], axis=0)
        up[...] = up[...] + scale * back_norm - x * (scale * scale * scale) * (inner / CHANNELS)

    grad_ref[...] = up[...]
    w_step4(0)
    for d in range(1, SIDE * SIDE):
        src = sc_all.at[tpeer(SIDE * SIDE - d)]
        remote(src, src, sc_send.at[d - 1], sc_recv.at[d - 1], {"tp": tpeer(d)}).wait_recv()
    scores_ref[...] = jnp.sum(sc_all[...], axis=0)
    for d in range(1, SEQ):
        src = gg_all.at[speer(SEQ - d)]
        remote(src, src, gg_send.at[d - 1], gg_recv.at[d - 1], {"seq": speer(d)}).wait_recv()
    gains_ref[...] = jnp.sum(gg_all[...], axis=0)[0:LAYERS, 0:LOCAL]
    for layer in reversed(range(LAYERS)):
        w_step5(layer)
    for copy in pending:
        copy.wait_send()


def dma(*shape):
    return pltpu.SemaphoreType.DMA(shape)


def section(*operands):
    vmem = pl.BlockSpec(memory_space=pltpu.VMEM)
    hbm = pl.BlockSpec(memory_space=pl.ANY)
    return pl.pallas_call(
        section_kernel,
        out_shape=(
            jax.ShapeDtypeStruct((1, JUNC), F32),
            jax.ShapeDtypeStruct((LOCAL, LENGTH), F32),
            jax.ShapeDtypeStruct((LAYERS, 3 * LOCAL, CHANNELS), BF16),
            jax.ShapeDtypeStruct((LAYERS, LOCAL), F32),
        ),
        in_specs=[vmem, hbm, vmem, hbm] + [vmem] * 6,
        out_specs=(vmem,) * 4,
        scratch_shapes=[
            pltpu.VMEM((LAYERS, 3 * LOCAL, CHANNELS), BF16),
            pltpu.VMEM((LOCAL, LENGTH), F32),
            pltpu.VMEM((LOCAL, 128), F32),
            pltpu.VMEM((128, 128), F32),
            pltpu.VMEM((384, 128), F32),
            pltpu.VMEM((LAYERS, 16, 2, HALF, WIN), BF16),
            pltpu.VMEM((LAYERS, CHANNELS, WIN), BF16),
            pltpu.VMEM((LAYERS, CHANNELS, LENGTH), BF16),
            pltpu.VMEM((LAYERS, 3 * LOCAL, LENGTH), F32),
            pltpu.VMEM((3 * LOCAL, WIN), F32),
            pltpu.VMEM((LAYERS, 16, 1, WIN), F32),
            pltpu.VMEM((LAYERS, 8, WIN), F32),
            pltpu.VMEM((LAYERS, CHANNELS, 3 * LOCAL), BF16),
            pltpu.VMEM((SEQ, 1, JUNC), jnp.int32),
            pltpu.VMEM((SEQ, LENGTH, JUNC), BF16),
            pltpu.VMEM((LENGTH, JUNC), BF16),
            pltpu.VMEM((LOCAL, JUNC), F32),
            pltpu.VMEM((LOCAL, LENGTH), BF16),
            pltpu.VMEM((SEQ - 1, LOCAL, JUNC), BF16),
            pltpu.VMEM((SEQ - 1, LOCAL, JUNC), BF16),
            pltpu.VMEM((LOCAL, JUNC), BF16),
            pltpu.VMEM((SEQ - 1, LOCAL, JUNC), BF16),
            pltpu.VMEM((16, 1, JUNC), F32),
            pltpu.VMEM((LOCAL, LENGTH), F32),
            pltpu.VMEM((LAYERS, LOCAL, LENGTH), BF16),
            pltpu.VMEM((2, LOCAL, 128), BF16),
            pltpu.VMEM((LAYERS, 2, LOCAL, 128), BF16),
            pltpu.VMEM((LAYERS, 2, 3, 192, LENGTH), BF16),
            pltpu.VMEM((LAYERS, 2, 3, 192, LENGTH), BF16),
            pltpu.VMEM((2, SIDE, HALF, LENGTH), F32),
            pltpu.VMEM((LAYERS, 2, SIDE, HALF, LENGTH), BF16),
            pltpu.VMEM((LAYERS, 2, 3, HALF, LENGTH), BF16),
            pltpu.VMEM((LAYERS, 16, 1, LENGTH), F32),
            pltpu.VMEM((LAYERS, 2, 144, CHANNELS), BF16),
            pltpu.VMEM((LAYERS, 144, CHANNELS), BF16),
            pltpu.VMEM((LAYERS, SIDE, 144, 384), BF16),
            pltpu.VMEM((LAYERS, 3, 144, 384), BF16),
            pltpu.VMEM((LAYERS, 2, SIDE, 144, 384), BF16),
            pltpu.VMEM((128, 128), F32),
            pltpu.VMEM((SEQ, 8, 128), F32),
            dma(4, 2),
            dma(4, 2),
            dma(LAYERS, 30),
            dma(LAYERS, 16, 2),
            dma(7),
            dma(7),
            dma(7),
            dma(7),
            dma(7),
            dma(7),
            dma(15),
            dma(15),
            dma(LAYERS, 2, 6),
            dma(LAYERS, 2, 6),
            dma(LAYERS, 15),
            dma(LAYERS, 15),
            dma(LAYERS, 11),
            dma(LAYERS, 11),
            dma(7),
            dma(7),
            dma(LAYERS, 15),
            dma(LAYERS, 15),
            dma(2),
        ],
        compiler_params=pltpu.CompilerParams(
            collective_id=0, has_side_effects=True, vmem_limit_bytes=62 * 1024 * 1024
        ),
        name="conv_section",
    )(*operands)


def local(
    sequence_in,
    conv_weight,
    norm_gain,
    tissue_scale,
    donor_offset,
    acceptor_owner,
    acceptor_offset,
    tissue,
    tower_grad,
    score_grad,
):
    stacked = conv_weight.transpose(0, 2, 1, 3).reshape(LAYERS, 3 * LOCAL, CHANNELS)
    table = lax.dynamic_slice_in_dim(tissue_scale, lax.axis_index("tp") * LOCAL, LOCAL, 1)
    scores, grad, weights, gains = section(
        sequence_in,
        stacked,
        norm_gain,
        tower_grad,
        table,
        acceptor_owner.T,
        acceptor_offset[None, :],
        donor_offset[None, :],
        tissue[None, :],
        score_grad[None, :],
    )
    weights = weights.reshape(LAYERS, 3, LOCAL, CHANNELS).transpose(0, 2, 1, 3).astype(F32)
    return (scores[0], grad, weights, gains)


def solution(mesh):
    return jax.shard_map(
        local,
        mesh=mesh,
        in_specs=(
            P("tp", "seq"),
            P(None, "tp", None, None),
            P(None, "tp"),
            P(),
            P("seq"),
            P("seq", None),
            P("seq"),
            P("seq"),
            P("tp", "seq"),
            P("seq"),
        ),
        out_specs=(P("seq"), P("tp", "seq"), P(None, "tp", None, None), P(None, "tp")),
        check_vma=False,
    )
```

```python
import math

import jax
import jax.numpy as jnp
from jax import lax
from jax.experimental import pallas as pl
from jax.experimental.pallas import tpu as pltpu
from jax.sharding import PartitionSpec as P

CHANNELS = 1536
LAYERS = 3
LOCAL = 96
HALF = 48
LENGTH = 512
WIN = 640
SIDE = 4
SEQ = 8
JUNC = 256
CAP = 128
MESH = pl.DeviceIdType.MESH
EPSILON = 1e-06
ROOT = math.sqrt(CHANNELS)
GELU_C = math.sqrt(2.0 / math.pi)
GELU_A = 0.044715
F32 = jnp.float32
BF16 = jnp.bfloat16
NEAR = (1, 3, 2)


def remote(src, dst, send_sem, recv_sem, device):
    return pltpu.make_async_remote_copy(
        src_ref=src,
        dst_ref=dst,
        send_sem=send_sem,
        recv_sem=recv_sem,
        device_id=device,
        device_id_type=MESH,
    )


def dot(a, b):
    return jnp.dot(a, b, preferred_element_type=F32)


def dot_rows(a, b):
    return lax.dot_general(a, b, (((1,), (1,)), ((), ())), preferred_element_type=F32)


def section_kernel(
    seq_ref,
    w_hbm,
    gain_in,
    tower_hbm,
    table_ref,
    owner_ref,
    offset_ref,
    donor_ref,
    tissue_ref,
    sgrad_ref,
    scores_ref,
    grad_ref,
    wgrad_ref,
    gains_ref,
    w_ref,
    tower_ref,
    gain_ref,
    turn,
    tab,
    gst,
    hid,
    mm,
    vv,
    ysum,
    pw,
    inv,
    wt,
    meta_all,
    pick,
    slots,
    donor_hot,
    tissue_rows,
    state3,
    acc_tx,
    acc_rx,
    ab_tx,
    ab_rx,
    sc_all,
    up,
    gbuf,
    halo_rx,
    halo_b,
    pab,
    rx,
    sf,
    sab,
    ry,
    inn,
    wg,
    wrx,
    wz_tx,
    wz_rx,
    wres,
    gg,
    gg_all,
    halo_send,
    halo_recv,
    gather_send,
    gather_recv,
    meta_send,
    meta_recv,
    acc_send,
    acc_recv,
    ab_send,
    ab_recv,
    sc_send,
    sc_recv,
    rs_send,
    rs_recv,
    inn_send,
    inn_recv,
    w_send,
    w_recv,
    gg_send,
    gg_recv,
    pw_send,
    pw_recv,
    load_sem,
):
    s = lax.axis_index("seq")
    me = lax.axis_index("tp")
    mx = me // SIDE
    my = lax.rem(me, SIDE)
    mz = s // 2
    core = lax.rem(s, 2)

    def xpeer(d):
        return lax.rem(mx + d, SIDE) * SIDE + my

    def ypeer(d):
        return mx * SIDE + lax.rem(my + d, SIDE)

    def tpeer(d):
        return lax.rem(me + d, SIDE * SIDE)

    def speer(d):
        return lax.rem(s + d, SEQ)

    def zpeer(d):
        return lax.rem(mz + d, SIDE) * 2 + core

    partner = mz * 2 + 1 - core

    load_w = pltpu.make_async_copy(w_hbm, w_ref, load_sem.at[0])
    load_tower = pltpu.make_async_copy(tower_hbm, tower_ref, load_sem.at[1])
    load_w.start()
    load_tower.start()

    barrier = pltpu.get_barrier_semaphore()
    for d in range(1, SIDE * SIDE):
        pl.semaphore_signal(barrier, inc=1, device_id={"tp": tpeer(d)}, device_id_type=MESH)
    for d in range(1, SEQ):
        pl.semaphore_signal(barrier, inc=1, device_id={"seq": speer(d)}, device_id_type=MESH)
    turn[...] = jnp.zeros((128, 128), F32)
    for k in range(3):
        turn[56 + 3 * k : 59 + 3 * k, 0:LOCAL] = gain_in[...]
    gain_ref[...] = turn[...].T[0:LOCAL]
    pl.semaphore_wait(barrier, SIDE * SIDE - 1 + SEQ - 1)

    pending = []

    def begin(copy):
        copy.start()
        pending.append(copy)

    def halo_left(src, dst, k):
        return remote(src.at[:, 0:128], dst.at[0], halo_send.at[k, 0], halo_recv.at[k, 0], {"seq": s - 1})

    def halo_right(src, dst, k):
        return remote(src.at[:, 384:512], dst.at[1], halo_send.at[k, 1], halo_recv.at[k, 1], {"seq": s + 1})

    def halo_start(src, dst, k):
        @pl.when(s > 0)
        def _():
            halo_left(src, dst, k).start()

        @pl.when(s < SEQ - 1)
        def _():
            halo_right(src, dst, k).start()

        @pl.when(s == 0)
        def _():
            dst[1] = jnp.zeros((LOCAL, 128), BF16)

        @pl.when(s == SEQ - 1)
        def _():
            dst[0] = jnp.zeros((LOCAL, 128), BF16)

    def halo_wait(src, dst, k):
        @pl.when(s > 0)
        def _():
            halo_left(src, dst, k).wait_send()
            remote(
                src.at[:, 384:512], dst.at[1], halo_send.at[k, 1], halo_recv.at[k, 1], {"seq": s - 1}
            ).wait_recv()

        @pl.when(s < SEQ - 1)
        def _():
            halo_right(src, dst, k).wait_send()
            remote(
                src.at[:, 0:128], dst.at[0], halo_send.at[k, 0], halo_recv.at[k, 0], {"seq": s + 1}
            ).wait_recv()

    lane = lax.broadcasted_iota(jnp.int32, (LOCAL, 128), 1)

    def halo_tile(dst):
        return jnp.where(lane < 64, dst[0].astype(F32), dst[1].astype(F32))

    halo_start(seq_ref, halo_rx, 0)

    gain = gain_ref[...]
    high = gain.astype(BF16).astype(F32)
    rest = gain - high
    mid = rest.astype(BF16).astype(F32)
    low = rest - mid
    packed = jnp.where(lane < 59, high, jnp.where(lane < 62, mid, low))
    in_gain = (lane >= 56) & (lane < 65)

    for h in range(2):
        gst[0, me, h, :, 0:512] = seq_ref[HALF * h : HALF * h + HALF, :]
    halo_wait(seq_ref, halo_rx, 0)
    tile = jnp.where(in_gain, packed, halo_tile(halo_rx)).astype(BF16)
    for h in range(2):
        gst[0, me, h, :, 512:640] = tile[HALF * h : HALF * h + HALF, :]

    col = lax.broadcasted_iota(jnp.int32, (LOCAL, WIN), 1)
    outside = ((s == SEQ - 1) & (col >= 512) & (col < 576)) | ((s == 0) & (col >= 576))

    def transpose_weights(layer):
        for x in range(SIDE):
            block = w_ref[layer, :, 384 * x : 384 * x + 384].astype(F32).T.astype(BF16)
            for y in range(SIDE):
                a = 192 * x + HALF * y
                b = 768 + 192 * y + HALF * x
                wt[layer, a : a + HALF, :] = block[96 * y : 96 * y + HALF]
                wt[layer, b : b + HALF, :] = block[96 * y + HALF : 96 * y + 96]

    def one_hot(rows, row_ids, base):
        ids = lax.broadcasted_iota(jnp.int32, (rows, JUNC), 0) + base
        return jnp.where(ids == row_ids, 1.0, 0.0).astype(BF16)

    def prepare_tissues():
        tab[...] = jnp.zeros((384, 128), F32)
        tab[0 : table_ref.shape[0], 0:LOCAL] = table_ref[...]
        table = tab[...].T[0:LOCAL]
        t_high = table.astype(BF16)
        t_rest = table - t_high.astype(F32)
        t_mid = t_rest.astype(BF16)
        t_low = (t_rest - t_mid.astype(F32)).astype(BF16)
        hot = one_hot(384, tissue_ref[...], 0)
        tissue_rows[...] = dot(t_high, hot) + dot(t_mid, hot) + dot(t_low, hot)
        donor_hot[...] = one_hot(LENGTH, donor_ref[...], 0)

    def send_meta():
        owner = owner_ref[...]
        member = one_hot(16, owner, 0)
        first = lax.broadcasted_iota(jnp.int32, (JUNC, JUNC), 0)
        second = lax.broadcasted_iota(jnp.int32, (JUNC, JUNC), 1)
        rank = dot(member, jnp.where(first <= second, 1.0, 0.0).astype(BF16))
        slot = jnp.sum(member.astype(F32) * rank, axis=0, keepdims=True) - 1.0
        slot = slot.astype(jnp.int32)
        meta_all[s] = (slot * SEQ + owner) * LENGTH + offset_ref[...]
        for d in range(1, SEQ):
            begin(
                remote(
                    meta_all.at[s], meta_all.at[s], meta_send.at[d - 1], meta_recv.at[d - 1], {"seq": speer(d)}
                )
            )
        ids = lax.broadcasted_iota(jnp.int32, (CAP, JUNC), 0)
        for d in range(SEQ):
            mine = (ids == slot) & (owner == speer(d))
            slots[CAP * d : CAP * d + CAP, :] = jnp.where(mine, 1.0, 0.0).astype(BF16)

    def wait_meta():
        for d in range(1, SEQ):
            src = speer(SEQ - d)
            remote(
                meta_all.at[src], meta_all.at[src], meta_send.at[d - 1], meta_recv.at[d - 1], {"seq": src}
            ).wait_recv()

    def prepare_picks(which):
        for d in which:
            row = meta_all[speer(d)]
            place = one_hot(LENGTH, row & (SEQ * LENGTH - 1), s * LENGTH)
            slot = one_hot(CAP, lax.shift_right_logical(row, 12), 0)
            pick[:, CAP * d : CAP * d + CAP] = dot_rows(place, slot).astype(BF16)

    for layer in range(LAYERS):
        reach = 2 ** (layer + 3)
        count = [0]

        def go(block, h, peer, layer=layer, count=count):
            begin(
                remote(
                    gst.at[layer, block, h],
                    gst.at[layer, block, h],
                    gather_send.at[layer, count[0]],
                    gather_recv.at[layer, block, h],
                    {"tp": peer},
                )
            )
            count[0] += 1

        def arrived(block, h, layer=layer):
            remote(
                gst.at[layer, block, h],
                gst.at[layer, block, h],
                gather_send.at[layer, 0],
                gather_recv.at[layer, block, h],
                {"tp": xpeer(1)},
            ).wait_recv()

        squares = jnp.concatenate([gst[layer, me, 0], gst[layer, me, 1]], axis=0).astype(F32)
        pw[layer, me] = jnp.sum(squares * squares, axis=0, keepdims=True)
        for d in range(1, SIDE * SIDE):
            begin(
                remote(
                    pw.at[layer, me],
                    pw.at[layer, me],
                    pw_send.at[layer, d - 1],
                    pw_recv.at[layer, d - 1],
                    {"tp": tpeer(d)},
                )
            )
        for d in NEAR:
            go(me, 0, xpeer(d))
            go(me, 1, ypeer(d))
        for d in NEAR:
            go(me, 0, ypeer(d))
            go(me, 1, xpeer(d))

        if layer == 0:
            send_meta()
            prepare_tissues()
            load_w.wait()
        if layer > 0:
            vv[layer - 1] = dot(w_ref[layer - 1], mm[layer - 1])

        for d in NEAR:
            arrived(xpeer(d), 0)
            for e in NEAR:
                go(xpeer(d), 0, ypeer(e))
            arrived(ypeer(d), 1)
            for e in NEAR:
                go(ypeer(d), 1, xpeer(e))

        for d in range(1, SIDE * SIDE):
            src = pw.at[layer, tpeer(SIDE * SIDE - d)]
            remote(
                src, src, pw_send.at[layer, d - 1], pw_recv.at[layer, d - 1], {"tp": tpeer(d)}
            ).wait_recv()
        power = jnp.sum(pw[layer], axis=0) / CHANNELS
        inverse = 1.0 / jnp.sqrt(power + EPSILON)
        inv[layer] = jnp.broadcast_to(inverse, (8, WIN))

        def hide(block, carry, layer=layer):
            scale = inv[layer, 0:1, :]
            for h in range(2):
                head = gst[0, block, h, :, 512:640].astype(F32)
                g = (
                    head[:, 56 + layer : 57 + layer]
                    + head[:, 59 + layer : 60 + layer]
                    + head[:, 62 + layer : 63 + layer]
                )
                rows = pl.ds(pl.multiple_of(block * LOCAL + HALF * h, 16), HALF)
                raw = gst[layer, block, h, :, 0:LENGTH].astype(F32) * g
                x = raw * scale[:, 0:LENGTH]
                xx = x * x
                t = jnp.tanh(GELU_C * (x + GELU_A * (xx * x)))
                upper = 0.5 * (1.0 + t)
                hid[layer, rows, 0:LENGTH] = (x * upper).astype(BF16)
                slope = upper + (0.5 * x) * (1.0 - t * t) * (GELU_C + (3.0 * GELU_A * GELU_C) * xx)
                mm[layer, rows, :] = (raw * slope).astype(BF16)
                x = gst[layer, block, h, :, LENGTH:WIN].astype(F32) * scale[:, LENGTH:WIN] * g
                t = jnp.tanh(GELU_C * (x + GELU_A * (x * x * x)))
                hid[layer, rows, LENGTH:WIN] = (0.5 * x * (1.0 + t)).astype(BF16)
            return carry

        for d in (0,) + NEAR:
            group = lax.rem(mx + d, SIDE)
            if d > 0:
                arrived(xpeer(d), 1)
            hide(group * SIDE + my, 0)

            def next_block(e, carry, d=d, group=group, arrived=arrived, hide=hide):
                block = group * SIDE + lax.rem(my + e, SIDE)
                arrived(block, 0)
                if d > 0:
                    arrived(block, 1)
                return hide(block, carry)

            lax.fori_loop(1, SIDE, next_block, 0)
            span = pl.ds(pl.multiple_of(group * 384, 128), 384)
            part = dot(w_ref[layer, :, span], hid[layer, span, :])
            if d == 0:
                ysum[...] = part
                transpose_weights(layer)
                if layer == 1:
                    wait_meta()
                    prepare_picks(range(0, 4))
                if layer == 2:
                    prepare_picks(range(4, 8))
            elif d != NEAR[-1]:
                ysum[...] += part
            else:
                y = ysum[...] + part

        mixed = pltpu.roll(y[0:96], reach, 1) + y[96:192] + pltpu.roll(y[192:288], WIN - reach, 1)
        own = jnp.concatenate([gst[layer, me, 0], gst[layer, me, 1]], axis=0)
        state = own.astype(F32) + mixed
        if layer < LAYERS - 1:
            state = jnp.where(outside, 0.0, state).astype(BF16)
            for h in range(2):
                gst[layer + 1, me, h] = state[HALF * h : HALF * h + HALF, :]
        else:
            state3[...] = state[:, 0:LENGTH].astype(BF16)

    def acc_copy(d):
        return remote(
            acc_tx.at[:, CAP * d : CAP * d + CAP],
            acc_rx.at[:, CAP * (SEQ - d) : CAP * (SEQ - d) + CAP],
            acc_send.at[d - 1],
            acc_recv.at[d - 1],
            {"seq": speer(d)},
        )

    def ab_copy(d):
        return remote(
            ab_tx.at[:, CAP * d : CAP * d + CAP],
            ab_rx.at[:, CAP * (SEQ - d) : CAP * (SEQ - d) + CAP],
            ab_send.at[d - 1],
            ab_recv.at[d - 1],
            {"seq": speer(d)},
        )

    acc_tx[...] = dot(state3[...], pick[...]).astype(BF16)
    for d in range(1, SEQ):
        begin(acc_copy(d))
    acc_rx[:, 0:CAP] = acc_tx[:, 0:CAP]
    donor = dot(state3[...], donor_hot[...])
    load_tower.wait()
    weight_j = sgrad_ref[...] / ROOT
    rows_q = tissue_rows[...]
    accept_back = (weight_j * donor * rows_q).astype(BF16)
    ab_tx[...] = dot_rows(accept_back, slots[...]).astype(BF16)
    for d in range(1, SEQ):
        begin(ab_copy(d))
    ab_rx[:, 0:CAP] = ab_tx[:, 0:CAP]
    vv[LAYERS - 1] = dot(w_ref[LAYERS - 1], mm[LAYERS - 1])
    for d in range(1, SEQ):
        acc_copy(d).wait_recv()
    accept = dot(acc_rx[...], slots[...])
    donor_back = weight_j * accept * rows_q
    d_high = donor_back.astype(BF16)
    d_low = (donor_back - d_high.astype(F32)).astype(BF16)
    up[...] = tower_ref[...] + dot_rows(d_high, donor_hot[...]) + dot_rows(d_low, donor_hot[...])
    sc_all[me] = jnp.sum(donor * accept * rows_q, axis=0, keepdims=True) / ROOT
    for d in range(1, SEQ):
        ab_copy(d).wait_recv()
    up[...] += dot_rows(ab_rx[...], pick[...])
    for d in range(1, SIDE * SIDE):
        begin(
            remote(sc_all.at[me], sc_all.at[me], sc_send.at[d - 1], sc_recv.at[d - 1], {"tp": tpeer(d)})
        )

    def w_cores(layer):
        return remote(
            wg.at[layer, 1 - core], wrx.at[layer], w_send.at[layer, 0], w_recv.at[layer, 0], {"seq": partner}
        )

    def w_slices(layer, d):
        return remote(
            wz_tx.at[layer, lax.rem(mz + d, SIDE)],
            wz_rx.at[layer, d - 1],
            w_send.at[layer, d],
            w_recv.at[layer, d],
            {"seq": zpeer(d)},
        )

    def w_result(layer, d):
        return remote(
            wres.at[layer, core, mz],
            wres.at[layer, core, mz],
            w_send.at[layer, 3 + d],
            w_recv.at[layer, 3 + d],
            {"seq": zpeer(d)},
        )

    def w_share(layer, d):
        part = wres.at[layer, core, lax.rem(mz + SIDE - d, SIDE)]
        return remote(part, part, w_send.at[layer, 7 + d], w_recv.at[layer, 7 + d], {"seq": partner})

    def w_step2(layer):
        w_cores(layer).wait_recv()
        summed = wg[layer, core].astype(F32) + wrx[layer].astype(F32)
        for q in range(SIDE):
            wz_tx[layer, q] = summed[:, 384 * q : 384 * q + 384].astype(BF16)
        for d in NEAR:
            begin(w_slices(layer, d))

    def w_step3(layer):
        result = wz_tx[layer, mz].astype(F32)
        for d in NEAR:
            w_slices(layer, d).wait_recv()
            result = result + wz_rx[layer, d - 1].astype(F32)
        wres[layer, core, mz] = result.astype(BF16)
        for d in NEAR:
            begin(w_result(layer, d))
        begin(w_share(layer, 0))

    def w_step4(layer):
        for d in NEAR:
            src = wres.at[layer, core, lax.rem(mz + SIDE - d, SIDE)]
            remote(
                src, src, w_send.at[layer, 3 + d], w_recv.at[layer, 3 + d], {"seq": zpeer(d)}
            ).wait_recv()
            begin(w_share(layer, d))

    def w_step5(layer):
        for d in range(SIDE):
            part = wres.at[layer, 1 - core, lax.rem(mz + SIDE - d, SIDE)]
            remote(
                part, part, w_send.at[layer, 7 + d], w_recv.at[layer, 7 + d], {"seq": partner}
            ).wait_recv()
        for h in range(2):
            for q in range(SIDE):
                wgrad_ref[layer, 144 * h : 144 * h + 144, 384 * q : 384 * q + 384] = wres[layer, h, q]

    gg[...] = jnp.zeros((128, 128), F32)
    for layer in reversed(range(LAYERS)):
        reach = 2 ** (layer + 3)
        shifts = (WIN - reach, 0, reach)
        gbuf[layer] = up[...].astype(BF16)
        halo_start(gbuf.at[layer], halo_b.at[layer], layer + 1)
        g = gbuf[layer].astype(F32)

        def shifted(window, shifts=shifts):
            rolled = [pltpu.roll(window, k, 1) if k else window for k in shifts]
            return jnp.concatenate(rolled, axis=0)

        inner_g = shifted(jnp.concatenate([g, jnp.zeros((LOCAL, 128), F32)], axis=1)).astype(BF16)
        for q in range(3):
            part = dot_rows(inner_g, hid[layer, 512 * q : 512 * q + 512, :]).astype(BF16)
            for h in range(2):
                wg[layer, h, :, 512 * q : 512 * q + 512] = part[144 * h : 144 * h + 144]
        begin(w_cores(layer))
        if layer < LAYERS - 1:
            w_step4(layer + 1)
        halo_wait(gbuf.at[layer], halo_b.at[layer], layer + 1)
        full_g = shifted(jnp.concatenate([g, halo_tile(halo_b.at[layer])], axis=1))
        full_g = full_g[:, 0:LENGTH]
        inn[layer, me] = jnp.sum(full_g * vv[layer], axis=0, keepdims=True)
        for d in range(1, SIDE * SIDE):
            begin(
                remote(
                    inn.at[layer, me],
                    inn.at[layer, me],
                    inn_send.at[layer, d - 1],
                    inn_recv.at[layer, d - 1],
                    {"tp": tpeer(d)},
                )
            )
        full_g = full_g.astype(BF16)

        def chunk(h, index, full_g=full_g, layer=layer):
            rows = pl.ds(pl.multiple_of(768 * h + 192 * index, 16), 192)
            return dot(wt[layer, rows, :], full_g)

        def rs_one(h, d, layer=layer):
            return remote(
                pab.at[layer, h, d - 1],
                rx.at[layer, h, d - 1],
                rs_send.at[layer, h, d - 1],
                rs_recv.at[layer, h, d - 1],
                {"tp": xpeer(d) if h == 0 else ypeer(d)},
            )

        def rs_two(h, d, layer=layer):
            index = lax.rem((my if h == 0 else mx) + d, SIDE)
            return remote(
                sab.at[layer, h, index],
                ry.at[layer, h, d - 1],
                rs_send.at[layer, h, 2 + d],
                rs_recv.at[layer, h, 2 + d],
                {"tp": ypeer(d) if h == 0 else xpeer(d)},
            )

        for d in NEAR:
            for h in range(2):
                base = mx if h == 0 else my
                pab[layer, h, d - 1] = chunk(h, lax.rem(base + d, SIDE)).astype(BF16)
                begin(rs_one(h, d))
        for h in range(2):
            sf[h] = chunk(h, mx if h == 0 else my).reshape(SIDE, HALF, LENGTH)
        w_step2(layer)
        for h in range(2):
            for d in NEAR:
                rs_one(h, d).wait_recv()
                sf[h] += rx[layer, h, d - 1].astype(F32).reshape(SIDE, HALF, LENGTH)
            sab[layer, h] = sf[h].astype(BF16)
            for d in NEAR:
                begin(rs_two(h, d))
            if h == 0 and layer == 0:
                w_step3(layer)
        if layer > 0:
            w_step3(layer)

        x = (seq_ref[...] if layer == 0 else jnp.concatenate(
            [gst[layer, me, 0, :, 0:LENGTH], gst[layer, me, 1, :, 0:LENGTH]], axis=0
        )).astype(F32)
        scale = inv[layer, 0:1, 0:LENGTH]
        g_col = gain_ref[:, 56 + layer : 57 + layer]
        norm = x * scale
        pre = norm * g_col
        t = jnp.tanh(GELU_C * (pre + GELU_A * (pre * pre * pre)))
        slope = 0.5 * (1.0 + t) + 0.5 * pre * (1.0 - t * t) * (
            GELU_C * (1.0 + 3.0 * GELU_A * (pre * pre))
        )
        halves = []
        for h in range(2):
            back = sf[h, my if h == 0 else mx]
            for d in NEAR:
                rs_two(h, d).wait_recv()
                back = back + ry[layer, h, d - 1].astype(F32)
            halves.append(back)
        back_pre = jnp.concatenate(halves, axis=0) * slope
        back_norm = back_pre * g_col
        gain_col = jnp.sum(back_pre * norm, axis=1, keepdims=True)
        gg[0:LOCAL, :] = jnp.where(lane == layer, gain_col, gg[0:LOCAL, :])
        if layer == 0:
            gg_all[s] = gg[...].T[0:8]
            for d in range(1, SEQ):
                begin(
                    remote(
                        gg_all.at[s], gg_all.at[s], gg_send.at[d - 1], gg_recv.at[d - 1], {"seq": speer(d)}
                    )
                )
        for d in range(1, SIDE * SIDE):
            src = inn.at[layer, tpeer(SIDE * SIDE - d)]
            remote(
                src, src, inn_send.at[layer, d - 1], inn_recv.at[layer, d - 1], {"tp": tpeer(d)}
            ).wait_recv()
        inner = jnp.sum(inn[layer], axis=0)
        up[...] = up[...] + scale * back_norm - x * (scale * scale * scale) * (inner / CHANNELS)

    grad_ref[...] = up[...]
    w_step4(0)
    for d in range(1, SIDE * SIDE):
        src = sc_all.at[tpeer(SIDE * SIDE - d)]
        remote(src, src, sc_send.at[d - 1], sc_recv.at[d - 1], {"tp": tpeer(d)}).wait_recv()
    scores_ref[...] = jnp.sum(sc_all[...], axis=0)
    for d in range(1, SEQ):
        src = gg_all.at[speer(SEQ - d)]
        remote(src, src, gg_send.at[d - 1], gg_recv.at[d - 1], {"seq": speer(d)}).wait_recv()
    gains_ref[...] = jnp.sum(gg_all[...], axis=0)[0:LAYERS, 0:LOCAL]
    for layer in reversed(range(LAYERS)):
        w_step5(layer)
    for copy in pending:
        copy.wait_send()


def dma(*shape):
    return pltpu.SemaphoreType.DMA(shape)


def section(*operands):
    vmem = pl.BlockSpec(memory_space=pltpu.VMEM)
    hbm = pl.BlockSpec(memory_space=pl.ANY)
    return pl.pallas_call(
        section_kernel,
        out_shape=(
            jax.ShapeDtypeStruct((1, JUNC), F32),
            jax.ShapeDtypeStruct((LOCAL, LENGTH), F32),
            jax.ShapeDtypeStruct((LAYERS, 3 * LOCAL, CHANNELS), BF16),
            jax.ShapeDtypeStruct((LAYERS, LOCAL), F32),
        ),
        in_specs=[vmem, hbm, vmem, hbm] + [vmem] * 6,
        out_specs=(vmem,) * 4,
        scratch_shapes=[
            pltpu.VMEM((LAYERS, 3 * LOCAL, CHANNELS), BF16),
            pltpu.VMEM((LOCAL, LENGTH), F32),
            pltpu.VMEM((LOCAL, 128), F32),
            pltpu.VMEM((128, 128), F32),
            pltpu.VMEM((384, 128), F32),
            pltpu.VMEM((LAYERS, 16, 2, HALF, WIN), BF16),
            pltpu.VMEM((LAYERS, CHANNELS, WIN), BF16),
            pltpu.VMEM((LAYERS, CHANNELS, LENGTH), BF16),
            pltpu.VMEM((LAYERS, 3 * LOCAL, LENGTH), F32),
            pltpu.VMEM((3 * LOCAL, WIN), F32),
            pltpu.VMEM((LAYERS, 16, 1, WIN), F32),
            pltpu.VMEM((LAYERS, 8, WIN), F32),
            pltpu.VMEM((LAYERS, CHANNELS, 3 * LOCAL), BF16),
            pltpu.VMEM((SEQ, 1, JUNC), jnp.int32),
            pltpu.VMEM((LENGTH, SEQ * CAP), BF16),
            pltpu.VMEM((SEQ * CAP, JUNC), BF16),
            pltpu.VMEM((LENGTH, JUNC), BF16),
            pltpu.VMEM((LOCAL, JUNC), F32),
            pltpu.VMEM((LOCAL, LENGTH), BF16),
            pltpu.VMEM((LOCAL, SEQ * CAP), BF16),
            pltpu.VMEM((LOCAL, SEQ * CAP), BF16),
            pltpu.VMEM((LOCAL, SEQ * CAP), BF16),
            pltpu.VMEM((LOCAL, SEQ * CAP), BF16),
            pltpu.VMEM((16, 1, JUNC), F32),
            pltpu.VMEM((LOCAL, LENGTH), F32),
            pltpu.VMEM((LAYERS, LOCAL, LENGTH), BF16),
            pltpu.VMEM((2, LOCAL, 128), BF16),
            pltpu.VMEM((LAYERS, 2, LOCAL, 128), BF16),
            pltpu.VMEM((LAYERS, 2, 3, 192, LENGTH), BF16),
            pltpu.VMEM((LAYERS, 2, 3, 192, LENGTH), BF16),
            pltpu.VMEM((2, SIDE, HALF, LENGTH), F32),
            pltpu.VMEM((LAYERS, 2, SIDE, HALF, LENGTH), BF16),
            pltpu.VMEM((LAYERS, 2, 3, HALF, LENGTH), BF16),
            pltpu.VMEM((LAYERS, 16, 1, LENGTH), F32),
            pltpu.VMEM((LAYERS, 2, 144, CHANNELS), BF16),
            pltpu.VMEM((LAYERS, 144, CHANNELS), BF16),
            pltpu.VMEM((LAYERS, SIDE, 144, 384), BF16),
            pltpu.VMEM((LAYERS, 3, 144, 384), BF16),
            pltpu.VMEM((LAYERS, 2, SIDE, 144, 384), BF16),
            pltpu.VMEM((128, 128), F32),
            pltpu.VMEM((SEQ, 8, 128), F32),
            dma(4, 2),
            dma(4, 2),
            dma(LAYERS, 30),
            dma(LAYERS, 16, 2),
            dma(7),
            dma(7),
            dma(7),
            dma(7),
            dma(7),
            dma(7),
            dma(15),
            dma(15),
            dma(LAYERS, 2, 6),
            dma(LAYERS, 2, 6),
            dma(LAYERS, 15),
            dma(LAYERS, 15),
            dma(LAYERS, 11),
            dma(LAYERS, 11),
            dma(7),
            dma(7),
            dma(LAYERS, 15),
            dma(LAYERS, 15),
            dma(2),
        ],
        compiler_params=pltpu.CompilerParams(
            collective_id=0, has_side_effects=True, vmem_limit_bytes=62 * 1024 * 1024
        ),
        name="conv_section",
    )(*operands)


def local(
    sequence_in,
    conv_weight,
    norm_gain,
    tissue_scale,
    donor_offset,
    acceptor_owner,
    acceptor_offset,
    tissue,
    tower_grad,
    score_grad,
):
    stacked = conv_weight.transpose(0, 2, 1, 3).reshape(LAYERS, 3 * LOCAL, CHANNELS)
    table = lax.dynamic_slice_in_dim(tissue_scale, lax.axis_index("tp") * LOCAL, LOCAL, 1)
    scores, grad, weights, gains = section(
        sequence_in,
        stacked,
        norm_gain,
        tower_grad,
        table,
        acceptor_owner.T,
        acceptor_offset[None, :],
        donor_offset[None, :],
        tissue[None, :],
        score_grad[None, :],
    )
    weights = weights.reshape(LAYERS, 3, LOCAL, CHANNELS).transpose(0, 2, 1, 3).astype(F32)
    return (scores[0], grad, weights, gains)


def solution(mesh):
    return jax.shard_map(
        local,
        mesh=mesh,
        in_specs=(
            P("tp", "seq"),
            P(None, "tp", None, None),
            P(None, "tp"),
            P(),
            P("seq"),
            P("seq", None),
            P("seq"),
            P("seq"),
            P("tp", "seq"),
            P("seq"),
        ),
        out_specs=(P("seq"), P("tp", "seq"), P(None, "tp", None, None), P(None, "tp")),
        check_vma=False,
    )
```

```python
import math

import jax
import jax.numpy as jnp
from jax import lax
from jax.experimental import pallas as pl
from jax.experimental.pallas import tpu as pltpu
from jax.sharding import PartitionSpec as P

CHANNELS = 1536
LAYERS = 3
LOCAL = 96
HALF = 48
LENGTH = 512
WIN = 640
SIDE = 4
SEQ = 8
JUNC = 256
CAP = 128
MESH = pl.DeviceIdType.MESH
EPSILON = 1e-06
ROOT = math.sqrt(CHANNELS)
GELU_C = math.sqrt(2.0 / math.pi)
GELU_A = 0.044715
F32 = jnp.float32
BF16 = jnp.bfloat16
NEAR = (1, 3, 2)


def remote(src, dst, send_sem, recv_sem, device):
    return pltpu.make_async_remote_copy(
        src_ref=src,
        dst_ref=dst,
        send_sem=send_sem,
        recv_sem=recv_sem,
        device_id=device,
        device_id_type=MESH,
    )


def dot(a, b):
    return jnp.dot(a, b, preferred_element_type=F32)


def dot_rows(a, b):
    return lax.dot_general(a, b, (((1,), (1,)), ((), ())), preferred_element_type=F32)


def section_kernel(
    seq_ref,
    w_hbm,
    gain_in,
    tower_hbm,
    table_hbm,
    owner_ref,
    offset_ref,
    donor_ref,
    tissue_ref,
    sgrad_ref,
    scores_ref,
    grad_ref,
    wgrad_ref,
    gains_ref,
    w_ref,
    tower_ref,
    gain_ref,
    window,
    turn,
    tab,
    gst,
    hid,
    mm,
    vv,
    ysum,
    pw,
    inv,
    wt,
    meta_all,
    pick,
    slots,
    donor_hot,
    tissue_rows,
    state3,
    acc_tx,
    acc_rx,
    ab_tx,
    ab_rx,
    sc_all,
    up,
    gbuf,
    halo_rx,
    halo_b,
    pab,
    rx,
    sf,
    sab,
    ry,
    inn,
    wg,
    wrx,
    wz_tx,
    wz_rx,
    wres,
    stage,
    gg,
    gg_all,
    halo_send,
    halo_recv,
    gather_send,
    gather_recv,
    meta_send,
    meta_recv,
    acc_send,
    acc_recv,
    ab_send,
    ab_recv,
    sc_send,
    sc_recv,
    rs_send,
    rs_recv,
    inn_send,
    inn_recv,
    w_send,
    w_recv,
    gg_send,
    gg_recv,
    pw_send,
    pw_recv,
    load_sem,
):
    s = lax.axis_index("seq")
    me = lax.axis_index("tp")
    mx = me // SIDE
    my = lax.rem(me, SIDE)
    mz = s // 2
    core = lax.rem(s, 2)

    def xpeer(d):
        return lax.rem(mx + d, SIDE) * SIDE + my

    def ypeer(d):
        return mx * SIDE + lax.rem(my + d, SIDE)

    def tpeer(d):
        return lax.rem(me + d, SIDE * SIDE)

    def speer(d):
        return lax.rem(s + d, SEQ)

    def zpeer(d):
        return lax.rem(mz + d, SIDE) * 2 + core

    partner = mz * 2 + 1 - core

    load_w = pltpu.make_async_copy(w_hbm, w_ref, load_sem.at[0])
    load_tower = pltpu.make_async_copy(tower_hbm, tower_ref, load_sem.at[1])
    start = jnp.minimum(me * LOCAL // 128, CHANNELS // 128 - 2) * 128
    skip = me * LOCAL - start
    load_table = pltpu.make_async_copy(
        table_hbm.at[:, pl.ds(pl.multiple_of(start, 128), 256)], window, load_sem.at[2]
    )
    load_w.start()
    load_table.start()
    load_tower.start()

    barrier = pltpu.get_barrier_semaphore()
    for d in range(1, SIDE * SIDE):
        pl.semaphore_signal(barrier, inc=1, device_id={"tp": tpeer(d)}, device_id_type=MESH)
    for d in range(1, SEQ):
        pl.semaphore_signal(barrier, inc=1, device_id={"seq": speer(d)}, device_id_type=MESH)
    turn[...] = jnp.zeros((128, 128), F32)
    for k in range(3):
        turn[56 + 3 * k : 59 + 3 * k, 0:LOCAL] = gain_in[...]
    gain_ref[...] = turn[...].T[0:LOCAL]
    pl.semaphore_wait(barrier, SIDE * SIDE - 1 + SEQ - 1)

    pending = []

    def begin(copy):
        copy.start()
        pending.append(copy)

    def halo_left(src, dst, k):
        return remote(src.at[:, 0:128], dst.at[0], halo_send.at[k, 0], halo_recv.at[k, 0], {"seq": s - 1})

    def halo_right(src, dst, k):
        return remote(src.at[:, 384:512], dst.at[1], halo_send.at[k, 1], halo_recv.at[k, 1], {"seq": s + 1})

    def halo_start(src, dst, k):
        @pl.when(s > 0)
        def _():
            halo_left(src, dst, k).start()

        @pl.when(s < SEQ - 1)
        def _():
            halo_right(src, dst, k).start()

        @pl.when(s == 0)
        def _():
            dst[1] = jnp.zeros((LOCAL, 128), BF16)

        @pl.when(s == SEQ - 1)
        def _():
            dst[0] = jnp.zeros((LOCAL, 128), BF16)

    def halo_wait(src, dst, k):
        @pl.when(s > 0)
        def _():
            halo_left(src, dst, k).wait_send()
            remote(
                src.at[:, 384:512], dst.at[1], halo_send.at[k, 1], halo_recv.at[k, 1], {"seq": s - 1}
            ).wait_recv()

        @pl.when(s < SEQ - 1)
        def _():
            halo_right(src, dst, k).wait_send()
            remote(
                src.at[:, 0:128], dst.at[0], halo_send.at[k, 0], halo_recv.at[k, 0], {"seq": s + 1}
            ).wait_recv()

    lane = lax.broadcasted_iota(jnp.int32, (LOCAL, 128), 1)

    def halo_tile(dst):
        return jnp.where(lane < 64, dst[0].astype(F32), dst[1].astype(F32))

    halo_start(seq_ref, halo_rx, 0)

    gain = gain_ref[...]
    high = gain.astype(BF16).astype(F32)
    rest = gain - high
    mid = rest.astype(BF16).astype(F32)
    low = rest - mid
    packed = jnp.where(lane < 59, high, jnp.where(lane < 62, mid, low))
    in_gain = (lane >= 56) & (lane < 65)

    for h in range(2):
        gst[0, me, h, :, 0:512] = seq_ref[HALF * h : HALF * h + HALF, :]
    halo_wait(seq_ref, halo_rx, 0)
    tile = jnp.where(in_gain, packed, halo_tile(halo_rx)).astype(BF16)
    for h in range(2):
        gst[0, me, h, :, 512:640] = tile[HALF * h : HALF * h + HALF, :]

    col = lax.broadcasted_iota(jnp.int32, (LOCAL, WIN), 1)
    outside = ((s == SEQ - 1) & (col >= 512) & (col < 576)) | ((s == 0) & (col >= 576))

    def transpose_weights(layer):
        for x in range(SIDE):
            block = w_ref[layer, :, 384 * x : 384 * x + 384].astype(F32).T.astype(BF16)
            for y in range(SIDE):
                a = 192 * x + HALF * y
                b = 768 + 192 * y + HALF * x
                wt[layer, a : a + HALF, :] = block[96 * y : 96 * y + HALF]
                wt[layer, b : b + HALF, :] = block[96 * y + HALF : 96 * y + 96]

    def one_hot(rows, row_ids, base):
        ids = lax.broadcasted_iota(jnp.int32, (rows, JUNC), 0) + base
        return jnp.where(ids == row_ids, 1.0, 0.0).astype(BF16)

    def prepare_tissues():
        load_table.wait()
        tab[...] = jnp.zeros((384, 128), F32)
        tab[0 : window.shape[0], :] = pltpu.roll(window[...], lax.rem(256 - skip, 256), 1)[:, 0:128]
        table = tab[...].T[0:LOCAL]
        t_high = table.astype(BF16)
        t_rest = table - t_high.astype(F32)
        t_mid = t_rest.astype(BF16)
        t_low = (t_rest - t_mid.astype(F32)).astype(BF16)
        hot = one_hot(384, tissue_ref[...], 0)
        tissue_rows[...] = dot(t_high, hot) + dot(t_mid, hot) + dot(t_low, hot)
        donor_hot[...] = one_hot(LENGTH, donor_ref[...], 0)

    def send_meta():
        owner = owner_ref[...]
        member = one_hot(16, owner, 0)
        first = lax.broadcasted_iota(jnp.int32, (JUNC, JUNC), 0)
        second = lax.broadcasted_iota(jnp.int32, (JUNC, JUNC), 1)
        rank = dot(member, jnp.where(first <= second, 1.0, 0.0).astype(BF16))
        slot = jnp.sum(member.astype(F32) * rank, axis=0, keepdims=True) - 1.0
        slot = slot.astype(jnp.int32)
        meta_all[s] = (slot * SEQ + owner) * LENGTH + offset_ref[...]
        for d in range(1, SEQ):
            begin(
                remote(
                    meta_all.at[s], meta_all.at[s], meta_send.at[d - 1], meta_recv.at[d - 1], {"seq": speer(d)}
                )
            )
        ids = lax.broadcasted_iota(jnp.int32, (CAP, JUNC), 0)
        for d in range(SEQ):
            mine = (ids == slot) & (owner == speer(d))
            slots[CAP * d : CAP * d + CAP, :] = jnp.where(mine, 1.0, 0.0).astype(BF16)

    def wait_meta():
        for d in range(1, SEQ):
            src = speer(SEQ - d)
            remote(
                meta_all.at[src], meta_all.at[src], meta_send.at[d - 1], meta_recv.at[d - 1], {"seq": src}
            ).wait_recv()

    def prepare_picks(which):
        for d in which:
            row = meta_all[speer(d)]
            place = one_hot(LENGTH, row & (SEQ * LENGTH - 1), s * LENGTH)
            slot = one_hot(CAP, lax.shift_right_logical(row, 12), 0)
            pick[:, CAP * d : CAP * d + CAP] = dot_rows(place, slot).astype(BF16)

    for layer in range(LAYERS):
        reach = 2 ** (layer + 3)
        count = [0]

        def go(block, h, peer, layer=layer, count=count):
            begin(
                remote(
                    gst.at[layer, block, h],
                    gst.at[layer, block, h],
                    gather_send.at[layer, count[0]],
                    gather_recv.at[layer, block, h],
                    {"tp": peer},
                )
            )
            count[0] += 1

        def arrived(block, h, layer=layer):
            remote(
                gst.at[layer, block, h],
                gst.at[layer, block, h],
                gather_send.at[layer, 0],
                gather_recv.at[layer, block, h],
                {"tp": xpeer(1)},
            ).wait_recv()

        squares = jnp.concatenate([gst[layer, me, 0], gst[layer, me, 1]], axis=0).astype(F32)
        pw[layer, me] = jnp.sum(squares * squares, axis=0, keepdims=True)
        for d in range(1, SIDE * SIDE):
            begin(
                remote(
                    pw.at[layer, me],
                    pw.at[layer, me],
                    pw_send.at[layer, d - 1],
                    pw_recv.at[layer, d - 1],
                    {"tp": tpeer(d)},
                )
            )
        def at(h, p, q):
            dx, dy = (p, q) if h == 0 else (q, p)
            return lax.rem(mx + dx, SIDE) * SIDE + lax.rem(my + dy, SIDE)

        waited = set()

        def wait_block(h, p, q, at=at, waited=waited, arrived=arrived):
            if (h, p, q) not in waited:
                waited.add((h, p, q))
                arrived(at(h, p, q), h)

        def relay(h, p, q, targets, at=at, go=go, wait_block=wait_block):
            if (p, q) != (0, 0):
                wait_block(h, p, q)
            for target in targets:
                go(at(h, p, q), h, at(h, *target))

        def second_axis(p, relay=relay):
            for h in range(2):
                if p % 2 == 0:
                    relay(h, p, 3, ((0, 1),))
                else:
                    relay(h, p, 1, ((0, 3),))

        ahead = (3, 1)
        for h in range(2):
            relay(h, 0, 0, ((1, 0), (3, 0)))
        for h in range(2):
            relay(h, 0, 0, ((0, 1), (0, 3)))
        for h in range(2):
            relay(h, ahead[h], 0, ((SIDE - ahead[h], 0), (0, 1), (0, 3)))
        for h in range(2):
            relay(h, SIDE - ahead[h], 0, ((0, 1), (0, 3)))
        second_axis(0)
        if layer == 0:
            send_meta()
            load_w.wait()
        else:
            vv[layer - 1] = dot(w_ref[layer - 1], mm[layer - 1])
        for h in range(2):
            relay(h, 2, 0, ((0, 1), (0, 3)))
        second_axis(1)
        second_axis(3)

        for d in range(1, SIDE * SIDE):
            src = pw.at[layer, tpeer(SIDE * SIDE - d)]
            remote(
                src, src, pw_send.at[layer, d - 1], pw_recv.at[layer, d - 1], {"tp": tpeer(d)}
            ).wait_recv()
        power = jnp.sum(pw[layer], axis=0) / CHANNELS
        inverse = 1.0 / jnp.sqrt(power + EPSILON)
        inv[layer] = jnp.broadcast_to(inverse, (8, WIN))

        def hide(block, carry, layer=layer):
            scale = inv[layer, 0:1, :]
            for h in range(2):
                head = gst[0, block, h, :, 512:640].astype(F32)
                g = (
                    head[:, 56 + layer : 57 + layer]
                    + head[:, 59 + layer : 60 + layer]
                    + head[:, 62 + layer : 63 + layer]
                )
                rows = pl.ds(pl.multiple_of(block * LOCAL + HALF * h, 16), HALF)
                raw = gst[layer, block, h, :, 0:LENGTH].astype(F32) * g
                x = raw * scale[:, 0:LENGTH]
                xx = x * x
                t = jnp.tanh(GELU_C * (x + GELU_A * (xx * x)))
                upper = 0.5 * (1.0 + t)
                hid[layer, rows, 0:LENGTH] = (x * upper).astype(BF16)
                slope = upper + (0.5 * x) * (1.0 - t * t) * (GELU_C + (3.0 * GELU_A * GELU_C) * xx)
                mm[layer, rows, :] = (raw * slope).astype(BF16)
                x = gst[layer, block, h, :, LENGTH:WIN].astype(F32) * scale[:, LENGTH:WIN] * g
                t = jnp.tanh(GELU_C * (x + GELU_A * (x * x * x)))
                hid[layer, rows, LENGTH:WIN] = (0.5 * x * (1.0 + t)).astype(BF16)
            return carry

        for d in (0,) + NEAR:
            group = lax.rem(mx + d, SIDE)
            for e in (0,) + NEAR:
                if d + e > 0:
                    wait_block(0, d, e)
                    wait_block(1, e, d)
                if d == NEAR[-1]:
                    hide(group * SIDE + lax.rem(my + e, SIDE), 0)
            if d != NEAR[-1]:
                lax.fori_loop(group * SIDE, group * SIDE + SIDE, hide, 0)
            span = pl.ds(pl.multiple_of(group * 384, 128), 384)
            part = dot(w_ref[layer, :, span], hid[layer, span, :])
            if d == 0:
                ysum[...] = part
                second_axis(2)
                transpose_weights(layer)
                if layer == 0:
                    prepare_tissues()
                if layer == 1:
                    wait_meta()
                    prepare_picks(range(0, 4))
                if layer == 2:
                    prepare_picks(range(4, 8))
            elif d != NEAR[-1]:
                ysum[...] += part
            else:
                y = ysum[...] + part

        mixed = pltpu.roll(y[0:96], reach, 1) + y[96:192] + pltpu.roll(y[192:288], WIN - reach, 1)
        own = jnp.concatenate([gst[layer, me, 0], gst[layer, me, 1]], axis=0)
        state = own.astype(F32) + mixed
        if layer < LAYERS - 1:
            state = jnp.where(outside, 0.0, state).astype(BF16)
            for h in range(2):
                gst[layer + 1, me, h] = state[HALF * h : HALF * h + HALF, :]
        else:
            state3[...] = state[:, 0:LENGTH].astype(BF16)

    def acc_copy(d):
        return remote(
            acc_tx.at[:, CAP * d : CAP * d + CAP],
            acc_rx.at[:, CAP * (SEQ - d) : CAP * (SEQ - d) + CAP],
            acc_send.at[d - 1],
            acc_recv.at[d - 1],
            {"seq": speer(d)},
        )

    def ab_copy(d):
        return remote(
            ab_tx.at[:, CAP * d : CAP * d + CAP],
            ab_rx.at[:, CAP * (SEQ - d) : CAP * (SEQ - d) + CAP],
            ab_send.at[d - 1],
            ab_recv.at[d - 1],
            {"seq": speer(d)},
        )

    acc_tx[...] = dot(state3[...], pick[...]).astype(BF16)
    for d in range(1, SEQ):
        begin(acc_copy(d))
    acc_rx[:, 0:CAP] = acc_tx[:, 0:CAP]
    donor = dot(state3[...], donor_hot[...])
    load_tower.wait()
    weight_j = sgrad_ref[...] / ROOT
    rows_q = tissue_rows[...]
    accept_back = (weight_j * donor * rows_q).astype(BF16)
    ab_tx[...] = dot_rows(accept_back, slots[...]).astype(BF16)
    for d in range(1, SEQ):
        begin(ab_copy(d))
    ab_rx[:, 0:CAP] = ab_tx[:, 0:CAP]
    vv[LAYERS - 1] = dot(w_ref[LAYERS - 1], mm[LAYERS - 1])
    for d in range(1, SEQ):
        acc_copy(d).wait_recv()
    accept = dot(acc_rx[...], slots[...])
    donor_back = weight_j * accept * rows_q
    d_high = donor_back.astype(BF16)
    d_low = (donor_back - d_high.astype(F32)).astype(BF16)
    up[...] = tower_ref[...] + dot_rows(d_high, donor_hot[...]) + dot_rows(d_low, donor_hot[...])
    sc_all[me] = jnp.sum(donor * accept * rows_q, axis=0, keepdims=True) / ROOT
    for d in range(1, SEQ):
        ab_copy(d).wait_recv()
    up[...] += dot_rows(ab_rx[...], pick[...])
    for d in range(1, SIDE * SIDE):
        begin(
            remote(sc_all.at[me], sc_all.at[me], sc_send.at[d - 1], sc_recv.at[d - 1], {"tp": tpeer(d)})
        )

    def w_cores(layer):
        return remote(
            wg.at[layer, 1 - core], wrx.at[layer], w_send.at[layer, 0], w_recv.at[layer, 0], {"seq": partner}
        )

    def w_slices(layer, d):
        return remote(
            wz_tx.at[layer, lax.rem(mz + d, SIDE)],
            wz_rx.at[layer, d - 1],
            w_send.at[layer, d],
            w_recv.at[layer, d],
            {"seq": zpeer(d)},
        )

    def w_result(layer, d):
        return remote(
            wres.at[layer, core, mz],
            wres.at[layer, core, mz],
            w_send.at[layer, 3 + d],
            w_recv.at[layer, 3 + d],
            {"seq": zpeer(d)},
        )

    def w_share(layer, d):
        part = wres.at[layer, core, lax.rem(mz + SIDE - d, SIDE)]
        return remote(part, part, w_send.at[layer, 7 + d], w_recv.at[layer, 7 + d], {"seq": partner})

    def w_step2(layer):
        w_cores(layer).wait_recv()
        summed = wg[layer, core].astype(F32) + wrx[layer].astype(F32)
        for q in range(SIDE):
            wz_tx[layer, q] = summed[:, 384 * q : 384 * q + 384].astype(BF16)
        for d in NEAR:
            begin(w_slices(layer, d))

    def w_step3(layer):
        result = wz_tx[layer, mz].astype(F32)
        for d in NEAR:
            w_slices(layer, d).wait_recv()
            result = result + wz_rx[layer, d - 1].astype(F32)
        wres[layer, core, mz] = result.astype(BF16)
        for d in NEAR:
            begin(w_result(layer, d))
        begin(w_share(layer, 0))

    def w_step4(layer):
        for d in NEAR:
            src = wres.at[layer, core, lax.rem(mz + SIDE - d, SIDE)]
            remote(
                src, src, w_send.at[layer, 3 + d], w_recv.at[layer, 3 + d], {"seq": zpeer(d)}
            ).wait_recv()
            begin(w_share(layer, d))

    def store_w(layer):
        return pltpu.make_async_copy(stage.at[layer], wgrad_ref.at[layer], load_sem.at[3 + layer])

    def w_step5(layer):
        for d in range(SIDE):
            part = wres.at[layer, 1 - core, lax.rem(mz + SIDE - d, SIDE)]
            remote(
                part, part, w_send.at[layer, 7 + d], w_recv.at[layer, 7 + d], {"seq": partner}
            ).wait_recv()
        for h in range(2):
            for q in range(SIDE):
                stage[layer, 144 * h : 144 * h + 144, 384 * q : 384 * q + 384] = wres[layer, h, q].astype(F32)
        store_w(layer).start()

    gg[...] = jnp.zeros((128, 128), F32)
    for layer in reversed(range(LAYERS)):
        reach = 2 ** (layer + 3)
        shifts = (WIN - reach, 0, reach)
        gbuf[layer] = up[...].astype(BF16)
        halo_start(gbuf.at[layer], halo_b.at[layer], layer + 1)
        g = gbuf[layer].astype(F32)

        def shifted(window, shifts=shifts):
            rolled = [pltpu.roll(window, k, 1) if k else window for k in shifts]
            return jnp.concatenate(rolled, axis=0)

        inner_g = shifted(jnp.concatenate([g, jnp.zeros((LOCAL, 128), F32)], axis=1)).astype(BF16)
        for q in range(3):
            part = dot_rows(inner_g, hid[layer, 512 * q : 512 * q + 512, :]).astype(BF16)
            for h in range(2):
                wg[layer, h, :, 512 * q : 512 * q + 512] = part[144 * h : 144 * h + 144]
        begin(w_cores(layer))
        if layer < LAYERS - 1:
            w_step4(layer + 1)
        halo_wait(gbuf.at[layer], halo_b.at[layer], layer + 1)
        full_g = shifted(jnp.concatenate([g, halo_tile(halo_b.at[layer])], axis=1))
        full_g = full_g[:, 0:LENGTH]
        inn[layer, me] = jnp.sum(full_g * vv[layer], axis=0, keepdims=True)
        for d in range(1, SIDE * SIDE):
            begin(
                remote(
                    inn.at[layer, me],
                    inn.at[layer, me],
                    inn_send.at[layer, d - 1],
                    inn_recv.at[layer, d - 1],
                    {"tp": tpeer(d)},
                )
            )
        full_g = full_g.astype(BF16)

        def chunk(h, index, full_g=full_g, layer=layer):
            rows = pl.ds(pl.multiple_of(768 * h + 192 * index, 16), 192)
            return dot(wt[layer, rows, :], full_g)

        def rs_one(h, d, layer=layer):
            return remote(
                pab.at[layer, h, d - 1],
                rx.at[layer, h, d - 1],
                rs_send.at[layer, h, d - 1],
                rs_recv.at[layer, h, d - 1],
                {"tp": xpeer(d) if h == 0 else ypeer(d)},
            )

        def rs_two(h, d, layer=layer):
            index = lax.rem((my if h == 0 else mx) + d, SIDE)
            return remote(
                sab.at[layer, h, index],
                ry.at[layer, h, d - 1],
                rs_send.at[layer, h, 2 + d],
                rs_recv.at[layer, h, 2 + d],
                {"tp": ypeer(d) if h == 0 else xpeer(d)},
            )

        for d in NEAR:
            for h in range(2):
                base = mx if h == 0 else my
                pab[layer, h, d - 1] = chunk(h, lax.rem(base + d, SIDE)).astype(BF16)
                begin(rs_one(h, d))
        for h in range(2):
            sf[h] = chunk(h, mx if h == 0 else my).reshape(SIDE, HALF, LENGTH)
        w_step2(layer)
        for h in range(2):
            for d in NEAR:
                rs_one(h, d).wait_recv()
                sf[h] += rx[layer, h, d - 1].astype(F32).reshape(SIDE, HALF, LENGTH)
            sab[layer, h] = sf[h].astype(BF16)
            for d in NEAR:
                begin(rs_two(h, d))
            if h == 0 and layer == 0:
                w_step3(layer)
        if layer > 0:
            w_step3(layer)
        if layer < LAYERS - 1:
            w_step5(layer + 1)

        x = (seq_ref[...] if layer == 0 else jnp.concatenate(
            [gst[layer, me, 0, :, 0:LENGTH], gst[layer, me, 1, :, 0:LENGTH]], axis=0
        )).astype(F32)
        scale = inv[layer, 0:1, 0:LENGTH]
        g_col = gain_ref[:, 56 + layer : 57 + layer]
        norm = x * scale
        pre = norm * g_col
        t = jnp.tanh(GELU_C * (pre + GELU_A * (pre * pre * pre)))
        slope = 0.5 * (1.0 + t) + 0.5 * pre * (1.0 - t * t) * (
            GELU_C * (1.0 + 3.0 * GELU_A * (pre * pre))
        )
        halves = []
        for h in range(2):
            back = sf[h, my if h == 0 else mx]
            for d in NEAR:
                rs_two(h, d).wait_recv()
                back = back + ry[layer, h, d - 1].astype(F32)
            halves.append(back)
        back_pre = jnp.concatenate(halves, axis=0) * slope
        back_norm = back_pre * g_col
        gain_col = jnp.sum(back_pre * norm, axis=1, keepdims=True)
        gg[0:LOCAL, :] = jnp.where(lane == layer, gain_col, gg[0:LOCAL, :])
        if layer == 0:
            gg_all[s] = gg[...].T[0:8]
            for d in range(1, SEQ):
                begin(
                    remote(
                        gg_all.at[s], gg_all.at[s], gg_send.at[d - 1], gg_recv.at[d - 1], {"seq": speer(d)}
                    )
                )
        for d in range(1, SIDE * SIDE):
            src = inn.at[layer, tpeer(SIDE * SIDE - d)]
            remote(
                src, src, inn_send.at[layer, d - 1], inn_recv.at[layer, d - 1], {"tp": tpeer(d)}
            ).wait_recv()
        inner = jnp.sum(inn[layer], axis=0)
        up[...] = up[...] + scale * back_norm - x * (scale * scale * scale) * (inner / CHANNELS)

    grad_ref[...] = up[...]
    w_step4(0)
    for d in range(1, SIDE * SIDE):
        src = sc_all.at[tpeer(SIDE * SIDE - d)]
        remote(src, src, sc_send.at[d - 1], sc_recv.at[d - 1], {"tp": tpeer(d)}).wait_recv()
    scores_ref[...] = jnp.sum(sc_all[...], axis=0)
    for d in range(1, SEQ):
        src = gg_all.at[speer(SEQ - d)]
        remote(src, src, gg_send.at[d - 1], gg_recv.at[d - 1], {"seq": speer(d)}).wait_recv()
    gains_ref[...] = jnp.sum(gg_all[...], axis=0)[0:LAYERS, 0:LOCAL]
    w_step5(0)
    for layer in range(LAYERS):
        store_w(layer).wait()
    for copy in pending:
        copy.wait_send()


def dma(*shape):
    return pltpu.SemaphoreType.DMA(shape)


def section(*operands):
    vmem = pl.BlockSpec(memory_space=pltpu.VMEM)
    hbm = pl.BlockSpec(memory_space=pl.ANY)
    return pl.pallas_call(
        section_kernel,
        out_shape=(
            jax.ShapeDtypeStruct((1, JUNC), F32),
            jax.ShapeDtypeStruct((LOCAL, LENGTH), F32),
            jax.ShapeDtypeStruct((LAYERS, 3 * LOCAL, CHANNELS), F32),
            jax.ShapeDtypeStruct((LAYERS, LOCAL), F32),
        ),
        in_specs=[vmem, hbm, vmem, hbm, hbm] + [vmem] * 5,
        out_specs=(vmem, vmem, hbm, vmem),
        scratch_shapes=[
            pltpu.VMEM((LAYERS, 3 * LOCAL, CHANNELS), BF16),
            pltpu.VMEM((LOCAL, LENGTH), F32),
            pltpu.VMEM((LOCAL, 128), F32),
            pltpu.VMEM((367, 256), F32),
            pltpu.VMEM((128, 128), F32),
            pltpu.VMEM((384, 128), F32),
            pltpu.VMEM((LAYERS, 16, 2, HALF, WIN), BF16),
            pltpu.VMEM((LAYERS, CHANNELS, WIN), BF16),
            pltpu.VMEM((LAYERS, CHANNELS, LENGTH), BF16),
            pltpu.VMEM((LAYERS, 3 * LOCAL, LENGTH), F32),
            pltpu.VMEM((3 * LOCAL, WIN), F32),
            pltpu.VMEM((LAYERS, 16, 1, WIN), F32),
            pltpu.VMEM((LAYERS, 8, WIN), F32),
            pltpu.VMEM((LAYERS, CHANNELS, 3 * LOCAL), BF16),
            pltpu.VMEM((SEQ, 1, JUNC), jnp.int32),
            pltpu.VMEM((LENGTH, SEQ * CAP), BF16),
            pltpu.VMEM((SEQ * CAP, JUNC), BF16),
            pltpu.VMEM((LENGTH, JUNC), BF16),
            pltpu.VMEM((LOCAL, JUNC), F32),
            pltpu.VMEM((LOCAL, LENGTH), BF16),
            pltpu.VMEM((LOCAL, SEQ * CAP), BF16),
            pltpu.VMEM((LOCAL, SEQ * CAP), BF16),
            pltpu.VMEM((LOCAL, SEQ * CAP), BF16),
            pltpu.VMEM((LOCAL, SEQ * CAP), BF16),
            pltpu.VMEM((16, 1, JUNC), F32),
            pltpu.VMEM((LOCAL, LENGTH), F32),
            pltpu.VMEM((LAYERS, LOCAL, LENGTH), BF16),
            pltpu.VMEM((2, LOCAL, 128), BF16),
            pltpu.VMEM((LAYERS, 2, LOCAL, 128), BF16),
            pltpu.VMEM((LAYERS, 2, 3, 192, LENGTH), BF16),
            pltpu.VMEM((LAYERS, 2, 3, 192, LENGTH), BF16),
            pltpu.VMEM((2, SIDE, HALF, LENGTH), F32),
            pltpu.VMEM((LAYERS, 2, SIDE, HALF, LENGTH), BF16),
            pltpu.VMEM((LAYERS, 2, 3, HALF, LENGTH), BF16),
            pltpu.VMEM((LAYERS, 16, 1, LENGTH), F32),
            pltpu.VMEM((LAYERS, 2, 144, CHANNELS), BF16),
            pltpu.VMEM((LAYERS, 144, CHANNELS), BF16),
            pltpu.VMEM((LAYERS, SIDE, 144, 384), BF16),
            pltpu.VMEM((LAYERS, 3, 144, 384), BF16),
            pltpu.VMEM((LAYERS, 2, SIDE, 144, 384), BF16),
            pltpu.VMEM((LAYERS, 3 * LOCAL, CHANNELS), F32),
            pltpu.VMEM((128, 128), F32),
            pltpu.VMEM((SEQ, 8, 128), F32),
            dma(4, 2),
            dma(4, 2),
            dma(LAYERS, 30),
            dma(LAYERS, 16, 2),
            dma(7),
            dma(7),
            dma(7),
            dma(7),
            dma(7),
            dma(7),
            dma(15),
            dma(15),
            dma(LAYERS, 2, 6),
            dma(LAYERS, 2, 6),
            dma(LAYERS, 15),
            dma(LAYERS, 15),
            dma(LAYERS, 11),
            dma(LAYERS, 11),
            dma(7),
            dma(7),
            dma(LAYERS, 15),
            dma(LAYERS, 15),
            dma(6),
        ],
        compiler_params=pltpu.CompilerParams(
            collective_id=0, has_side_effects=True, vmem_limit_bytes=62 * 1024 * 1024
        ),
        name="conv_section",
    )(*operands)


def local(
    sequence_in,
    conv_weight,
    norm_gain,
    tissue_scale,
    donor_offset,
    acceptor_owner,
    acceptor_offset,
    tissue,
    tower_grad,
    score_grad,
):
    stacked = conv_weight.transpose(0, 2, 1, 3).reshape(LAYERS, 3 * LOCAL, CHANNELS)
    scores, grad, weights, gains = section(
        sequence_in,
        stacked,
        norm_gain,
        tower_grad,
        tissue_scale,
        acceptor_owner.T,
        acceptor_offset[None, :],
        donor_offset[None, :],
        tissue[None, :],
        score_grad[None, :],
    )
    weights = weights.reshape(LAYERS, 3, LOCAL, CHANNELS).transpose(0, 2, 1, 3)
    return (scores[0], grad, weights, gains)


def solution(mesh):
    return jax.shard_map(
        local,
        mesh=mesh,
        in_specs=(
            P("tp", "seq"),
            P(None, "tp", None, None),
            P(None, "tp"),
            P(),
            P("seq"),
            P("seq", None),
            P("seq"),
            P("seq"),
            P("tp", "seq"),
            P("seq"),
        ),
        out_specs=(P("seq"), P("tp", "seq"), P(None, "tp", None, None), P(None, "tp")),
        check_vma=False,
    )
```

```python
import math

import jax
import jax.numpy as jnp
from jax import lax
from jax.experimental import pallas as pl
from jax.experimental.pallas import tpu as pltpu
from jax.sharding import PartitionSpec as P

CHANNELS = 1536
LAYERS = 3
LOCAL = 96
HALF = 48
LENGTH = 512
WIN = 640
SIDE = 4
SEQ = 8
JUNC = 256
CAP = 128
MESH = pl.DeviceIdType.MESH
EPSILON = 1e-06
ROOT = math.sqrt(CHANNELS)
GELU_C = math.sqrt(2.0 / math.pi)
GELU_A = 0.044715
F32 = jnp.float32
BF16 = jnp.bfloat16
NEAR = (1, 3, 2)


def remote(src, dst, send_sem, recv_sem, device):
    return pltpu.make_async_remote_copy(
        src_ref=src,
        dst_ref=dst,
        send_sem=send_sem,
        recv_sem=recv_sem,
        device_id=device,
        device_id_type=MESH,
    )


def dot(a, b):
    return jnp.dot(a, b, preferred_element_type=F32)


def dot_rows(a, b):
    return lax.dot_general(a, b, (((1,), (1,)), ((), ())), preferred_element_type=F32)


def section_kernel(
    seq_ref,
    w_hbm,
    gain_in,
    tower_hbm,
    table_hbm,
    owner_ref,
    offset_ref,
    donor_ref,
    tissue_ref,
    sgrad_ref,
    scores_ref,
    grad_ref,
    wgrad_ref,
    gains_ref,
    w_ref,
    tower_ref,
    gain_ref,
    window,
    turn,
    tab,
    gst,
    hid,
    mm,
    vv,
    ysum,
    pw,
    inv,
    wt,
    meta_all,
    pick,
    slots,
    donor_hot,
    tissue_rows,
    state3,
    acc_tx,
    acc_rx,
    ab_tx,
    ab_rx,
    sc_all,
    up,
    gbuf,
    halo_rx,
    halo_b,
    pab,
    rx,
    sf,
    sab,
    ry,
    inn,
    wg,
    wrx,
    wz_tx,
    wz_rx,
    wres,
    gg,
    gg_all,
    halo_send,
    halo_recv,
    gather_send,
    gather_recv,
    meta_send,
    meta_recv,
    acc_send,
    acc_recv,
    ab_send,
    ab_recv,
    sc_send,
    sc_recv,
    rs_send,
    rs_recv,
    inn_send,
    inn_recv,
    w_send,
    w_recv,
    gg_send,
    gg_recv,
    pw_send,
    pw_recv,
    load_sem,
):
    s = lax.axis_index("seq")
    me = lax.axis_index("tp")
    mx = me // SIDE
    my = lax.rem(me, SIDE)
    mz = s // 2
    core = lax.rem(s, 2)

    def xpeer(d):
        return lax.rem(mx + d, SIDE) * SIDE + my

    def ypeer(d):
        return mx * SIDE + lax.rem(my + d, SIDE)

    def tpeer(d):
        return lax.rem(me + d, SIDE * SIDE)

    def speer(d):
        return lax.rem(s + d, SEQ)

    def zpeer(d):
        return lax.rem(mz + d, SIDE) * 2 + core

    partner = mz * 2 + 1 - core

    load_w = pltpu.make_async_copy(w_hbm, w_ref, load_sem.at[0])
    load_tower = pltpu.make_async_copy(tower_hbm, tower_ref, load_sem.at[1])
    start = jnp.minimum(me * LOCAL // 128, CHANNELS // 128 - 2) * 128
    skip = me * LOCAL - start
    load_table = pltpu.make_async_copy(
        table_hbm.at[:, pl.ds(pl.multiple_of(start, 128), 256)], window, load_sem.at[2]
    )
    load_w.start()
    load_table.start()
    load_tower.start()

    barrier = pltpu.get_barrier_semaphore()
    for d in range(1, SIDE * SIDE):
        pl.semaphore_signal(barrier, inc=1, device_id={"tp": tpeer(d)}, device_id_type=MESH)
    for d in range(1, SEQ):
        pl.semaphore_signal(barrier, inc=1, device_id={"seq": speer(d)}, device_id_type=MESH)
    turn[...] = jnp.zeros((128, 128), F32)
    for k in range(3):
        turn[56 + 3 * k : 59 + 3 * k, 0:LOCAL] = gain_in[...]
    gain_ref[...] = turn[...].T[0:LOCAL]
    pl.semaphore_wait(barrier, SIDE * SIDE - 1 + SEQ - 1)

    pending = []

    def begin(copy):
        copy.start()
        pending.append(copy)

    def halo_left(src, dst, k):
        return remote(src.at[:, 0:128], dst.at[0], halo_send.at[k, 0], halo_recv.at[k, 0], {"seq": s - 1})

    def halo_right(src, dst, k):
        return remote(src.at[:, 384:512], dst.at[1], halo_send.at[k, 1], halo_recv.at[k, 1], {"seq": s + 1})

    def halo_start(src, dst, k):
        @pl.when(s > 0)
        def _():
            halo_left(src, dst, k).start()

        @pl.when(s < SEQ - 1)
        def _():
            halo_right(src, dst, k).start()

        @pl.when(s == 0)
        def _():
            dst[1] = jnp.zeros((LOCAL, 128), BF16)

        @pl.when(s == SEQ - 1)
        def _():
            dst[0] = jnp.zeros((LOCAL, 128), BF16)

    def halo_wait(src, dst, k):
        @pl.when(s > 0)
        def _():
            halo_left(src, dst, k).wait_send()
            remote(
                src.at[:, 384:512], dst.at[1], halo_send.at[k, 1], halo_recv.at[k, 1], {"seq": s - 1}
            ).wait_recv()

        @pl.when(s < SEQ - 1)
        def _():
            halo_right(src, dst, k).wait_send()
            remote(
                src.at[:, 0:128], dst.at[0], halo_send.at[k, 0], halo_recv.at[k, 0], {"seq": s + 1}
            ).wait_recv()

    lane = lax.broadcasted_iota(jnp.int32, (LOCAL, 128), 1)

    def halo_tile(dst):
        return jnp.where(lane < 64, dst[0].astype(F32), dst[1].astype(F32))

    halo_start(seq_ref, halo_rx, 0)

    gain = gain_ref[...]
    high = gain.astype(BF16).astype(F32)
    rest = gain - high
    mid = rest.astype(BF16).astype(F32)
    low = rest - mid
    packed = jnp.where(lane < 59, high, jnp.where(lane < 62, mid, low))
    in_gain = (lane >= 56) & (lane < 65)

    for h in range(2):
        gst[0, me, h, :, 0:512] = seq_ref[HALF * h : HALF * h + HALF, :]
    halo_wait(seq_ref, halo_rx, 0)
    tile = jnp.where(in_gain, packed, halo_tile(halo_rx)).astype(BF16)
    for h in range(2):
        gst[0, me, h, :, 512:640] = tile[HALF * h : HALF * h + HALF, :]

    col = lax.broadcasted_iota(jnp.int32, (LOCAL, WIN), 1)
    outside = ((s == SEQ - 1) & (col >= 512) & (col < 576)) | ((s == 0) & (col >= 576))

    def transpose_weights(layer):
        for x in range(SIDE):
            block = w_ref[layer, :, 384 * x : 384 * x + 384].astype(F32).T.astype(BF16)
            for y in range(SIDE):
                a = 192 * x + HALF * y
                b = 768 + 192 * y + HALF * x
                wt[layer, a : a + HALF, :] = block[96 * y : 96 * y + HALF]
                wt[layer, b : b + HALF, :] = block[96 * y + HALF : 96 * y + 96]

    def one_hot(rows, row_ids, base):
        ids = lax.broadcasted_iota(jnp.int32, (rows, JUNC), 0) + base
        return jnp.where(ids == row_ids, 1.0, 0.0).astype(BF16)

    def prepare_tissues():
        load_table.wait()
        tab[...] = jnp.zeros((384, 128), F32)
        tab[0 : window.shape[0], :] = pltpu.roll(window[...], lax.rem(256 - skip, 256), 1)[:, 0:128]
        table = tab[...].T[0:LOCAL]
        t_high = table.astype(BF16)
        t_rest = table - t_high.astype(F32)
        t_mid = t_rest.astype(BF16)
        t_low = (t_rest - t_mid.astype(F32)).astype(BF16)
        hot = one_hot(384, tissue_ref[...], 0)
        tissue_rows[...] = dot(t_high, hot) + dot(t_mid, hot) + dot(t_low, hot)
        donor_hot[...] = one_hot(LENGTH, donor_ref[...], 0)

    def send_meta():
        owner = owner_ref[...]
        member = one_hot(16, owner, 0)
        first = lax.broadcasted_iota(jnp.int32, (JUNC, JUNC), 0)
        second = lax.broadcasted_iota(jnp.int32, (JUNC, JUNC), 1)
        rank = dot(member, jnp.where(first <= second, 1.0, 0.0).astype(BF16))
        slot = jnp.sum(member.astype(F32) * rank, axis=0, keepdims=True) - 1.0
        slot = slot.astype(jnp.int32)
        meta_all[s] = (slot * SEQ + owner) * LENGTH + offset_ref[...]
        for d in range(1, SEQ):
            begin(
                remote(
                    meta_all.at[s], meta_all.at[s], meta_send.at[d - 1], meta_recv.at[d - 1], {"seq": speer(d)}
                )
            )
        ids = lax.broadcasted_iota(jnp.int32, (CAP, JUNC), 0)
        for d in range(SEQ):
            mine = (ids == slot) & (owner == speer(d))
            slots[CAP * d : CAP * d + CAP, :] = jnp.where(mine, 1.0, 0.0).astype(BF16)

    def wait_meta():
        for d in range(1, SEQ):
            src = speer(SEQ - d)
            remote(
                meta_all.at[src], meta_all.at[src], meta_send.at[d - 1], meta_recv.at[d - 1], {"seq": src}
            ).wait_recv()

    def prepare_picks(which):
        for d in which:
            row = meta_all[speer(d)]
            place = one_hot(LENGTH, row & (SEQ * LENGTH - 1), s * LENGTH)
            slot = one_hot(CAP, lax.shift_right_logical(row, 12), 0)
            pick[:, CAP * d : CAP * d + CAP] = dot_rows(place, slot).astype(BF16)

    for layer in range(LAYERS):
        reach = 2 ** (layer + 3)
        count = [0]

        def go(block, h, peer, layer=layer, count=count):
            begin(
                remote(
                    gst.at[layer, block, h],
                    gst.at[layer, block, h],
                    gather_send.at[layer, count[0]],
                    gather_recv.at[layer, block, h],
                    {"tp": peer},
                )
            )
            count[0] += 1

        def arrived(block, h, layer=layer):
            remote(
                gst.at[layer, block, h],
                gst.at[layer, block, h],
                gather_send.at[layer, 0],
                gather_recv.at[layer, block, h],
                {"tp": xpeer(1)},
            ).wait_recv()

        squares = jnp.concatenate([gst[layer, me, 0], gst[layer, me, 1]], axis=0).astype(F32)
        pw[layer, me] = jnp.sum(squares * squares, axis=0, keepdims=True)
        for d in range(1, SIDE * SIDE):
            begin(
                remote(
                    pw.at[layer, me],
                    pw.at[layer, me],
                    pw_send.at[layer, d - 1],
                    pw_recv.at[layer, d - 1],
                    {"tp": tpeer(d)},
                )
            )
        def at(h, p, q):
            dx, dy = (p, q) if h == 0 else (q, p)
            return lax.rem(mx + dx, SIDE) * SIDE + lax.rem(my + dy, SIDE)

        waited = set()

        def wait_block(h, p, q, at=at, waited=waited, arrived=arrived):
            if (h, p, q) not in waited:
                waited.add((h, p, q))
                arrived(at(h, p, q), h)

        def relay(h, p, q, targets, at=at, go=go, wait_block=wait_block):
            if (p, q) != (0, 0):
                wait_block(h, p, q)
            for target in targets:
                go(at(h, p, q), h, at(h, *target))

        def second_axis(p, relay=relay):
            for h in range(2):
                if p % 2 == 0:
                    relay(h, p, 3, ((0, 1),))
                else:
                    relay(h, p, 1, ((0, 3),))

        ahead = (3, 1)
        for h in range(2):
            relay(h, 0, 0, ((1, 0), (3, 0)))
        for h in range(2):
            relay(h, 0, 0, ((0, 1), (0, 3)))
        for h in range(2):
            relay(h, ahead[h], 0, ((SIDE - ahead[h], 0), (0, 1), (0, 3)))
        for h in range(2):
            relay(h, SIDE - ahead[h], 0, ((0, 1), (0, 3)))
        second_axis(0)
        if layer == 0:
            send_meta()
            load_w.wait()
        else:
            vv[layer - 1] = dot(w_ref[layer - 1], mm[layer - 1])
        for h in range(2):
            relay(h, 2, 0, ((0, 1), (0, 3)))
        second_axis(1)
        second_axis(3)

        for d in range(1, SIDE * SIDE):
            src = pw.at[layer, tpeer(SIDE * SIDE - d)]
            remote(
                src, src, pw_send.at[layer, d - 1], pw_recv.at[layer, d - 1], {"tp": tpeer(d)}
            ).wait_recv()
        power = jnp.sum(pw[layer], axis=0) / CHANNELS
        inverse = 1.0 / jnp.sqrt(power + EPSILON)
        inv[layer] = jnp.broadcast_to(inverse, (8, WIN))

        def hide(block, carry, layer=layer):
            scale = inv[layer, 0:1, :]
            for h in range(2):
                head = gst[0, block, h, :, 512:640].astype(F32)
                g = (
                    head[:, 56 + layer : 57 + layer]
                    + head[:, 59 + layer : 60 + layer]
                    + head[:, 62 + layer : 63 + layer]
                )
                rows = pl.ds(pl.multiple_of(block * LOCAL + HALF * h, 16), HALF)
                raw = gst[layer, block, h, :, 0:LENGTH].astype(F32) * g
                x = raw * scale[:, 0:LENGTH]
                xx = x * x
                t = jnp.tanh(GELU_C * (x + GELU_A * (xx * x)))
                upper = 0.5 * (1.0 + t)
                hid[layer, rows, 0:LENGTH] = (x * upper).astype(BF16)
                slope = upper + (0.5 * x) * (1.0 - t * t) * (GELU_C + (3.0 * GELU_A * GELU_C) * xx)
                mm[layer, rows, :] = (raw * slope).astype(BF16)
                x = gst[layer, block, h, :, LENGTH:WIN].astype(F32) * scale[:, LENGTH:WIN] * g
                t = jnp.tanh(GELU_C * (x + GELU_A * (x * x * x)))
                hid[layer, rows, LENGTH:WIN] = (0.5 * x * (1.0 + t)).astype(BF16)
            return carry

        for d in (0,) + NEAR:
            group = lax.rem(mx + d, SIDE)
            for e in (0,) + NEAR:
                if d + e > 0:
                    wait_block(0, d, e)
                    wait_block(1, e, d)
                if d == NEAR[-1]:
                    hide(group * SIDE + lax.rem(my + e, SIDE), 0)
            if d != NEAR[-1]:
                lax.fori_loop(group * SIDE, group * SIDE + SIDE, hide, 0)
            span = pl.ds(pl.multiple_of(group * 384, 128), 384)
            part = dot(w_ref[layer, :, span], hid[layer, span, :])
            if d == 0:
                ysum[...] = part
                second_axis(2)
                transpose_weights(layer)
                if layer == 0:
                    prepare_tissues()
                if layer == 1:
                    wait_meta()
                    prepare_picks(range(0, 4))
                if layer == 2:
                    prepare_picks(range(4, 8))
            elif d != NEAR[-1]:
                ysum[...] += part
            else:
                y = ysum[...] + part

        mixed = pltpu.roll(y[0:96], reach, 1) + y[96:192] + pltpu.roll(y[192:288], WIN - reach, 1)
        own = jnp.concatenate([gst[layer, me, 0], gst[layer, me, 1]], axis=0)
        state = own.astype(F32) + mixed
        if layer < LAYERS - 1:
            state = jnp.where(outside, 0.0, state).astype(BF16)
            for h in range(2):
                gst[layer + 1, me, h] = state[HALF * h : HALF * h + HALF, :]
        else:
            state3[...] = state[:, 0:LENGTH].astype(BF16)

    def acc_copy(d):
        return remote(
            acc_tx.at[:, CAP * d : CAP * d + CAP],
            acc_rx.at[:, CAP * (SEQ - d) : CAP * (SEQ - d) + CAP],
            acc_send.at[d - 1],
            acc_recv.at[d - 1],
            {"seq": speer(d)},
        )

    def ab_copy(d):
        return remote(
            ab_tx.at[:, CAP * d : CAP * d + CAP],
            ab_rx.at[:, CAP * (SEQ - d) : CAP * (SEQ - d) + CAP],
            ab_send.at[d - 1],
            ab_recv.at[d - 1],
            {"seq": speer(d)},
        )

    acc_tx[...] = dot(state3[...], pick[...]).astype(BF16)
    for d in range(1, SEQ):
        begin(acc_copy(d))
    acc_rx[:, 0:CAP] = acc_tx[:, 0:CAP]
    donor = dot(state3[...], donor_hot[...])
    load_tower.wait()
    weight_j = sgrad_ref[...] / ROOT
    rows_q = tissue_rows[...]
    accept_back = (weight_j * donor * rows_q).astype(BF16)
    ab_tx[...] = dot_rows(accept_back, slots[...]).astype(BF16)
    for d in range(1, SEQ):
        begin(ab_copy(d))
    ab_rx[:, 0:CAP] = ab_tx[:, 0:CAP]
    vv[LAYERS - 1] = dot(w_ref[LAYERS - 1], mm[LAYERS - 1])
    for d in range(1, SEQ):
        acc_copy(d).wait_recv()
    accept = dot(acc_rx[...], slots[...])
    donor_back = weight_j * accept * rows_q
    d_high = donor_back.astype(BF16)
    d_low = (donor_back - d_high.astype(F32)).astype(BF16)
    up[...] = tower_ref[...] + dot_rows(d_high, donor_hot[...]) + dot_rows(d_low, donor_hot[...])
    sc_all[me] = jnp.sum(donor * accept * rows_q, axis=0, keepdims=True) / ROOT
    for d in range(1, SEQ):
        ab_copy(d).wait_recv()
    up[...] += dot_rows(ab_rx[...], pick[...])
    for d in range(1, SIDE * SIDE):
        begin(
            remote(sc_all.at[me], sc_all.at[me], sc_send.at[d - 1], sc_recv.at[d - 1], {"tp": tpeer(d)})
        )

    def w_cores(layer):
        return remote(
            wg.at[layer, 1 - core], wrx.at[layer], w_send.at[layer, 0], w_recv.at[layer, 0], {"seq": partner}
        )

    def w_slices(layer, d):
        return remote(
            wz_tx.at[layer, lax.rem(mz + d, SIDE)],
            wz_rx.at[layer, d - 1],
            w_send.at[layer, d],
            w_recv.at[layer, d],
            {"seq": zpeer(d)},
        )

    def w_result(layer, d):
        return remote(
            wres.at[layer, core, mz],
            wres.at[layer, core, mz],
            w_send.at[layer, 3 + d],
            w_recv.at[layer, 3 + d],
            {"seq": zpeer(d)},
        )

    def w_share(layer, d):
        part = wres.at[layer, core, lax.rem(mz + SIDE - d, SIDE)]
        return remote(part, part, w_send.at[layer, 7 + d], w_recv.at[layer, 7 + d], {"seq": partner})

    def w_step2(layer):
        w_cores(layer).wait_recv()
        summed = wg[layer, core].astype(F32) + wrx[layer].astype(F32)
        for q in range(SIDE):
            wz_tx[layer, q] = summed[:, 384 * q : 384 * q + 384].astype(BF16)
        for d in NEAR:
            begin(w_slices(layer, d))

    def w_step3(layer):
        result = wz_tx[layer, mz].astype(F32)
        for d in NEAR:
            w_slices(layer, d).wait_recv()
            result = result + wz_rx[layer, d - 1].astype(F32)
        wres[layer, core, mz] = result.astype(BF16)
        for d in NEAR:
            begin(w_result(layer, d))
        begin(w_share(layer, 0))

    def w_step4(layer):
        for d in NEAR:
            src = wres.at[layer, core, lax.rem(mz + SIDE - d, SIDE)]
            remote(
                src, src, w_send.at[layer, 3 + d], w_recv.at[layer, 3 + d], {"seq": zpeer(d)}
            ).wait_recv()
            begin(w_share(layer, d))

    def store_w(layer):
        return pltpu.make_async_copy(wres.at[layer], wgrad_ref.at[layer], load_sem.at[3 + layer])

    def w_step5(layer):
        for d in range(SIDE):
            part = wres.at[layer, 1 - core, lax.rem(mz + SIDE - d, SIDE)]
            remote(
                part, part, w_send.at[layer, 7 + d], w_recv.at[layer, 7 + d], {"seq": partner}
            ).wait_recv()
        store_w(layer).start()

    gg[...] = jnp.zeros((128, 128), F32)
    for layer in reversed(range(LAYERS)):
        reach = 2 ** (layer + 3)
        shifts = (WIN - reach, 0, reach)
        gbuf[layer] = up[...].astype(BF16)
        halo_start(gbuf.at[layer], halo_b.at[layer], layer + 1)
        g = gbuf[layer].astype(F32)

        def shifted(window, shifts=shifts):
            rolled = [pltpu.roll(window, k, 1) if k else window for k in shifts]
            return jnp.concatenate(rolled, axis=0)

        inner_g = shifted(jnp.concatenate([g, jnp.zeros((LOCAL, 128), F32)], axis=1)).astype(BF16)

        def chunk(h, index, window, layer=layer):
            rows = pl.ds(pl.multiple_of(768 * h + 192 * index, 16), 192)
            return dot(wt[layer, rows, :], window)

        def rs_one(h, c, d, layer=layer):
            return remote(
                pab.at[layer, h, c, d - 1],
                rx.at[layer, h, c, d - 1],
                rs_send.at[layer, h, c, d - 1],
                rs_recv.at[layer, h, c, d - 1],
                {"tp": xpeer(d) if h == 0 else ypeer(d)},
            )

        def rs_two(h, c, d, layer=layer):
            index = lax.rem((my if h == 0 else mx) + d, SIDE)
            return remote(
                sab.at[layer, h, c, index],
                ry.at[layer, h, c, d - 1],
                rs_send.at[layer, h, c, 2 + d],
                rs_recv.at[layer, h, c, 2 + d],
                {"tp": ypeer(d) if h == 0 else xpeer(d)},
            )

        def partials(c, window, layer=layer, chunk=chunk, rs_one=rs_one):
            for d in NEAR:
                for h in range(2):
                    base = mx if h == 0 else my
                    pab[layer, h, c, d - 1] = chunk(h, lax.rem(base + d, SIDE), window).astype(BF16)
                    begin(rs_one(h, c, d))
            for h in range(2):
                own = chunk(h, mx if h == 0 else my, window)
                sf[h, c] = own.reshape(SIDE, HALF, 256)

        partials(0, inner_g[:, 128:384])
        for q in range(3):
            part = dot_rows(inner_g, hid[layer, 512 * q : 512 * q + 512, :]).astype(BF16)
            for h in range(2):
                wg[layer, h, :, 512 * q : 512 * q + 512] = part[144 * h : 144 * h + 144]
        begin(w_cores(layer))
        halo_wait(gbuf.at[layer], halo_b.at[layer], layer + 1)
        full_g = shifted(jnp.concatenate([g, halo_tile(halo_b.at[layer])], axis=1))
        full_g = full_g[:, 0:LENGTH]
        partials(1, jnp.concatenate([full_g[:, 0:128], full_g[:, 384:512]], axis=1).astype(BF16))
        inn[layer, me] = jnp.sum(full_g * vv[layer], axis=0, keepdims=True)
        for d in range(1, SIDE * SIDE):
            begin(
                remote(
                    inn.at[layer, me],
                    inn.at[layer, me],
                    inn_send.at[layer, d - 1],
                    inn_recv.at[layer, d - 1],
                    {"tp": tpeer(d)},
                )
            )
        if layer < LAYERS - 1:
            w_step4(layer + 1)
        w_step2(layer)
        for c in range(2):
            for h in range(2):
                for d in NEAR:
                    rs_one(h, c, d).wait_recv()
                    sf[h, c] += rx[layer, h, c, d - 1].astype(F32).reshape(SIDE, HALF, 256)
                sab[layer, h, c] = sf[h, c].astype(BF16)
                for d in NEAR:
                    begin(rs_two(h, c, d))
            if c == 0 and layer == 0:
                w_step3(layer)
        if layer > 0:
            w_step3(layer)
        if layer < LAYERS - 1:
            w_step5(layer + 1)

        x = (seq_ref[...] if layer == 0 else jnp.concatenate(
            [gst[layer, me, 0, :, 0:LENGTH], gst[layer, me, 1, :, 0:LENGTH]], axis=0
        )).astype(F32)
        scale = inv[layer, 0:1, 0:LENGTH]
        g_col = gain_ref[:, 56 + layer : 57 + layer]
        norm = x * scale
        pre = norm * g_col
        t = jnp.tanh(GELU_C * (pre + GELU_A * (pre * pre * pre)))
        slope = 0.5 * (1.0 + t) + 0.5 * pre * (1.0 - t * t) * (
            GELU_C * (1.0 + 3.0 * GELU_A * (pre * pre))
        )
        halves = []
        for h in range(2):
            sides = []
            for c in range(2):
                back = sf[h, c, my if h == 0 else mx]
                for d in NEAR:
                    rs_two(h, c, d).wait_recv()
                    back = back + ry[layer, h, c, d - 1].astype(F32)
                sides.append(back)
            middle, edges = sides
            halves.append(jnp.concatenate([edges[:, 0:128], middle, edges[:, 128:256]], axis=1))
        back_pre = jnp.concatenate(halves, axis=0) * slope
        back_norm = back_pre * g_col
        gain_col = jnp.sum(back_pre * norm, axis=1, keepdims=True)
        gg[0:LOCAL, :] = jnp.where(lane == layer, gain_col, gg[0:LOCAL, :])
        if layer == 0:
            gg_all[s] = gg[...].T[0:8]
            for d in range(1, SEQ):
                begin(
                    remote(
                        gg_all.at[s], gg_all.at[s], gg_send.at[d - 1], gg_recv.at[d - 1], {"seq": speer(d)}
                    )
                )
        for d in range(1, SIDE * SIDE):
            src = inn.at[layer, tpeer(SIDE * SIDE - d)]
            remote(
                src, src, inn_send.at[layer, d - 1], inn_recv.at[layer, d - 1], {"tp": tpeer(d)}
            ).wait_recv()
        inner = jnp.sum(inn[layer], axis=0)
        up[...] = up[...] + scale * back_norm - x * (scale * scale * scale) * (inner / CHANNELS)

    grad_ref[...] = up[...]
    w_step4(0)
    for d in range(1, SIDE * SIDE):
        src = sc_all.at[tpeer(SIDE * SIDE - d)]
        remote(src, src, sc_send.at[d - 1], sc_recv.at[d - 1], {"tp": tpeer(d)}).wait_recv()
    scores_ref[...] = jnp.sum(sc_all[...], axis=0)
    for d in range(1, SEQ):
        src = gg_all.at[speer(SEQ - d)]
        remote(src, src, gg_send.at[d - 1], gg_recv.at[d - 1], {"seq": speer(d)}).wait_recv()
    gains_ref[...] = jnp.sum(gg_all[...], axis=0)[0:LAYERS, 0:LOCAL]
    w_step5(0)
    for layer in range(LAYERS):
        store_w(layer).wait()
    for copy in pending:
        copy.wait_send()


def dma(*shape):
    return pltpu.SemaphoreType.DMA(shape)


def section(*operands):
    vmem = pl.BlockSpec(memory_space=pltpu.VMEM)
    hbm = pl.BlockSpec(memory_space=pl.ANY)
    return pl.pallas_call(
        section_kernel,
        out_shape=(
            jax.ShapeDtypeStruct((1, JUNC), F32),
            jax.ShapeDtypeStruct((LOCAL, LENGTH), F32),
            jax.ShapeDtypeStruct((LAYERS, 2, SIDE, 144, 384), BF16),
            jax.ShapeDtypeStruct((LAYERS, LOCAL), F32),
        ),
        in_specs=[vmem, hbm, vmem, hbm, hbm] + [vmem] * 5,
        out_specs=(vmem, vmem, hbm, vmem),
        scratch_shapes=[
            pltpu.VMEM((LAYERS, 3 * LOCAL, CHANNELS), BF16),
            pltpu.VMEM((LOCAL, LENGTH), F32),
            pltpu.VMEM((LOCAL, 128), F32),
            pltpu.VMEM((367, 256), F32),
            pltpu.VMEM((128, 128), F32),
            pltpu.VMEM((384, 128), F32),
            pltpu.VMEM((LAYERS, 16, 2, HALF, WIN), BF16),
            pltpu.VMEM((LAYERS, CHANNELS, WIN), BF16),
            pltpu.VMEM((LAYERS, CHANNELS, LENGTH), BF16),
            pltpu.VMEM((LAYERS, 3 * LOCAL, LENGTH), F32),
            pltpu.VMEM((3 * LOCAL, WIN), F32),
            pltpu.VMEM((LAYERS, 16, 1, WIN), F32),
            pltpu.VMEM((LAYERS, 8, WIN), F32),
            pltpu.VMEM((LAYERS, CHANNELS, 3 * LOCAL), BF16),
            pltpu.VMEM((SEQ, 1, JUNC), jnp.int32),
            pltpu.VMEM((LENGTH, SEQ * CAP), BF16),
            pltpu.VMEM((SEQ * CAP, JUNC), BF16),
            pltpu.VMEM((LENGTH, JUNC), BF16),
            pltpu.VMEM((LOCAL, JUNC), F32),
            pltpu.VMEM((LOCAL, LENGTH), BF16),
            pltpu.VMEM((LOCAL, SEQ * CAP), BF16),
            pltpu.VMEM((LOCAL, SEQ * CAP), BF16),
            pltpu.VMEM((LOCAL, SEQ * CAP), BF16),
            pltpu.VMEM((LOCAL, SEQ * CAP), BF16),
            pltpu.VMEM((16, 1, JUNC), F32),
            pltpu.VMEM((LOCAL, LENGTH), F32),
            pltpu.VMEM((LAYERS, LOCAL, LENGTH), BF16),
            pltpu.VMEM((2, LOCAL, 128), BF16),
            pltpu.VMEM((LAYERS, 2, LOCAL, 128), BF16),
            pltpu.VMEM((LAYERS, 2, 2, 3, 192, 256), BF16),
            pltpu.VMEM((LAYERS, 2, 2, 3, 192, 256), BF16),
            pltpu.VMEM((2, 2, SIDE, HALF, 256), F32),
            pltpu.VMEM((LAYERS, 2, 2, SIDE, HALF, 256), BF16),
            pltpu.VMEM((LAYERS, 2, 2, 3, HALF, 256), BF16),
            pltpu.VMEM((LAYERS, 16, 1, LENGTH), F32),
            pltpu.VMEM((LAYERS, 2, 144, CHANNELS), BF16),
            pltpu.VMEM((LAYERS, 144, CHANNELS), BF16),
            pltpu.VMEM((LAYERS, SIDE, 144, 384), BF16),
            pltpu.VMEM((LAYERS, 3, 144, 384), BF16),
            pltpu.VMEM((LAYERS, 2, SIDE, 144, 384), BF16),
            pltpu.VMEM((128, 128), F32),
            pltpu.VMEM((SEQ, 8, 128), F32),
            dma(4, 2),
            dma(4, 2),
            dma(LAYERS, 30),
            dma(LAYERS, 16, 2),
            dma(7),
            dma(7),
            dma(7),
            dma(7),
            dma(7),
            dma(7),
            dma(15),
            dma(15),
            dma(LAYERS, 2, 2, 6),
            dma(LAYERS, 2, 2, 6),
            dma(LAYERS, 15),
            dma(LAYERS, 15),
            dma(LAYERS, 11),
            dma(LAYERS, 11),
            dma(7),
            dma(7),
            dma(LAYERS, 15),
            dma(LAYERS, 15),
            dma(6),
        ],
        compiler_params=pltpu.CompilerParams(
            collective_id=0, has_side_effects=True, vmem_limit_bytes=62 * 1024 * 1024
        ),
        name="conv_section",
    )(*operands)


def finish_kernel(w_ref, scores_ref, grad_ref, gains_ref, w_out, scores_out, grad_out, gains_out):
    for q in range(SIDE):
        w_out[0, :, 384 * q : 384 * q + 384] = w_ref[0, 0, q].astype(F32)
    scores_out[...] = scores_ref[...]
    grad_out[...] = grad_ref[...]
    gains_out[...] = gains_ref[...]


def finish(weights, scores, grad, gains):
    def whole(x):
        return pl.BlockSpec(x.shape, lambda i, j: (0, 0))

    return pl.pallas_call(
        finish_kernel,
        grid=(LAYERS, 2),
        out_shape=(
            jax.ShapeDtypeStruct((LAYERS, 3 * LOCAL, CHANNELS), F32),
            jax.ShapeDtypeStruct(scores.shape, F32),
            jax.ShapeDtypeStruct(grad.shape, F32),
            jax.ShapeDtypeStruct(gains.shape, F32),
        ),
        in_specs=[
            pl.BlockSpec((1, 1, SIDE, 144, 384), lambda i, j: (i, j, 0, 0, 0)),
            whole(scores),
            whole(grad),
            whole(gains),
        ],
        out_specs=(
            pl.BlockSpec((1, 144, CHANNELS), lambda i, j: (i, j, 0)),
            whole(scores),
            whole(grad),
            whole(gains),
        ),
        name="finish",
    )(weights, scores, grad, gains)


def local(
    sequence_in,
    conv_weight,
    norm_gain,
    tissue_scale,
    donor_offset,
    acceptor_owner,
    acceptor_offset,
    tissue,
    tower_grad,
    score_grad,
):
    stacked = conv_weight.transpose(0, 2, 1, 3).reshape(LAYERS, 3 * LOCAL, CHANNELS)
    scores, grad, weights, gains = section(
        sequence_in,
        stacked,
        norm_gain,
        tower_grad,
        tissue_scale,
        acceptor_owner.T,
        acceptor_offset[None, :],
        donor_offset[None, :],
        tissue[None, :],
        score_grad[None, :],
    )
    weights, scores, grad, gains = finish(weights, scores, grad, gains)
    weights = weights.reshape(LAYERS, 3, LOCAL, CHANNELS).transpose(0, 2, 1, 3)
    return (scores[0], grad, weights, gains)


def solution(mesh):
    return jax.shard_map(
        local,
        mesh=mesh,
        in_specs=(
            P("tp", "seq"),
            P(None, "tp", None, None),
            P(None, "tp"),
            P(),
            P("seq"),
            P("seq", None),
            P("seq"),
            P("seq"),
            P("tp", "seq"),
            P("seq"),
        ),
        out_specs=(P("seq"), P("tp", "seq"), P(None, "tp", None, None), P(None, "tp")),
        check_vma=False,
    )
```

```python
import math

import jax
import jax.numpy as jnp
from jax import lax
from jax.experimental import pallas as pl
from jax.experimental.pallas import tpu as pltpu
from jax.sharding import PartitionSpec as P

CHANNELS = 1536
LAYERS = 3
LOCAL = 96
HALF = 48
LENGTH = 512
WIN = 640
SIDE = 4
SEQ = 8
JUNC = 256
CAP = 128
MESH = pl.DeviceIdType.MESH
EPSILON = 1e-06
ROOT = math.sqrt(CHANNELS)
GELU_C = math.sqrt(2.0 / math.pi)
GELU_A = 0.044715
F32 = jnp.float32
BF16 = jnp.bfloat16
NEAR = (1, 3, 2)


def remote(src, dst, send_sem, recv_sem, device):
    return pltpu.make_async_remote_copy(
        src_ref=src,
        dst_ref=dst,
        send_sem=send_sem,
        recv_sem=recv_sem,
        device_id=device,
        device_id_type=MESH,
    )


def dot(a, b):
    return jnp.dot(a, b, preferred_element_type=F32)


def dot_rows(a, b):
    return lax.dot_general(a, b, (((1,), (1,)), ((), ())), preferred_element_type=F32)


def section_kernel(
    seq_ref,
    w_hbm,
    gain_in,
    tower_hbm,
    table_hbm,
    owner_ref,
    offset_ref,
    donor_ref,
    tissue_ref,
    sgrad_ref,
    scores_ref,
    grad_ref,
    wgrad_ref,
    gains_ref,
    w_ref,
    tower_ref,
    gain_ref,
    window,
    turn,
    tab,
    gst,
    hid,
    mm,
    vv,
    ysum,
    pw,
    inv,
    wt,
    meta_all,
    pick,
    slots,
    donor_hot,
    tissue_rows,
    state3,
    acc_tx,
    acc_rx,
    ab_tx,
    ab_rx,
    sc_all,
    up,
    gbuf,
    halo_rx,
    halo_b,
    pab,
    rx,
    sf,
    sab,
    ry,
    inn,
    wg,
    wrx,
    wz_tx,
    wz_rx,
    wres,
    gg,
    gg_all,
    halo_send,
    halo_recv,
    gather_send,
    gather_recv,
    meta_send,
    meta_recv,
    acc_send,
    acc_recv,
    ab_send,
    ab_recv,
    sc_send,
    sc_recv,
    rs_send,
    rs_recv,
    inn_send,
    inn_recv,
    w_send,
    w_recv,
    gg_send,
    gg_recv,
    pw_send,
    pw_recv,
    tile_send,
    tile_recv,
    load_sem,
):
    s = lax.axis_index("seq")
    me = lax.axis_index("tp")
    mx = me // SIDE
    my = lax.rem(me, SIDE)
    mz = s // 2
    core = lax.rem(s, 2)

    def xpeer(d):
        return lax.rem(mx + d, SIDE) * SIDE + my

    def ypeer(d):
        return mx * SIDE + lax.rem(my + d, SIDE)

    def tpeer(d):
        return lax.rem(me + d, SIDE * SIDE)

    def speer(d):
        return lax.rem(s + d, SEQ)

    def zpeer(d):
        return lax.rem(mz + d, SIDE) * 2 + core

    partner = mz * 2 + 1 - core

    load_w = pltpu.make_async_copy(w_hbm, w_ref, load_sem.at[0])
    load_tower = pltpu.make_async_copy(tower_hbm, tower_ref, load_sem.at[1])
    start = jnp.minimum(me * LOCAL // 128, CHANNELS // 128 - 2) * 128
    skip = me * LOCAL - start
    load_table = pltpu.make_async_copy(
        table_hbm.at[:, pl.ds(pl.multiple_of(start, 128), 256)], window, load_sem.at[2]
    )
    load_w.start()
    load_table.start()
    load_tower.start()

    barrier = pltpu.get_barrier_semaphore()
    for d in range(1, SIDE * SIDE):
        pl.semaphore_signal(barrier, inc=1, device_id={"tp": tpeer(d)}, device_id_type=MESH)
    for d in range(1, SEQ):
        pl.semaphore_signal(barrier, inc=1, device_id={"seq": speer(d)}, device_id_type=MESH)
    turn[...] = jnp.zeros((128, 128), F32)
    for k in range(3):
        turn[56 + 3 * k : 59 + 3 * k, 0:LOCAL] = gain_in[...]
    gain_ref[...] = turn[...].T[0:LOCAL]
    pl.semaphore_wait(barrier, SIDE * SIDE - 1 + SEQ - 1)

    pending = []

    def begin(copy):
        copy.start()
        pending.append(copy)

    def halo_left(src, dst, k):
        return remote(src.at[:, 0:128], dst.at[0], halo_send.at[k, 0], halo_recv.at[k, 0], {"seq": s - 1})

    def halo_right(src, dst, k):
        return remote(src.at[:, 384:512], dst.at[1], halo_send.at[k, 1], halo_recv.at[k, 1], {"seq": s + 1})

    def halo_start(src, dst, k):
        @pl.when(s > 0)
        def _():
            halo_left(src, dst, k).start()

        @pl.when(s < SEQ - 1)
        def _():
            halo_right(src, dst, k).start()

        @pl.when(s == 0)
        def _():
            dst[1] = jnp.zeros((LOCAL, 128), BF16)

        @pl.when(s == SEQ - 1)
        def _():
            dst[0] = jnp.zeros((LOCAL, 128), BF16)

    def halo_wait(src, dst, k):
        @pl.when(s > 0)
        def _():
            halo_left(src, dst, k).wait_send()
            remote(
                src.at[:, 384:512], dst.at[1], halo_send.at[k, 1], halo_recv.at[k, 1], {"seq": s - 1}
            ).wait_recv()

        @pl.when(s < SEQ - 1)
        def _():
            halo_right(src, dst, k).wait_send()
            remote(
                src.at[:, 0:128], dst.at[0], halo_send.at[k, 0], halo_recv.at[k, 0], {"seq": s + 1}
            ).wait_recv()

    lane = lax.broadcasted_iota(jnp.int32, (LOCAL, 128), 1)

    def halo_tile(dst):
        return jnp.where(lane < 64, dst[0].astype(F32), dst[1].astype(F32))

    halo_start(seq_ref, halo_rx, 0)

    gain = gain_ref[...]
    high = gain.astype(BF16).astype(F32)
    rest = gain - high
    mid = rest.astype(BF16).astype(F32)
    low = rest - mid
    packed = jnp.where(lane < 59, high, jnp.where(lane < 62, mid, low))
    in_gain = (lane >= 56) & (lane < 65)

    for h in range(2):
        gst[0, me, h, :, 0:512] = seq_ref[HALF * h : HALF * h + HALF, :]

    def finish_tile():
        halo_wait(seq_ref, halo_rx, 0)
        tile = jnp.where(in_gain, packed, halo_tile(halo_rx)).astype(BF16)
        for h in range(2):
            gst[0, me, h, :, 512:640] = tile[HALF * h : HALF * h + HALF, :]
        for d in range(1, SIDE * SIDE):
            own = gst.at[0, me, :, :, 512:640]
            begin(remote(own, own, tile_send.at[d - 1], tile_recv.at[d - 1], {"tp": tpeer(d)}))

    col = lax.broadcasted_iota(jnp.int32, (LOCAL, WIN), 1)
    outside = ((s == SEQ - 1) & (col >= 512) & (col < 576)) | ((s == 0) & (col >= 576))

    def transpose_weights(layer):
        for x in range(SIDE):
            block = w_ref[layer, :, 384 * x : 384 * x + 384].astype(F32).T.astype(BF16)
            for y in range(SIDE):
                a = 192 * x + HALF * y
                b = 768 + 192 * y + HALF * x
                wt[layer, a : a + HALF, :] = block[96 * y : 96 * y + HALF]
                wt[layer, b : b + HALF, :] = block[96 * y + HALF : 96 * y + 96]

    def one_hot(rows, row_ids, base):
        ids = lax.broadcasted_iota(jnp.int32, (rows, JUNC), 0) + base
        return jnp.where(ids == row_ids, 1.0, 0.0).astype(BF16)

    def prepare_tissues():
        load_table.wait()
        tab[...] = jnp.zeros((384, 128), F32)
        tab[0 : window.shape[0], :] = pltpu.roll(window[...], lax.rem(256 - skip, 256), 1)[:, 0:128]
        table = tab[...].T[0:LOCAL]
        t_high = table.astype(BF16)
        t_rest = table - t_high.astype(F32)
        t_mid = t_rest.astype(BF16)
        t_low = (t_rest - t_mid.astype(F32)).astype(BF16)
        hot = one_hot(384, tissue_ref[...], 0)
        tissue_rows[...] = dot(t_high, hot) + dot(t_mid, hot) + dot(t_low, hot)
        donor_hot[...] = one_hot(LENGTH, donor_ref[...], 0)

    def send_meta():
        owner = owner_ref[...]
        member = one_hot(16, owner, 0)
        first = lax.broadcasted_iota(jnp.int32, (JUNC, JUNC), 0)
        second = lax.broadcasted_iota(jnp.int32, (JUNC, JUNC), 1)
        rank = dot(member, jnp.where(first <= second, 1.0, 0.0).astype(BF16))
        slot = jnp.sum(member.astype(F32) * rank, axis=0, keepdims=True) - 1.0
        slot = slot.astype(jnp.int32)
        meta_all[s] = (slot * SEQ + owner) * LENGTH + offset_ref[...]
        for d in range(1, SEQ):
            begin(
                remote(
                    meta_all.at[s], meta_all.at[s], meta_send.at[d - 1], meta_recv.at[d - 1], {"seq": speer(d)}
                )
            )
        ids = lax.broadcasted_iota(jnp.int32, (CAP, JUNC), 0)
        for d in range(SEQ):
            mine = (ids == slot) & (owner == speer(d))
            slots[CAP * d : CAP * d + CAP, :] = jnp.where(mine, 1.0, 0.0).astype(BF16)

    def wait_meta():
        for d in range(1, SEQ):
            src = speer(SEQ - d)
            remote(
                meta_all.at[src], meta_all.at[src], meta_send.at[d - 1], meta_recv.at[d - 1], {"seq": src}
            ).wait_recv()

    def prepare_picks(which):
        for d in which:
            row = meta_all[speer(d)]
            place = one_hot(LENGTH, row & (SEQ * LENGTH - 1), s * LENGTH)
            slot = one_hot(CAP, lax.shift_right_logical(row, 12), 0)
            pick[:, CAP * d : CAP * d + CAP] = dot_rows(place, slot).astype(BF16)

    for layer in range(LAYERS):
        reach = 2 ** (layer + 3)
        count = [0]

        def piece(block, h, layer=layer):
            if layer == 0:
                return gst.at[layer, block, h, :, 0:LENGTH]
            return gst.at[layer, block, h]

        def go(block, h, peer, layer=layer, count=count, piece=piece):
            begin(
                remote(
                    piece(block, h),
                    piece(block, h),
                    gather_send.at[layer, count[0]],
                    gather_recv.at[layer, block, h],
                    {"tp": peer},
                )
            )
            count[0] += 1

        def arrived(block, h, layer=layer, piece=piece):
            remote(
                piece(block, h),
                piece(block, h),
                gather_send.at[layer, 0],
                gather_recv.at[layer, block, h],
                {"tp": xpeer(1)},
            ).wait_recv()

        def send_powers(layer=layer):
            squares = jnp.concatenate([gst[layer, me, 0], gst[layer, me, 1]], axis=0).astype(F32)
            pw[layer, me] = jnp.sum(squares * squares, axis=0, keepdims=True)
            for d in range(1, SIDE * SIDE):
                begin(
                    remote(
                        pw.at[layer, me],
                        pw.at[layer, me],
                        pw_send.at[layer, d - 1],
                        pw_recv.at[layer, d - 1],
                        {"tp": tpeer(d)},
                    )
                )

        if layer > 0:
            send_powers()

        def at(h, p, q):
            dx, dy = (p, q) if h == 0 else (q, p)
            return lax.rem(mx + dx, SIDE) * SIDE + lax.rem(my + dy, SIDE)

        waited = set()

        def wait_block(h, p, q, at=at, waited=waited, arrived=arrived):
            if (h, p, q) not in waited:
                waited.add((h, p, q))
                arrived(at(h, p, q), h)

        def relay(h, p, q, targets, at=at, go=go, wait_block=wait_block):
            if (p, q) != (0, 0):
                wait_block(h, p, q)
            for target in targets:
                go(at(h, p, q), h, at(h, *target))

        def second_axis(p, relay=relay):
            for h in range(2):
                if p % 2 == 0:
                    relay(h, p, 3, ((0, 1),))
                else:
                    relay(h, p, 1, ((0, 3),))

        for h in range(2):
            relay(h, 0, 0, ((1, 0), (3, 0), (2, 0)))
        for h in range(2):
            relay(h, 0, 0, ((0, 1), (0, 3)))
        for p in (3, 1):
            for h in range(2):
                relay(h, p, 0, ((0, 1), (0, 3)))
        for h in range(2):
            relay(h, 2, 0, ((0, 1), (0, 3), (0, 2)))
        if layer == 0:
            finish_tile()
            send_powers()
        second_axis(0)
        if layer == 0:
            send_meta()
            load_w.wait()
            prepare_tissues()
        else:
            vv[layer - 1] = dot(w_ref[layer - 1], mm[layer - 1])
        second_axis(1)
        second_axis(3)
        if layer == 0:
            transpose_weights(0)
            for d in range(1, SIDE * SIDE):
                src = gst.at[0, tpeer(SIDE * SIDE - d), :, :, 512:640]
                remote(src, src, tile_send.at[d - 1], tile_recv.at[d - 1], {"tp": tpeer(d)}).wait_recv()

        for d in range(1, SIDE * SIDE):
            src = pw.at[layer, tpeer(SIDE * SIDE - d)]
            remote(
                src, src, pw_send.at[layer, d - 1], pw_recv.at[layer, d - 1], {"tp": tpeer(d)}
            ).wait_recv()
        power = jnp.sum(pw[layer], axis=0) / CHANNELS
        inverse = 1.0 / jnp.sqrt(power + EPSILON)
        inv[layer] = jnp.broadcast_to(inverse, (8, WIN))

        def hide(block, carry, layer=layer):
            scale = inv[layer, 0:1, :]
            for h in range(2):
                head = gst[0, block, h, :, 512:640].astype(F32)
                g = (
                    head[:, 56 + layer : 57 + layer]
                    + head[:, 59 + layer : 60 + layer]
                    + head[:, 62 + layer : 63 + layer]
                )
                rows = pl.ds(pl.multiple_of(block * LOCAL + HALF * h, 16), HALF)
                raw = gst[layer, block, h, :, 0:LENGTH].astype(F32) * g
                x = raw * scale[:, 0:LENGTH]
                xx = x * x
                t = jnp.tanh(GELU_C * (x + GELU_A * (xx * x)))
                upper = 0.5 * (1.0 + t)
                hid[layer, rows, 0:LENGTH] = (x * upper).astype(BF16)
                slope = upper + (0.5 * x) * (1.0 - t * t) * (GELU_C + (3.0 * GELU_A * GELU_C) * xx)
                mm[layer, rows, :] = (raw * slope).astype(BF16)
                x = gst[layer, block, h, :, LENGTH:WIN].astype(F32) * scale[:, LENGTH:WIN] * g
                t = jnp.tanh(GELU_C * (x + GELU_A * (x * x * x)))
                hid[layer, rows, LENGTH:WIN] = (0.5 * x * (1.0 + t)).astype(BF16)
            return carry

        for d in (0,) + NEAR:
            group = lax.rem(mx + d, SIDE)
            for e in (0,) + NEAR:
                if d + e > 0:
                    wait_block(0, d, e)
                    wait_block(1, e, d)
                if d == NEAR[-1]:
                    hide(group * SIDE + lax.rem(my + e, SIDE), 0)
            if d != NEAR[-1]:
                lax.fori_loop(group * SIDE, group * SIDE + SIDE, hide, 0)
            span = pl.ds(pl.multiple_of(group * 384, 128), 384)
            part = dot(w_ref[layer, :, span], hid[layer, span, :])
            if d == 0:
                ysum[...] = part
                if layer > 0:
                    transpose_weights(layer)
                if layer == 1:
                    wait_meta()
                    prepare_picks(range(0, 4))
                if layer == 2:
                    prepare_picks(range(4, 8))
            elif d != NEAR[-1]:
                ysum[...] += part
            else:
                y = ysum[...] + part

        mixed = pltpu.roll(y[0:96], reach, 1) + y[96:192] + pltpu.roll(y[192:288], WIN - reach, 1)
        own = jnp.concatenate([gst[layer, me, 0], gst[layer, me, 1]], axis=0)
        state = own.astype(F32) + mixed
        if layer < LAYERS - 1:
            state = jnp.where(outside, 0.0, state).astype(BF16)
            for h in range(2):
                gst[layer + 1, me, h] = state[HALF * h : HALF * h + HALF, :]
        else:
            state3[...] = state[:, 0:LENGTH].astype(BF16)

    def acc_copy(d):
        return remote(
            acc_tx.at[:, CAP * d : CAP * d + CAP],
            acc_rx.at[:, CAP * (SEQ - d) : CAP * (SEQ - d) + CAP],
            acc_send.at[d - 1],
            acc_recv.at[d - 1],
            {"seq": speer(d)},
        )

    def ab_copy(d):
        return remote(
            ab_tx.at[:, CAP * d : CAP * d + CAP],
            ab_rx.at[:, CAP * (SEQ - d) : CAP * (SEQ - d) + CAP],
            ab_send.at[d - 1],
            ab_recv.at[d - 1],
            {"seq": speer(d)},
        )

    acc_tx[...] = dot(state3[...], pick[...]).astype(BF16)
    for d in range(1, SEQ):
        begin(acc_copy(d))
    acc_rx[:, 0:CAP] = acc_tx[:, 0:CAP]
    donor = dot(state3[...], donor_hot[...])
    load_tower.wait()
    weight_j = sgrad_ref[...] / ROOT
    rows_q = tissue_rows[...]
    accept_back = (weight_j * donor * rows_q).astype(BF16)
    ab_tx[...] = dot_rows(accept_back, slots[...]).astype(BF16)
    for d in range(1, SEQ):
        begin(ab_copy(d))
    ab_rx[:, 0:CAP] = ab_tx[:, 0:CAP]
    vv[LAYERS - 1] = dot(w_ref[LAYERS - 1], mm[LAYERS - 1])
    for d in range(1, SEQ):
        acc_copy(d).wait_recv()
    accept = dot(acc_rx[...], slots[...])
    donor_back = weight_j * accept * rows_q
    d_high = donor_back.astype(BF16)
    d_low = (donor_back - d_high.astype(F32)).astype(BF16)
    up[...] = tower_ref[...] + dot_rows(d_high, donor_hot[...]) + dot_rows(d_low, donor_hot[...])
    sc_all[me] = jnp.sum(donor * accept * rows_q, axis=0, keepdims=True) / ROOT
    for d in range(1, SEQ):
        ab_copy(d).wait_recv()
    up[...] += dot_rows(ab_rx[...], pick[...])
    for d in range(1, SIDE * SIDE):
        begin(
            remote(sc_all.at[me], sc_all.at[me], sc_send.at[d - 1], sc_recv.at[d - 1], {"tp": tpeer(d)})
        )

    def w_cores(layer):
        return remote(
            wg.at[layer, 1 - core], wrx.at[layer], w_send.at[layer, 0], w_recv.at[layer, 0], {"seq": partner}
        )

    def w_slices(layer, d):
        return remote(
            wz_tx.at[layer, lax.rem(mz + d, SIDE)],
            wz_rx.at[layer, d - 1],
            w_send.at[layer, d],
            w_recv.at[layer, d],
            {"seq": zpeer(d)},
        )

    def w_result(layer, d):
        return remote(
            wres.at[layer, core, mz],
            wres.at[layer, core, mz],
            w_send.at[layer, 3 + d],
            w_recv.at[layer, 3 + d],
            {"seq": zpeer(d)},
        )

    def w_share(layer, d):
        part = wres.at[layer, core, lax.rem(mz + SIDE - d, SIDE)]
        return remote(part, part, w_send.at[layer, 7 + d], w_recv.at[layer, 7 + d], {"seq": partner})

    def w_step2(layer):
        w_cores(layer).wait_recv()
        summed = wg[layer, core].astype(F32) + wrx[layer].astype(F32)
        for q in range(SIDE):
            wz_tx[layer, q] = summed[:, 384 * q : 384 * q + 384].astype(BF16)
        for d in NEAR:
            begin(w_slices(layer, d))

    def w_step3(layer):
        result = wz_tx[layer, mz].astype(F32)
        for d in NEAR:
            w_slices(layer, d).wait_recv()
            result = result + wz_rx[layer, d - 1].astype(F32)
        wres[layer, core, mz] = result.astype(BF16)
        for d in NEAR:
            begin(w_result(layer, d))
        begin(w_share(layer, 0))

    def w_step4(layer):
        for d in NEAR:
            src = wres.at[layer, core, lax.rem(mz + SIDE - d, SIDE)]
            remote(
                src, src, w_send.at[layer, 3 + d], w_recv.at[layer, 3 + d], {"seq": zpeer(d)}
            ).wait_recv()
            begin(w_share(layer, d))

    def store_w(layer):
        return pltpu.make_async_copy(wres.at[layer], wgrad_ref.at[layer], load_sem.at[3 + layer])

    def w_step5(layer):
        for d in range(SIDE):
            part = wres.at[layer, 1 - core, lax.rem(mz + SIDE - d, SIDE)]
            remote(
                part, part, w_send.at[layer, 7 + d], w_recv.at[layer, 7 + d], {"seq": partner}
            ).wait_recv()
        store_w(layer).start()

    gg[...] = jnp.zeros((128, 128), F32)
    for layer in reversed(range(LAYERS)):
        reach = 2 ** (layer + 3)
        shifts = (WIN - reach, 0, reach)
        gbuf[layer] = up[...].astype(BF16)
        halo_start(gbuf.at[layer], halo_b.at[layer], layer + 1)
        g = gbuf[layer].astype(F32)

        def shifted(window, shifts=shifts):
            rolled = [pltpu.roll(window, k, 1) if k else window for k in shifts]
            return jnp.concatenate(rolled, axis=0)

        inner_g = shifted(jnp.concatenate([g, jnp.zeros((LOCAL, 128), F32)], axis=1)).astype(BF16)

        def chunk(h, index, window, layer=layer):
            rows = pl.ds(pl.multiple_of(768 * h + 192 * index, 16), 192)
            return dot(wt[layer, rows, :], window)

        def rs_one(h, c, d, layer=layer):
            return remote(
                pab.at[layer, h, c, d - 1],
                rx.at[layer, h, c, d - 1],
                rs_send.at[layer, h, c, d - 1],
                rs_recv.at[layer, h, c, d - 1],
                {"tp": xpeer(d) if h == 0 else ypeer(d)},
            )

        def rs_two(h, c, d, layer=layer):
            index = lax.rem((my if h == 0 else mx) + d, SIDE)
            return remote(
                sab.at[layer, h, c, index],
                ry.at[layer, h, c, d - 1],
                rs_send.at[layer, h, c, 2 + d],
                rs_recv.at[layer, h, c, 2 + d],
                {"tp": ypeer(d) if h == 0 else xpeer(d)},
            )

        def partials(c, window, layer=layer, chunk=chunk, rs_one=rs_one):
            for d in NEAR:
                for h in range(2):
                    base = mx if h == 0 else my
                    pab[layer, h, c, d - 1] = chunk(h, lax.rem(base + d, SIDE), window).astype(BF16)
                    begin(rs_one(h, c, d))
            for h in range(2):
                own = chunk(h, mx if h == 0 else my, window)
                sf[h, c] = own.reshape(SIDE, HALF, 256)

        partials(0, inner_g[:, 128:384])
        for q in range(3):
            part = dot_rows(inner_g, hid[layer, 512 * q : 512 * q + 512, :]).astype(BF16)
            for h in range(2):
                wg[layer, h, :, 512 * q : 512 * q + 512] = part[144 * h : 144 * h + 144]
        begin(w_cores(layer))
        halo_wait(gbuf.at[layer], halo_b.at[layer], layer + 1)
        full_g = shifted(jnp.concatenate([g, halo_tile(halo_b.at[layer])], axis=1))
        full_g = full_g[:, 0:LENGTH]
        partials(1, jnp.concatenate([full_g[:, 0:128], full_g[:, 384:512]], axis=1).astype(BF16))
        inn[layer, me] = jnp.sum(full_g * vv[layer], axis=0, keepdims=True)
        for d in range(1, SIDE * SIDE):
            begin(
                remote(
                    inn.at[layer, me],
                    inn.at[layer, me],
                    inn_send.at[layer, d - 1],
                    inn_recv.at[layer, d - 1],
                    {"tp": tpeer(d)},
                )
            )
        if layer < LAYERS - 1:
            w_step4(layer + 1)
        w_step2(layer)
        for c in range(2):
            for h in range(2):
                for d in NEAR:
                    rs_one(h, c, d).wait_recv()
                    sf[h, c] += rx[layer, h, c, d - 1].astype(F32).reshape(SIDE, HALF, 256)
                sab[layer, h, c] = sf[h, c].astype(BF16)
                for d in NEAR:
                    begin(rs_two(h, c, d))
            if c == 0 and layer == 0:
                w_step3(layer)
        if layer > 0:
            w_step3(layer)
        if layer < LAYERS - 1:
            w_step5(layer + 1)

        x = (seq_ref[...] if layer == 0 else jnp.concatenate(
            [gst[layer, me, 0, :, 0:LENGTH], gst[layer, me, 1, :, 0:LENGTH]], axis=0
        )).astype(F32)
        scale = inv[layer, 0:1, 0:LENGTH]
        g_col = gain_ref[:, 56 + layer : 57 + layer]
        norm = x * scale
        pre = norm * g_col
        t = jnp.tanh(GELU_C * (pre + GELU_A * (pre * pre * pre)))
        slope = 0.5 * (1.0 + t) + 0.5 * pre * (1.0 - t * t) * (
            GELU_C * (1.0 + 3.0 * GELU_A * (pre * pre))
        )
        halves = []
        for h in range(2):
            sides = []
            for c in range(2):
                back = sf[h, c, my if h == 0 else mx]
                for d in NEAR:
                    rs_two(h, c, d).wait_recv()
                    back = back + ry[layer, h, c, d - 1].astype(F32)
                sides.append(back)
            middle, edges = sides
            halves.append(jnp.concatenate([edges[:, 0:128], middle, edges[:, 128:256]], axis=1))
        back_pre = jnp.concatenate(halves, axis=0) * slope
        back_norm = back_pre * g_col
        gain_col = jnp.sum(back_pre * norm, axis=1, keepdims=True)
        gg[0:LOCAL, :] = jnp.where(lane == layer, gain_col, gg[0:LOCAL, :])
        if layer == 0:
            gg_all[s] = gg[...].T[0:8]
            for d in range(1, SEQ):
                begin(
                    remote(
                        gg_all.at[s], gg_all.at[s], gg_send.at[d - 1], gg_recv.at[d - 1], {"seq": speer(d)}
                    )
                )
        for d in range(1, SIDE * SIDE):
            src = inn.at[layer, tpeer(SIDE * SIDE - d)]
            remote(
                src, src, inn_send.at[layer, d - 1], inn_recv.at[layer, d - 1], {"tp": tpeer(d)}
            ).wait_recv()
        inner = jnp.sum(inn[layer], axis=0)
        up[...] = up[...] + scale * back_norm - x * (scale * scale * scale) * (inner / CHANNELS)

    grad_ref[...] = up[...]
    w_step4(0)
    for d in range(1, SIDE * SIDE):
        src = sc_all.at[tpeer(SIDE * SIDE - d)]
        remote(src, src, sc_send.at[d - 1], sc_recv.at[d - 1], {"tp": tpeer(d)}).wait_recv()
    scores_ref[...] = jnp.sum(sc_all[...], axis=0)
    for d in range(1, SEQ):
        src = gg_all.at[speer(SEQ - d)]
        remote(src, src, gg_send.at[d - 1], gg_recv.at[d - 1], {"seq": speer(d)}).wait_recv()
    gains_ref[...] = jnp.sum(gg_all[...], axis=0)[0:LAYERS, 0:LOCAL]
    w_step5(0)
    for layer in range(LAYERS):
        store_w(layer).wait()
    for copy in pending:
        copy.wait_send()


def dma(*shape):
    return pltpu.SemaphoreType.DMA(shape)


def section(*operands):
    vmem = pl.BlockSpec(memory_space=pltpu.VMEM)
    hbm = pl.BlockSpec(memory_space=pl.ANY)
    return pl.pallas_call(
        section_kernel,
        out_shape=(
            jax.ShapeDtypeStruct((1, JUNC), F32),
            jax.ShapeDtypeStruct((LOCAL, LENGTH), F32),
            jax.ShapeDtypeStruct((LAYERS, 2, SIDE, 144, 384), BF16),
            jax.ShapeDtypeStruct((LAYERS, LOCAL), F32),
        ),
        in_specs=[vmem, hbm, vmem, hbm, hbm] + [vmem] * 5,
        out_specs=(vmem, vmem, hbm, vmem),
        scratch_shapes=[
            pltpu.VMEM((LAYERS, 3 * LOCAL, CHANNELS), BF16),
            pltpu.VMEM((LOCAL, LENGTH), F32),
            pltpu.VMEM((LOCAL, 128), F32),
            pltpu.VMEM((367, 256), F32),
            pltpu.VMEM((128, 128), F32),
            pltpu.VMEM((384, 128), F32),
            pltpu.VMEM((LAYERS, 16, 2, HALF, WIN), BF16),
            pltpu.VMEM((LAYERS, CHANNELS, WIN), BF16),
            pltpu.VMEM((LAYERS, CHANNELS, LENGTH), BF16),
            pltpu.VMEM((LAYERS, 3 * LOCAL, LENGTH), F32),
            pltpu.VMEM((3 * LOCAL, WIN), F32),
            pltpu.VMEM((LAYERS, 16, 1, WIN), F32),
            pltpu.VMEM((LAYERS, 8, WIN), F32),
            pltpu.VMEM((LAYERS, CHANNELS, 3 * LOCAL), BF16),
            pltpu.VMEM((SEQ, 1, JUNC), jnp.int32),
            pltpu.VMEM((LENGTH, SEQ * CAP), BF16),
            pltpu.VMEM((SEQ * CAP, JUNC), BF16),
            pltpu.VMEM((LENGTH, JUNC), BF16),
            pltpu.VMEM((LOCAL, JUNC), F32),
            pltpu.VMEM((LOCAL, LENGTH), BF16),
            pltpu.VMEM((LOCAL, SEQ * CAP), BF16),
            pltpu.VMEM((LOCAL, SEQ * CAP), BF16),
            pltpu.VMEM((LOCAL, SEQ * CAP), BF16),
            pltpu.VMEM((LOCAL, SEQ * CAP), BF16),
            pltpu.VMEM((16, 1, JUNC), F32),
            pltpu.VMEM((LOCAL, LENGTH), F32),
            pltpu.VMEM((LAYERS, LOCAL, LENGTH), BF16),
            pltpu.VMEM((2, LOCAL, 128), BF16),
            pltpu.VMEM((LAYERS, 2, LOCAL, 128), BF16),
            pltpu.VMEM((LAYERS, 2, 2, 3, 192, 256), BF16),
            pltpu.VMEM((LAYERS, 2, 2, 3, 192, 256), BF16),
            pltpu.VMEM((2, 2, SIDE, HALF, 256), F32),
            pltpu.VMEM((LAYERS, 2, 2, SIDE, HALF, 256), BF16),
            pltpu.VMEM((LAYERS, 2, 2, 3, HALF, 256), BF16),
            pltpu.VMEM((LAYERS, 16, 1, LENGTH), F32),
            pltpu.VMEM((LAYERS, 2, 144, CHANNELS), BF16),
            pltpu.VMEM((LAYERS, 144, CHANNELS), BF16),
            pltpu.VMEM((LAYERS, SIDE, 144, 384), BF16),
            pltpu.VMEM((LAYERS, 3, 144, 384), BF16),
            pltpu.VMEM((LAYERS, 2, SIDE, 144, 384), BF16),
            pltpu.VMEM((128, 128), F32),
            pltpu.VMEM((SEQ, 8, 128), F32),
            dma(4, 2),
            dma(4, 2),
            dma(LAYERS, 30),
            dma(LAYERS, 16, 2),
            dma(7),
            dma(7),
            dma(7),
            dma(7),
            dma(7),
            dma(7),
            dma(15),
            dma(15),
            dma(LAYERS, 2, 2, 6),
            dma(LAYERS, 2, 2, 6),
            dma(LAYERS, 15),
            dma(LAYERS, 15),
            dma(LAYERS, 11),
            dma(LAYERS, 11),
            dma(7),
            dma(7),
            dma(LAYERS, 15),
            dma(LAYERS, 15),
            dma(15),
            dma(15),
            dma(6),
        ],
        compiler_params=pltpu.CompilerParams(
            collective_id=0, has_side_effects=True, vmem_limit_bytes=62 * 1024 * 1024
        ),
        name="conv_section",
    )(*operands)


def finish_kernel(
    w_in, scores_in, grad_in, gains_in, w_out, scores_out, grad_out, gains_out, wb, wf, sb, gb, nb, sem
):
    small = ((scores_in, sb, scores_out), (grad_in, gb, grad_out), (gains_in, nb, gains_out))
    loads = [pltpu.make_async_copy(w_in.at[k], wb.at[k], sem.at[k]) for k in range(LAYERS)]
    for k, (source, buffer, _) in enumerate(small):
        loads.append(pltpu.make_async_copy(source, buffer, sem.at[LAYERS + k]))
    for load in loads:
        load.start()
    stores = []
    for k in range(LAYERS):
        loads[k].wait()
        for h in range(2):
            for q in range(SIDE):
                wf[k, 144 * h : 144 * h + 144, 384 * q : 384 * q + 384] = wb[k, h, q].astype(F32)
            rows = pl.ds(144 * h, 144)
            store = pltpu.make_async_copy(wf.at[k, rows], w_out.at[k, rows], sem.at[6 + 2 * k + h])
            store.start()
            stores.append(store)
    for k, (_, buffer, target) in enumerate(small):
        loads[LAYERS + k].wait()
        store = pltpu.make_async_copy(buffer, target, sem.at[12 + k])
        store.start()
        stores.append(store)
    for store in stores:
        store.wait()


def finish(weights, scores, grad, gains):
    hbm = pl.BlockSpec(memory_space=pl.ANY)
    return pl.pallas_call(
        finish_kernel,
        out_shape=(
            jax.ShapeDtypeStruct((LAYERS, 3 * LOCAL, CHANNELS), F32),
            jax.ShapeDtypeStruct(scores.shape, F32),
            jax.ShapeDtypeStruct(grad.shape, F32),
            jax.ShapeDtypeStruct(gains.shape, F32),
        ),
        in_specs=[hbm] * 4,
        out_specs=(hbm,) * 4,
        scratch_shapes=[
            pltpu.VMEM(weights.shape, BF16),
            pltpu.VMEM((LAYERS, 3 * LOCAL, CHANNELS), F32),
            pltpu.VMEM(scores.shape, F32),
            pltpu.VMEM(grad.shape, F32),
            pltpu.VMEM(gains.shape, F32),
            dma(15),
        ],
        name="finish",
    )(weights, scores, grad, gains)


def local(
    sequence_in,
    conv_weight,
    norm_gain,
    tissue_scale,
    donor_offset,
    acceptor_owner,
    acceptor_offset,
    tissue,
    tower_grad,
    score_grad,
):
    stacked = conv_weight.transpose(0, 2, 1, 3).reshape(LAYERS, 3 * LOCAL, CHANNELS)
    scores, grad, weights, gains = section(
        sequence_in,
        stacked,
        norm_gain,
        tower_grad,
        tissue_scale,
        acceptor_owner.T,
        acceptor_offset[None, :],
        donor_offset[None, :],
        tissue[None, :],
        score_grad[None, :],
    )
    weights, scores, grad, gains = finish(weights, scores, grad, gains)
    weights = weights.reshape(LAYERS, 3, LOCAL, CHANNELS).transpose(0, 2, 1, 3)
    return (scores[0], grad, weights, gains)


def solution(mesh):
    return jax.shard_map(
        local,
        mesh=mesh,
        in_specs=(
            P("tp", "seq"),
            P(None, "tp", None, None),
            P(None, "tp"),
            P(),
            P("seq"),
            P("seq", None),
            P("seq"),
            P("seq"),
            P("tp", "seq"),
            P("seq"),
        ),
        out_specs=(P("seq"), P("tp", "seq"), P(None, "tp", None, None), P(None, "tp")),
        check_vma=False,
    )
```

```python
import math

import jax
import jax.numpy as jnp
from jax import lax
from jax.experimental import pallas as pl
from jax.experimental.pallas import tpu as pltpu
from jax.sharding import PartitionSpec as P

CHANNELS = 1536
LAYERS = 3
LOCAL = 96
HALF = 48
LENGTH = 512
WIN = 640
SIDE = 4
SEQ = 8
JUNC = 256
CAP = 128
MESH = pl.DeviceIdType.MESH
EPSILON = 1e-06
ROOT = math.sqrt(CHANNELS)
GELU_C = math.sqrt(2.0 / math.pi)
GELU_A = 0.044715
F32 = jnp.float32
BF16 = jnp.bfloat16
NEAR = (1, 3, 2)


def remote(src, dst, send_sem, recv_sem, device):
    return pltpu.make_async_remote_copy(
        src_ref=src,
        dst_ref=dst,
        send_sem=send_sem,
        recv_sem=recv_sem,
        device_id=device,
        device_id_type=MESH,
    )


def dot(a, b):
    return jnp.dot(a, b, preferred_element_type=F32)


def dot_rows(a, b):
    return lax.dot_general(a, b, (((1,), (1,)), ((), ())), preferred_element_type=F32)


def section_kernel(
    seq_ref,
    w_hbm,
    gain_in,
    tower_hbm,
    table_hbm,
    owner_ref,
    offset_ref,
    donor_ref,
    tissue_ref,
    sgrad_ref,
    scores_ref,
    grad_ref,
    wgrad_ref,
    gains_ref,
    w_ref,
    tower_ref,
    gain_ref,
    window,
    turn,
    tab,
    gst,
    hid,
    mm,
    vv,
    ysum,
    pw,
    inv,
    wt,
    meta_all,
    pick,
    slots,
    donor_hot,
    tissue_rows,
    state3,
    acc_tx,
    acc_rx,
    ab_tx,
    ab_rx,
    sc_all,
    up,
    gbuf,
    halo_rx,
    halo_b,
    pab,
    rx,
    sf,
    sab,
    ry,
    inn,
    wg,
    wrx,
    wz_tx,
    wz_rx,
    wres,
    gg,
    gg_all,
    halo_send,
    halo_recv,
    gather_send,
    gather_recv,
    meta_send,
    meta_recv,
    acc_send,
    acc_recv,
    ab_send,
    ab_recv,
    sc_send,
    sc_recv,
    rs_send,
    rs_recv,
    inn_send,
    inn_recv,
    w_send,
    w_recv,
    gg_send,
    gg_recv,
    pw_send,
    pw_recv,
    load_sem,
):
    s = lax.axis_index("seq")
    me = lax.axis_index("tp")
    mx = me // SIDE
    my = lax.rem(me, SIDE)
    mz = s // 2
    core = lax.rem(s, 2)

    def xpeer(d):
        return lax.rem(mx + d, SIDE) * SIDE + my

    def ypeer(d):
        return mx * SIDE + lax.rem(my + d, SIDE)

    def tpeer(d):
        return lax.rem(me + d, SIDE * SIDE)

    def speer(d):
        return lax.rem(s + d, SEQ)

    def zpeer(d):
        return lax.rem(mz + d, SIDE) * 2 + core

    partner = mz * 2 + 1 - core

    load_w = pltpu.make_async_copy(w_hbm, w_ref, load_sem.at[0])
    load_tower = pltpu.make_async_copy(tower_hbm, tower_ref, load_sem.at[1])
    start = jnp.minimum(me * LOCAL // 128, CHANNELS // 128 - 2) * 128
    skip = me * LOCAL - start
    load_table = pltpu.make_async_copy(
        table_hbm.at[:, pl.ds(pl.multiple_of(start, 128), 256)], window, load_sem.at[2]
    )
    load_w.start()
    load_table.start()
    load_tower.start()

    barrier = pltpu.get_barrier_semaphore()
    for d in range(1, SIDE * SIDE):
        pl.semaphore_signal(barrier, inc=1, device_id={"tp": tpeer(d)}, device_id_type=MESH)
    for d in range(1, SEQ):
        pl.semaphore_signal(barrier, inc=1, device_id={"seq": speer(d)}, device_id_type=MESH)
    turn[...] = jnp.zeros((128, 128), F32)
    for k in range(3):
        turn[56 + 3 * k : 59 + 3 * k, 0:LOCAL] = gain_in[...]
    gain_ref[...] = turn[...].T[0:LOCAL]
    pl.semaphore_wait(barrier, SIDE * SIDE - 1 + SEQ - 1)

    pending = []

    def begin(copy):
        copy.start()
        pending.append(copy)

    def halo_left(src, dst, k):
        return remote(src.at[:, 0:128], dst.at[0], halo_send.at[k, 0], halo_recv.at[k, 0], {"seq": s - 1})

    def halo_right(src, dst, k):
        return remote(src.at[:, 384:512], dst.at[1], halo_send.at[k, 1], halo_recv.at[k, 1], {"seq": s + 1})

    def halo_start(src, dst, k):
        @pl.when(s > 0)
        def _():
            halo_left(src, dst, k).start()

        @pl.when(s < SEQ - 1)
        def _():
            halo_right(src, dst, k).start()

        @pl.when(s == 0)
        def _():
            dst[1] = jnp.zeros((LOCAL, 128), BF16)

        @pl.when(s == SEQ - 1)
        def _():
            dst[0] = jnp.zeros((LOCAL, 128), BF16)

    def halo_wait(src, dst, k):
        @pl.when(s > 0)
        def _():
            halo_left(src, dst, k).wait_send()
            remote(
                src.at[:, 384:512], dst.at[1], halo_send.at[k, 1], halo_recv.at[k, 1], {"seq": s - 1}
            ).wait_recv()

        @pl.when(s < SEQ - 1)
        def _():
            halo_right(src, dst, k).wait_send()
            remote(
                src.at[:, 0:128], dst.at[0], halo_send.at[k, 0], halo_recv.at[k, 0], {"seq": s + 1}
            ).wait_recv()

    lane = lax.broadcasted_iota(jnp.int32, (LOCAL, 128), 1)

    def halo_tile(dst):
        return jnp.where(lane < 64, dst[0].astype(F32), dst[1].astype(F32))

    halo_start(seq_ref, halo_rx, 0)

    gain = gain_ref[...]
    high = gain.astype(BF16).astype(F32)
    rest = gain - high
    mid = rest.astype(BF16).astype(F32)
    low = rest - mid
    packed = jnp.where(lane < 59, high, jnp.where(lane < 62, mid, low))
    in_gain = (lane >= 56) & (lane < 65)

    for h in range(2):
        gst[0, me, h, :, 0:512] = seq_ref[HALF * h : HALF * h + HALF, :]
    halo_wait(seq_ref, halo_rx, 0)
    tile = jnp.where(in_gain, packed, halo_tile(halo_rx)).astype(BF16)
    for h in range(2):
        gst[0, me, h, :, 512:640] = tile[HALF * h : HALF * h + HALF, :]

    col = lax.broadcasted_iota(jnp.int32, (LOCAL, WIN), 1)
    outside = ((s == SEQ - 1) & (col >= 512) & (col < 576)) | ((s == 0) & (col >= 576))

    def transpose_weights(layer):
        for x in range(SIDE):
            block = w_ref[layer, :, 384 * x : 384 * x + 384].astype(F32).T.astype(BF16)
            for y in range(SIDE):
                a = 192 * x + HALF * y
                b = 768 + 192 * y + HALF * x
                wt[layer, a : a + HALF, :] = block[96 * y : 96 * y + HALF]
                wt[layer, b : b + HALF, :] = block[96 * y + HALF : 96 * y + 96]

    def one_hot(rows, row_ids, base):
        ids = lax.broadcasted_iota(jnp.int32, (rows, JUNC), 0) + base
        return jnp.where(ids == row_ids, 1.0, 0.0).astype(BF16)

    def prepare_tissues():
        load_table.wait()
        tab[...] = jnp.zeros((384, 128), F32)
        tab[0 : window.shape[0], :] = pltpu.roll(window[...], lax.rem(256 - skip, 256), 1)[:, 0:128]
        table = tab[...].T[0:LOCAL]
        t_high = table.astype(BF16)
        t_rest = table - t_high.astype(F32)
        t_mid = t_rest.astype(BF16)
        t_low = (t_rest - t_mid.astype(F32)).astype(BF16)
        hot = one_hot(384, tissue_ref[...], 0)
        tissue_rows[...] = dot(t_high, hot) + dot(t_mid, hot) + dot(t_low, hot)
        donor_hot[...] = one_hot(LENGTH, donor_ref[...], 0)

    def send_meta():
        owner = owner_ref[...]
        member = one_hot(16, owner, 0)
        first = lax.broadcasted_iota(jnp.int32, (JUNC, JUNC), 0)
        second = lax.broadcasted_iota(jnp.int32, (JUNC, JUNC), 1)
        rank = dot(member, jnp.where(first <= second, 1.0, 0.0).astype(BF16))
        slot = jnp.sum(member.astype(F32) * rank, axis=0, keepdims=True) - 1.0
        slot = slot.astype(jnp.int32)
        meta_all[s] = (slot * SEQ + owner) * LENGTH + offset_ref[...]
        for d in range(1, SEQ):
            begin(
                remote(
                    meta_all.at[s], meta_all.at[s], meta_send.at[d - 1], meta_recv.at[d - 1], {"seq": speer(d)}
                )
            )
        ids = lax.broadcasted_iota(jnp.int32, (CAP, JUNC), 0)
        for d in range(SEQ):
            mine = (ids == slot) & (owner == speer(d))
            slots[CAP * d : CAP * d + CAP, :] = jnp.where(mine, 1.0, 0.0).astype(BF16)

    def wait_meta():
        for d in range(1, SEQ):
            src = speer(SEQ - d)
            remote(
                meta_all.at[src], meta_all.at[src], meta_send.at[d - 1], meta_recv.at[d - 1], {"seq": src}
            ).wait_recv()

    def prepare_picks(which):
        for d in which:
            row = meta_all[speer(d)]
            place = one_hot(LENGTH, row & (SEQ * LENGTH - 1), s * LENGTH)
            slot = one_hot(CAP, lax.shift_right_logical(row, 12), 0)
            pick[:, CAP * d : CAP * d + CAP] = dot_rows(place, slot).astype(BF16)

    for layer in range(LAYERS):
        reach = 2 ** (layer + 3)
        count = [0]

        def go(block, h, peer, layer=layer, count=count):
            begin(
                remote(
                    gst.at[layer, block, h],
                    gst.at[layer, block, h],
                    gather_send.at[layer, count[0]],
                    gather_recv.at[layer, block, h],
                    {"tp": peer},
                )
            )
            count[0] += 1

        def arrived(block, h, layer=layer):
            remote(
                gst.at[layer, block, h],
                gst.at[layer, block, h],
                gather_send.at[layer, 0],
                gather_recv.at[layer, block, h],
                {"tp": xpeer(1)},
            ).wait_recv()

        squares = jnp.concatenate([gst[layer, me, 0], gst[layer, me, 1]], axis=0).astype(F32)
        pw[layer, me] = jnp.sum(squares * squares, axis=0, keepdims=True)
        for d in range(1, SIDE * SIDE):
            begin(
                remote(
                    pw.at[layer, me],
                    pw.at[layer, me],
                    pw_send.at[layer, d - 1],
                    pw_recv.at[layer, d - 1],
                    {"tp": tpeer(d)},
                )
            )
        def at(h, p, q):
            dx, dy = (p, q) if h == 0 else (q, p)
            return lax.rem(mx + dx, SIDE) * SIDE + lax.rem(my + dy, SIDE)

        waited = set()

        def wait_block(h, p, q, at=at, waited=waited, arrived=arrived):
            if (h, p, q) not in waited:
                waited.add((h, p, q))
                arrived(at(h, p, q), h)

        def relay(h, p, q, targets, at=at, go=go, wait_block=wait_block):
            if (p, q) != (0, 0):
                wait_block(h, p, q)
            for target in targets:
                go(at(h, p, q), h, at(h, *target))

        def second_axis(p, relay=relay):
            for h in range(2):
                if p % 2 == 0:
                    relay(h, p, 3, ((0, 1),))
                else:
                    relay(h, p, 1, ((0, 3),))

        ahead = (3, 1)
        for h in range(2):
            relay(h, 0, 0, ((1, 0), (3, 0)))
        for h in range(2):
            relay(h, 0, 0, ((0, 1), (0, 3)))
        for h in range(2):
            relay(h, ahead[h], 0, ((SIDE - ahead[h], 0), (0, 1), (0, 3)))
        for h in range(2):
            relay(h, SIDE - ahead[h], 0, ((0, 1), (0, 3)))
        second_axis(0)
        if layer == 0:
            send_meta()
            load_w.wait()
        else:
            vv[layer - 1] = dot(w_ref[layer - 1], mm[layer - 1])
        for h in range(2):
            relay(h, 2, 0, ((0, 1), (0, 3)))
        second_axis(1)
        second_axis(3)

        for d in range(1, SIDE * SIDE):
            src = pw.at[layer, tpeer(SIDE * SIDE - d)]
            remote(
                src, src, pw_send.at[layer, d - 1], pw_recv.at[layer, d - 1], {"tp": tpeer(d)}
            ).wait_recv()
        power = jnp.sum(pw[layer], axis=0) / CHANNELS
        inverse = 1.0 / jnp.sqrt(power + EPSILON)
        inv[layer] = jnp.broadcast_to(inverse, (8, WIN))

        def hide(block, carry, layer=layer):
            scale = inv[layer, 0:1, :]
            for h in range(2):
                head = gst[0, block, h, :, 512:640].astype(F32)
                g = (
                    head[:, 56 + layer : 57 + layer]
                    + head[:, 59 + layer : 60 + layer]
                    + head[:, 62 + layer : 63 + layer]
                )
                rows = pl.ds(pl.multiple_of(block * LOCAL + HALF * h, 16), HALF)
                raw = gst[layer, block, h, :, 0:LENGTH].astype(F32) * g
                x = raw * scale[:, 0:LENGTH]
                xx = x * x
                t = jnp.tanh(GELU_C * (x + GELU_A * (xx * x)))
                upper = 0.5 * (1.0 + t)
                hid[layer, rows, 0:LENGTH] = (x * upper).astype(BF16)
                slope = upper + (0.5 * x) * (1.0 - t * t) * (GELU_C + (3.0 * GELU_A * GELU_C) * xx)
                mm[layer, rows, :] = (raw * slope).astype(BF16)
                x = gst[layer, block, h, :, LENGTH:WIN].astype(F32) * scale[:, LENGTH:WIN] * g
                t = jnp.tanh(GELU_C * (x + GELU_A * (x * x * x)))
                hid[layer, rows, LENGTH:WIN] = (0.5 * x * (1.0 + t)).astype(BF16)
            return carry

        for d in (0,) + NEAR:
            group = lax.rem(mx + d, SIDE)
            for e in (0,) + NEAR:
                if d + e > 0:
                    wait_block(0, d, e)
                    wait_block(1, e, d)
                if d == NEAR[-1]:
                    hide(group * SIDE + lax.rem(my + e, SIDE), 0)
            if d != NEAR[-1]:
                lax.fori_loop(group * SIDE, group * SIDE + SIDE, hide, 0)
            span = pl.ds(pl.multiple_of(group * 384, 128), 384)
            part = dot(w_ref[layer, :, span], hid[layer, span, :])
            if d == 0:
                ysum[...] = part
                second_axis(2)
                transpose_weights(layer)
                if layer == 0:
                    prepare_tissues()
                if layer == 1:
                    wait_meta()
                    prepare_picks(range(0, 4))
                if layer == 2:
                    prepare_picks(range(4, 8))
            elif d != NEAR[-1]:
                ysum[...] += part
            else:
                y = ysum[...] + part

        mixed = pltpu.roll(y[0:96], reach, 1) + y[96:192] + pltpu.roll(y[192:288], WIN - reach, 1)
        own = jnp.concatenate([gst[layer, me, 0], gst[layer, me, 1]], axis=0)
        state = own.astype(F32) + mixed
        if layer < LAYERS - 1:
            state = jnp.where(outside, 0.0, state).astype(BF16)
            for h in range(2):
                gst[layer + 1, me, h] = state[HALF * h : HALF * h + HALF, :]
        else:
            state3[...] = state[:, 0:LENGTH].astype(BF16)

    def acc_copy(d):
        return remote(
            acc_tx.at[:, CAP * d : CAP * d + CAP],
            acc_rx.at[:, CAP * (SEQ - d) : CAP * (SEQ - d) + CAP],
            acc_send.at[d - 1],
            acc_recv.at[d - 1],
            {"seq": speer(d)},
        )

    def ab_copy(d):
        return remote(
            ab_tx.at[:, CAP * d : CAP * d + CAP],
            ab_rx.at[:, CAP * (SEQ - d) : CAP * (SEQ - d) + CAP],
            ab_send.at[d - 1],
            ab_recv.at[d - 1],
            {"seq": speer(d)},
        )

    acc_tx[...] = dot(state3[...], pick[...]).astype(BF16)
    for d in range(1, SEQ):
        begin(acc_copy(d))
    acc_rx[:, 0:CAP] = acc_tx[:, 0:CAP]
    donor = dot(state3[...], donor_hot[...])
    load_tower.wait()
    weight_j = sgrad_ref[...] / ROOT
    rows_q = tissue_rows[...]
    accept_back = (weight_j * donor * rows_q).astype(BF16)
    ab_tx[...] = dot_rows(accept_back, slots[...]).astype(BF16)
    for d in range(1, SEQ):
        begin(ab_copy(d))
    ab_rx[:, 0:CAP] = ab_tx[:, 0:CAP]
    vv[LAYERS - 1] = dot(w_ref[LAYERS - 1], mm[LAYERS - 1])
    for d in range(1, SEQ):
        acc_copy(d).wait_recv()
    accept = dot(acc_rx[...], slots[...])
    donor_back = weight_j * accept * rows_q
    d_high = donor_back.astype(BF16)
    d_low = (donor_back - d_high.astype(F32)).astype(BF16)
    up[...] = tower_ref[...] + dot_rows(d_high, donor_hot[...]) + dot_rows(d_low, donor_hot[...])
    sc_all[me] = jnp.sum(donor * accept * rows_q, axis=0, keepdims=True) / ROOT
    for d in range(1, SEQ):
        ab_copy(d).wait_recv()
    up[...] += dot_rows(ab_rx[...], pick[...])
    for d in range(1, SIDE * SIDE):
        begin(
            remote(sc_all.at[me], sc_all.at[me], sc_send.at[d - 1], sc_recv.at[d - 1], {"tp": tpeer(d)})
        )

    def w_cores(layer):
        return remote(
            wg.at[layer, 1 - core], wrx.at[layer], w_send.at[layer, 0], w_recv.at[layer, 0], {"seq": partner}
        )

    def w_slices(layer, d):
        return remote(
            wz_tx.at[layer, lax.rem(mz + d, SIDE)],
            wz_rx.at[layer, d - 1],
            w_send.at[layer, d],
            w_recv.at[layer, d],
            {"seq": zpeer(d)},
        )

    def w_result(layer, d):
        return remote(
            wres.at[layer, core, mz],
            wres.at[layer, core, mz],
            w_send.at[layer, 3 + d],
            w_recv.at[layer, 3 + d],
            {"seq": zpeer(d)},
        )

    def w_share(layer, d):
        part = wres.at[layer, core, lax.rem(mz + SIDE - d, SIDE)]
        return remote(part, part, w_send.at[layer, 7 + d], w_recv.at[layer, 7 + d], {"seq": partner})

    def w_step2(layer):
        w_cores(layer).wait_recv()
        summed = wg[layer, core].astype(F32) + wrx[layer].astype(F32)
        for q in range(SIDE):
            wz_tx[layer, q] = summed[:, 384 * q : 384 * q + 384].astype(BF16)
        for d in NEAR:
            begin(w_slices(layer, d))

    def w_step3(layer):
        result = wz_tx[layer, mz].astype(F32)
        for d in NEAR:
            w_slices(layer, d).wait_recv()
            result = result + wz_rx[layer, d - 1].astype(F32)
        wres[layer, core, mz] = result.astype(BF16)
        for d in NEAR:
            begin(w_result(layer, d))
        begin(w_share(layer, 0))

    def w_step4(layer):
        for d in NEAR:
            src = wres.at[layer, core, lax.rem(mz + SIDE - d, SIDE)]
            remote(
                src, src, w_send.at[layer, 3 + d], w_recv.at[layer, 3 + d], {"seq": zpeer(d)}
            ).wait_recv()
            begin(w_share(layer, d))

    def store_w(layer):
        return pltpu.make_async_copy(wres.at[layer], wgrad_ref.at[layer], load_sem.at[3 + layer])

    def w_step5(layer):
        for d in range(SIDE):
            part = wres.at[layer, 1 - core, lax.rem(mz + SIDE - d, SIDE)]
            remote(
                part, part, w_send.at[layer, 7 + d], w_recv.at[layer, 7 + d], {"seq": partner}
            ).wait_recv()
        store_w(layer).start()

    gg[...] = jnp.zeros((128, 128), F32)
    for layer in reversed(range(LAYERS)):
        reach = 2 ** (layer + 3)
        shifts = (WIN - reach, 0, reach)
        gbuf[layer] = up[...].astype(BF16)
        halo_start(gbuf.at[layer], halo_b.at[layer], layer + 1)
        g = gbuf[layer].astype(F32)

        def shifted(window, shifts=shifts):
            rolled = [pltpu.roll(window, k, 1) if k else window for k in shifts]
            return jnp.concatenate(rolled, axis=0)

        inner_g = shifted(jnp.concatenate([g, jnp.zeros((LOCAL, 128), F32)], axis=1)).astype(BF16)

        def chunk(h, index, window, layer=layer):
            rows = pl.ds(pl.multiple_of(768 * h + 192 * index, 16), 192)
            return dot(wt[layer, rows, :], window)

        def rs_one(h, c, d, layer=layer):
            return remote(
                pab.at[layer, h, c, d - 1],
                rx.at[layer, h, c, d - 1],
                rs_send.at[layer, h, c, d - 1],
                rs_recv.at[layer, h, c, d - 1],
                {"tp": xpeer(d) if h == 0 else ypeer(d)},
            )

        def rs_two(h, c, d, layer=layer):
            index = lax.rem((my if h == 0 else mx) + d, SIDE)
            return remote(
                sab.at[layer, h, c, index],
                ry.at[layer, h, c, d - 1],
                rs_send.at[layer, h, c, 2 + d],
                rs_recv.at[layer, h, c, 2 + d],
                {"tp": ypeer(d) if h == 0 else xpeer(d)},
            )

        def partials(c, window, layer=layer, chunk=chunk, rs_one=rs_one):
            for d in NEAR:
                for h in range(2):
                    base = mx if h == 0 else my
                    pab[layer, h, c, d - 1] = chunk(h, lax.rem(base + d, SIDE), window).astype(BF16)
                    begin(rs_one(h, c, d))
            for h in range(2):
                own = chunk(h, mx if h == 0 else my, window)
                sf[h, c] = own.reshape(SIDE, HALF, 256)

        partials(0, inner_g[:, 128:384])
        for q in range(3):
            part = dot_rows(inner_g, hid[layer, 512 * q : 512 * q + 512, :]).astype(BF16)
            for h in range(2):
                wg[layer, h, :, 512 * q : 512 * q + 512] = part[144 * h : 144 * h + 144]
        begin(w_cores(layer))
        halo_wait(gbuf.at[layer], halo_b.at[layer], layer + 1)
        full_g = shifted(jnp.concatenate([g, halo_tile(halo_b.at[layer])], axis=1))
        full_g = full_g[:, 0:LENGTH]
        partials(1, jnp.concatenate([full_g[:, 0:128], full_g[:, 384:512]], axis=1).astype(BF16))
        inn[layer, me] = jnp.sum(full_g * vv[layer], axis=0, keepdims=True)
        for d in range(1, SIDE * SIDE):
            begin(
                remote(
                    inn.at[layer, me],
                    inn.at[layer, me],
                    inn_send.at[layer, d - 1],
                    inn_recv.at[layer, d - 1],
                    {"tp": tpeer(d)},
                )
            )
        if layer < LAYERS - 1:
            w_step4(layer + 1)
        w_step2(layer)
        for c in range(2):
            for h in range(2):
                for d in NEAR:
                    rs_one(h, c, d).wait_recv()
                    sf[h, c] += rx[layer, h, c, d - 1].astype(F32).reshape(SIDE, HALF, 256)
                sab[layer, h, c] = sf[h, c].astype(BF16)
                for d in NEAR:
                    begin(rs_two(h, c, d))
            if c == 0 and layer == 0:
                w_step3(layer)
        if layer > 0:
            w_step3(layer)
        if layer < LAYERS - 1:
            w_step5(layer + 1)

        x = (seq_ref[...] if layer == 0 else jnp.concatenate(
            [gst[layer, me, 0, :, 0:LENGTH], gst[layer, me, 1, :, 0:LENGTH]], axis=0
        )).astype(F32)
        scale = inv[layer, 0:1, 0:LENGTH]
        g_col = gain_ref[:, 56 + layer : 57 + layer]
        norm = x * scale
        pre = norm * g_col
        t = jnp.tanh(GELU_C * (pre + GELU_A * (pre * pre * pre)))
        slope = 0.5 * (1.0 + t) + 0.5 * pre * (1.0 - t * t) * (
            GELU_C * (1.0 + 3.0 * GELU_A * (pre * pre))
        )
        halves = []
        for h in range(2):
            sides = []
            for c in range(2):
                back = sf[h, c, my if h == 0 else mx]
                for d in NEAR:
                    rs_two(h, c, d).wait_recv()
                    back = back + ry[layer, h, c, d - 1].astype(F32)
                sides.append(back)
            middle, edges = sides
            halves.append(jnp.concatenate([edges[:, 0:128], middle, edges[:, 128:256]], axis=1))
        back_pre = jnp.concatenate(halves, axis=0) * slope
        back_norm = back_pre * g_col
        gain_col = jnp.sum(back_pre * norm, axis=1, keepdims=True)
        gg[0:LOCAL, :] = jnp.where(lane == layer, gain_col, gg[0:LOCAL, :])
        if layer == 0:
            gg_all[s] = gg[...].T[0:8]
            for d in range(1, SEQ):
                begin(
                    remote(
                        gg_all.at[s], gg_all.at[s], gg_send.at[d - 1], gg_recv.at[d - 1], {"seq": speer(d)}
                    )
                )
        for d in range(1, SIDE * SIDE):
            src = inn.at[layer, tpeer(SIDE * SIDE - d)]
            remote(
                src, src, inn_send.at[layer, d - 1], inn_recv.at[layer, d - 1], {"tp": tpeer(d)}
            ).wait_recv()
        inner = jnp.sum(inn[layer], axis=0)
        up[...] = up[...] + scale * back_norm - x * (scale * scale * scale) * (inner / CHANNELS)

    grad_ref[...] = up[...]
    w_step4(0)
    for d in range(1, SIDE * SIDE):
        src = sc_all.at[tpeer(SIDE * SIDE - d)]
        remote(src, src, sc_send.at[d - 1], sc_recv.at[d - 1], {"tp": tpeer(d)}).wait_recv()
    scores_ref[...] = jnp.sum(sc_all[...], axis=0)
    for d in range(1, SEQ):
        src = gg_all.at[speer(SEQ - d)]
        remote(src, src, gg_send.at[d - 1], gg_recv.at[d - 1], {"seq": speer(d)}).wait_recv()
    gains_ref[...] = jnp.sum(gg_all[...], axis=0)[0:LAYERS, 0:LOCAL]
    w_step5(0)
    for layer in range(LAYERS):
        store_w(layer).wait()
    for copy in pending:
        copy.wait_send()


def dma(*shape):
    return pltpu.SemaphoreType.DMA(shape)


def section(*operands):
    vmem = pl.BlockSpec(memory_space=pltpu.VMEM)
    hbm = pl.BlockSpec(memory_space=pl.ANY)
    return pl.pallas_call(
        section_kernel,
        out_shape=(
            jax.ShapeDtypeStruct((1, JUNC), F32),
            jax.ShapeDtypeStruct((LOCAL, LENGTH), F32),
            jax.ShapeDtypeStruct((LAYERS, 2, SIDE, 144, 384), BF16),
            jax.ShapeDtypeStruct((LAYERS, LOCAL), F32),
        ),
        in_specs=[vmem, hbm, vmem, hbm, hbm] + [vmem] * 5,
        out_specs=(vmem, vmem, hbm, vmem),
        scratch_shapes=[
            pltpu.VMEM((LAYERS, 3 * LOCAL, CHANNELS), BF16),
            pltpu.VMEM((LOCAL, LENGTH), F32),
            pltpu.VMEM((LOCAL, 128), F32),
            pltpu.VMEM((367, 256), F32),
            pltpu.VMEM((128, 128), F32),
            pltpu.VMEM((384, 128), F32),
            pltpu.VMEM((LAYERS, 16, 2, HALF, WIN), BF16),
            pltpu.VMEM((LAYERS, CHANNELS, WIN), BF16),
            pltpu.VMEM((LAYERS, CHANNELS, LENGTH), BF16),
            pltpu.VMEM((LAYERS, 3 * LOCAL, LENGTH), F32),
            pltpu.VMEM((3 * LOCAL, WIN), F32),
            pltpu.VMEM((LAYERS, 16, 1, WIN), F32),
            pltpu.VMEM((LAYERS, 8, WIN), F32),
            pltpu.VMEM((LAYERS, CHANNELS, 3 * LOCAL), BF16),
            pltpu.VMEM((SEQ, 1, JUNC), jnp.int32),
            pltpu.VMEM((LENGTH, SEQ * CAP), BF16),
            pltpu.VMEM((SEQ * CAP, JUNC), BF16),
            pltpu.VMEM((LENGTH, JUNC), BF16),
            pltpu.VMEM((LOCAL, JUNC), F32),
            pltpu.VMEM((LOCAL, LENGTH), BF16),
            pltpu.VMEM((LOCAL, SEQ * CAP), BF16),
            pltpu.VMEM((LOCAL, SEQ * CAP), BF16),
            pltpu.VMEM((LOCAL, SEQ * CAP), BF16),
            pltpu.VMEM((LOCAL, SEQ * CAP), BF16),
            pltpu.VMEM((16, 1, JUNC), F32),
            pltpu.VMEM((LOCAL, LENGTH), F32),
            pltpu.VMEM((LAYERS, LOCAL, LENGTH), BF16),
            pltpu.VMEM((2, LOCAL, 128), BF16),
            pltpu.VMEM((LAYERS, 2, LOCAL, 128), BF16),
            pltpu.VMEM((LAYERS, 2, 2, 3, 192, 256), BF16),
            pltpu.VMEM((LAYERS, 2, 2, 3, 192, 256), BF16),
            pltpu.VMEM((2, 2, SIDE, HALF, 256), F32),
            pltpu.VMEM((LAYERS, 2, 2, SIDE, HALF, 256), BF16),
            pltpu.VMEM((LAYERS, 2, 2, 3, HALF, 256), BF16),
            pltpu.VMEM((LAYERS, 16, 1, LENGTH), F32),
            pltpu.VMEM((LAYERS, 2, 144, CHANNELS), BF16),
            pltpu.VMEM((LAYERS, 144, CHANNELS), BF16),
            pltpu.VMEM((LAYERS, SIDE, 144, 384), BF16),
            pltpu.VMEM((LAYERS, 3, 144, 384), BF16),
            pltpu.VMEM((LAYERS, 2, SIDE, 144, 384), BF16),
            pltpu.VMEM((128, 128), F32),
            pltpu.VMEM((SEQ, 8, 128), F32),
            dma(4, 2),
            dma(4, 2),
            dma(LAYERS, 30),
            dma(LAYERS, 16, 2),
            dma(7),
            dma(7),
            dma(7),
            dma(7),
            dma(7),
            dma(7),
            dma(15),
            dma(15),
            dma(LAYERS, 2, 2, 6),
            dma(LAYERS, 2, 2, 6),
            dma(LAYERS, 15),
            dma(LAYERS, 15),
            dma(LAYERS, 11),
            dma(LAYERS, 11),
            dma(7),
            dma(7),
            dma(LAYERS, 15),
            dma(LAYERS, 15),
            dma(6),
        ],
        compiler_params=pltpu.CompilerParams(
            collective_id=0, has_side_effects=True, vmem_limit_bytes=62 * 1024 * 1024
        ),
        name="conv_section",
    )(*operands)


def finish_kernel(
    w_in, scores_in, grad_in, gains_in, w_out, scores_out, grad_out, gains_out, wb, wf, sb, gb, nb, sem
):
    small = ((scores_in, sb, scores_out), (grad_in, gb, grad_out), (gains_in, nb, gains_out))
    loads = [pltpu.make_async_copy(w_in.at[k], wb.at[k], sem.at[k]) for k in range(LAYERS)]
    for k, (source, buffer, _) in enumerate(small):
        loads.append(pltpu.make_async_copy(source, buffer, sem.at[LAYERS + k]))
    for load in loads:
        load.start()
    stores = []
    for k in range(LAYERS):
        loads[k].wait()
        for h in range(2):
            for q in range(SIDE):
                wf[k, 144 * h : 144 * h + 144, 384 * q : 384 * q + 384] = wb[k, h, q].astype(F32)
            rows = pl.ds(144 * h, 144)
            store = pltpu.make_async_copy(wf.at[k, rows], w_out.at[k, rows], sem.at[6 + 2 * k + h])
            store.start()
            stores.append(store)
    for k, (_, buffer, target) in enumerate(small):
        loads[LAYERS + k].wait()
        store = pltpu.make_async_copy(buffer, target, sem.at[12 + k])
        store.start()
        stores.append(store)
    for store in stores:
        store.wait()


def finish(weights, scores, grad, gains):
    hbm = pl.BlockSpec(memory_space=pl.ANY)
    return pl.pallas_call(
        finish_kernel,
        out_shape=(
            jax.ShapeDtypeStruct((LAYERS, 3 * LOCAL, CHANNELS), F32),
            jax.ShapeDtypeStruct(scores.shape, F32),
            jax.ShapeDtypeStruct(grad.shape, F32),
            jax.ShapeDtypeStruct(gains.shape, F32),
        ),
        in_specs=[hbm] * 4,
        out_specs=(hbm,) * 4,
        scratch_shapes=[
            pltpu.VMEM(weights.shape, BF16),
            pltpu.VMEM((LAYERS, 3 * LOCAL, CHANNELS), F32),
            pltpu.VMEM(scores.shape, F32),
            pltpu.VMEM(grad.shape, F32),
            pltpu.VMEM(gains.shape, F32),
            dma(15),
        ],
        name="finish",
    )(weights, scores, grad, gains)


def local(
    sequence_in,
    conv_weight,
    norm_gain,
    tissue_scale,
    donor_offset,
    acceptor_owner,
    acceptor_offset,
    tissue,
    tower_grad,
    score_grad,
):
    stacked = conv_weight.transpose(0, 2, 1, 3).reshape(LAYERS, 3 * LOCAL, CHANNELS)
    scores, grad, weights, gains = section(
        sequence_in,
        stacked,
        norm_gain,
        tower_grad,
        tissue_scale,
        acceptor_owner.T,
        acceptor_offset[None, :],
        donor_offset[None, :],
        tissue[None, :],
        score_grad[None, :],
    )
    weights, scores, grad, gains = finish(weights, scores, grad, gains)
    weights = weights.reshape(LAYERS, 3, LOCAL, CHANNELS).transpose(0, 2, 1, 3)
    return (scores[0], grad, weights, gains)


def solution(mesh):
    return jax.shard_map(
        local,
        mesh=mesh,
        in_specs=(
            P("tp", "seq"),
            P(None, "tp", None, None),
            P(None, "tp"),
            P(),
            P("seq"),
            P("seq", None),
            P("seq"),
            P("seq"),
            P("tp", "seq"),
            P("seq"),
        ),
        out_specs=(P("seq"), P("tp", "seq"), P(None, "tp", None, None), P(None, "tp")),
        check_vma=False,
    )
```

```python
import math

import jax
import jax.numpy as jnp
from jax import lax
from jax.experimental import pallas as pl
from jax.experimental.pallas import tpu as pltpu
from jax.sharding import PartitionSpec as P

CHANNELS = 1536
LAYERS = 3
LOCAL = 96
HALF = 48
LENGTH = 512
WIN = 640
SIDE = 4
SEQ = 8
JUNC = 256
CAP = 128
MESH = pl.DeviceIdType.MESH
EPSILON = 1e-06
ROOT = math.sqrt(CHANNELS)
GELU_C = math.sqrt(2.0 / math.pi)
GELU_A = 0.044715
F32 = jnp.float32
BF16 = jnp.bfloat16
NEAR = (1, 3, 2)


def remote(src, dst, send_sem, recv_sem, device):
    return pltpu.make_async_remote_copy(
        src_ref=src,
        dst_ref=dst,
        send_sem=send_sem,
        recv_sem=recv_sem,
        device_id=device,
        device_id_type=MESH,
    )


def dot(a, b):
    return jnp.dot(a, b, preferred_element_type=F32)


def dot_rows(a, b):
    return lax.dot_general(a, b, (((1,), (1,)), ((), ())), preferred_element_type=F32)


def section_kernel(
    seq_ref,
    w_hbm,
    gain_in,
    tower_hbm,
    table_hbm,
    owner_ref,
    offset_ref,
    donor_ref,
    tissue_ref,
    sgrad_ref,
    scores_ref,
    grad_ref,
    wgrad_ref,
    gains_ref,
    w_ref,
    tower_ref,
    gain_ref,
    window,
    turn,
    tab,
    gst,
    hid,
    mm,
    vv,
    ysum,
    pw,
    inv,
    wt,
    meta_all,
    pick,
    slots,
    donor_hot,
    tissue_rows,
    state3,
    acc_tx,
    acc_rx,
    ab_tx,
    ab_rx,
    sc_all,
    up,
    gbuf,
    halo_rx,
    halo_b,
    pab,
    rx,
    sf,
    sab,
    ry,
    inn,
    wg,
    wrx,
    wz_tx,
    wz_rx,
    wres,
    gg,
    gg_all,
    halo_send,
    halo_recv,
    gather_send,
    gather_recv,
    meta_send,
    meta_recv,
    acc_send,
    acc_recv,
    ab_send,
    ab_recv,
    sc_send,
    sc_recv,
    rs_send,
    rs_recv,
    inn_send,
    inn_recv,
    w_send,
    w_recv,
    gg_send,
    gg_recv,
    pw_send,
    pw_recv,
    load_sem,
):
    s = lax.axis_index("seq")
    me = lax.axis_index("tp")
    mx = me // SIDE
    my = lax.rem(me, SIDE)
    mz = s // 2
    core = lax.rem(s, 2)

    def xpeer(d):
        return lax.rem(mx + d, SIDE) * SIDE + my

    def ypeer(d):
        return mx * SIDE + lax.rem(my + d, SIDE)

    def tpeer(d):
        return lax.rem(me + d, SIDE * SIDE)

    def speer(d):
        return lax.rem(s + d, SEQ)

    def zpeer(d):
        return lax.rem(mz + d, SIDE) * 2 + core

    partner = mz * 2 + 1 - core

    load_w = pltpu.make_async_copy(w_hbm, w_ref, load_sem.at[0])
    load_tower = pltpu.make_async_copy(tower_hbm, tower_ref, load_sem.at[1])
    start = jnp.minimum(me * LOCAL // 128, CHANNELS // 128 - 2) * 128
    skip = me * LOCAL - start
    load_table = pltpu.make_async_copy(
        table_hbm.at[:, pl.ds(pl.multiple_of(start, 128), 256)], window, load_sem.at[2]
    )
    load_w.start()
    load_table.start()
    load_tower.start()

    barrier = pltpu.get_barrier_semaphore()
    for d in range(1, SIDE * SIDE):
        pl.semaphore_signal(barrier, inc=1, device_id={"tp": tpeer(d)}, device_id_type=MESH)
    for d in range(1, SEQ):
        pl.semaphore_signal(barrier, inc=1, device_id={"seq": speer(d)}, device_id_type=MESH)
    turn[...] = jnp.zeros((128, 128), F32)
    for k in range(3):
        turn[56 + 3 * k : 59 + 3 * k, 0:LOCAL] = gain_in[...]
    gain_ref[...] = turn[...].T[0:LOCAL]
    pl.semaphore_wait(barrier, SIDE * SIDE - 1 + SEQ - 1)

    pending = []

    def begin(copy):
        copy.start()
        pending.append(copy)

    def halo_left(src, dst, k):
        return remote(src.at[:, 0:128], dst.at[0], halo_send.at[k, 0], halo_recv.at[k, 0], {"seq": s - 1})

    def halo_right(src, dst, k):
        return remote(src.at[:, 384:512], dst.at[1], halo_send.at[k, 1], halo_recv.at[k, 1], {"seq": s + 1})

    def halo_start(src, dst, k):
        @pl.when(s > 0)
        def _():
            halo_left(src, dst, k).start()

        @pl.when(s < SEQ - 1)
        def _():
            halo_right(src, dst, k).start()

        @pl.when(s == 0)
        def _():
            dst[1] = jnp.zeros((LOCAL, 128), BF16)

        @pl.when(s == SEQ - 1)
        def _():
            dst[0] = jnp.zeros((LOCAL, 128), BF16)

    def halo_wait(src, dst, k):
        @pl.when(s > 0)
        def _():
            halo_left(src, dst, k).wait_send()
            remote(
                src.at[:, 384:512], dst.at[1], halo_send.at[k, 1], halo_recv.at[k, 1], {"seq": s - 1}
            ).wait_recv()

        @pl.when(s < SEQ - 1)
        def _():
            halo_right(src, dst, k).wait_send()
            remote(
                src.at[:, 0:128], dst.at[0], halo_send.at[k, 0], halo_recv.at[k, 0], {"seq": s + 1}
            ).wait_recv()

    lane = lax.broadcasted_iota(jnp.int32, (LOCAL, 128), 1)

    def halo_tile(dst):
        return jnp.where(lane < 64, dst[0].astype(F32), dst[1].astype(F32))

    halo_start(seq_ref, halo_rx, 0)

    gain = gain_ref[...]
    high = gain.astype(BF16).astype(F32)
    rest = gain - high
    mid = rest.astype(BF16).astype(F32)
    low = rest - mid
    packed = jnp.where(lane < 59, high, jnp.where(lane < 62, mid, low))
    in_gain = (lane >= 56) & (lane < 65)

    for h in range(2):
        gst[0, me, h, :, 0:512] = seq_ref[HALF * h : HALF * h + HALF, :]
    halo_wait(seq_ref, halo_rx, 0)
    tile = jnp.where(in_gain, packed, halo_tile(halo_rx)).astype(BF16)
    for h in range(2):
        gst[0, me, h, :, 512:640] = tile[HALF * h : HALF * h + HALF, :]

    col = lax.broadcasted_iota(jnp.int32, (LOCAL, WIN), 1)
    outside = ((s == SEQ - 1) & (col >= 512) & (col < 576)) | ((s == 0) & (col >= 576))

    def transpose_weights(layer):
        for x in range(SIDE):
            block = w_ref[layer, :, 384 * x : 384 * x + 384].astype(F32).T.astype(BF16)
            for y in range(SIDE):
                a = 192 * x + HALF * y
                b = 768 + 192 * y + HALF * x
                wt[layer, a : a + HALF, :] = block[96 * y : 96 * y + HALF]
                wt[layer, b : b + HALF, :] = block[96 * y + HALF : 96 * y + 96]

    def one_hot(rows, row_ids, base):
        ids = lax.broadcasted_iota(jnp.int32, (rows, JUNC), 0) + base
        return jnp.where(ids == row_ids, 1.0, 0.0).astype(BF16)

    def prepare_tissues():
        load_table.wait()
        tab[...] = jnp.zeros((384, 128), F32)
        tab[0 : window.shape[0], :] = pltpu.roll(window[...], lax.rem(256 - skip, 256), 1)[:, 0:128]
        table = tab[...].T[0:LOCAL]
        t_high = table.astype(BF16)
        t_rest = table - t_high.astype(F32)
        t_mid = t_rest.astype(BF16)
        t_low = (t_rest - t_mid.astype(F32)).astype(BF16)
        hot = one_hot(384, tissue_ref[...], 0)
        tissue_rows[...] = dot(t_high, hot) + dot(t_mid, hot) + dot(t_low, hot)
        donor_hot[...] = one_hot(LENGTH, donor_ref[...], 0)

    def send_meta():
        owner = owner_ref[...]
        member = one_hot(16, owner, 0)
        first = lax.broadcasted_iota(jnp.int32, (JUNC, JUNC), 0)
        second = lax.broadcasted_iota(jnp.int32, (JUNC, JUNC), 1)
        rank = dot(member, jnp.where(first <= second, 1.0, 0.0).astype(BF16))
        slot = jnp.sum(member.astype(F32) * rank, axis=0, keepdims=True) - 1.0
        slot = slot.astype(jnp.int32)
        meta_all[s] = (slot * SEQ + owner) * LENGTH + offset_ref[...]
        for d in range(1, SEQ):
            begin(
                remote(
                    meta_all.at[s], meta_all.at[s], meta_send.at[d - 1], meta_recv.at[d - 1], {"seq": speer(d)}
                )
            )
        ids = lax.broadcasted_iota(jnp.int32, (CAP, JUNC), 0)
        for d in range(SEQ):
            mine = (ids == slot) & (owner == speer(d))
            slots[CAP * d : CAP * d + CAP, :] = jnp.where(mine, 1.0, 0.0).astype(BF16)

    def wait_meta():
        for d in range(1, SEQ):
            src = speer(SEQ - d)
            remote(
                meta_all.at[src], meta_all.at[src], meta_send.at[d - 1], meta_recv.at[d - 1], {"seq": src}
            ).wait_recv()

    def prepare_picks(which):
        for d in which:
            row = meta_all[speer(d)]
            place = one_hot(LENGTH, row & (SEQ * LENGTH - 1), s * LENGTH)
            slot = one_hot(CAP, lax.shift_right_logical(row, 12), 0)
            pick[:, CAP * d : CAP * d + CAP] = dot_rows(place, slot).astype(BF16)

    for layer in range(LAYERS):
        reach = 2 ** (layer + 3)
        count = [0]

        def go(block, h, peer, layer=layer, count=count):
            begin(
                remote(
                    gst.at[layer, block, h],
                    gst.at[layer, block, h],
                    gather_send.at[layer, count[0]],
                    gather_recv.at[layer, block, h],
                    {"tp": peer},
                )
            )
            count[0] += 1

        def arrived(block, h, layer=layer):
            remote(
                gst.at[layer, block, h],
                gst.at[layer, block, h],
                gather_send.at[layer, 0],
                gather_recv.at[layer, block, h],
                {"tp": xpeer(1)},
            ).wait_recv()

        squares = jnp.concatenate([gst[layer, me, 0], gst[layer, me, 1]], axis=0).astype(F32)
        pw[layer, me] = jnp.sum(squares * squares, axis=0, keepdims=True)
        for d in range(1, SIDE * SIDE):
            begin(
                remote(
                    pw.at[layer, me],
                    pw.at[layer, me],
                    pw_send.at[layer, d - 1],
                    pw_recv.at[layer, d - 1],
                    {"tp": tpeer(d)},
                )
            )
        def at(h, p, q):
            dx, dy = (p, q) if h == 0 else (q, p)
            return lax.rem(mx + dx, SIDE) * SIDE + lax.rem(my + dy, SIDE)

        waited = set()

        def wait_block(h, p, q, at=at, waited=waited, arrived=arrived):
            if (h, p, q) not in waited:
                waited.add((h, p, q))
                arrived(at(h, p, q), h)

        def relay(h, p, q, targets, at=at, go=go, wait_block=wait_block):
            if (p, q) != (0, 0):
                wait_block(h, p, q)
            for target in targets:
                go(at(h, p, q), h, at(h, *target))

        def second_axis(p, relay=relay):
            for h in range(2):
                if p % 2 == 0:
                    relay(h, p, 3, ((0, 1),))
                else:
                    relay(h, p, 1, ((0, 3),))

        ahead = (3, 1)
        for h in range(2):
            relay(h, 0, 0, ((1, 0), (3, 0)))
        for h in range(2):
            relay(h, 0, 0, ((0, 1), (0, 3)))
        for h in range(2):
            relay(h, ahead[h], 0, ((SIDE - ahead[h], 0), (0, 1), (0, 3)))
        for h in range(2):
            relay(h, SIDE - ahead[h], 0, ((0, 1), (0, 3)))
        second_axis(0)
        if layer == 0:
            send_meta()
            load_w.wait()
        else:
            vv[layer - 1] = dot(w_ref[layer - 1], mm[layer - 1])
        for h in range(2):
            relay(h, 2, 0, ((0, 1), (0, 3)))
        second_axis(1)
        second_axis(3)

        for d in range(1, SIDE * SIDE):
            src = pw.at[layer, tpeer(SIDE * SIDE - d)]
            remote(
                src, src, pw_send.at[layer, d - 1], pw_recv.at[layer, d - 1], {"tp": tpeer(d)}
            ).wait_recv()
        power = jnp.sum(pw[layer], axis=0) / CHANNELS
        inverse = 1.0 / jnp.sqrt(power + EPSILON)
        inv[layer] = jnp.broadcast_to(inverse, (8, WIN))

        def hide(block, carry, layer=layer):
            scale = inv[layer, 0:1, :]
            for h in range(2):
                head = gst[0, block, h, :, 512:640].astype(F32)
                g = (
                    head[:, 56 + layer : 57 + layer]
                    + head[:, 59 + layer : 60 + layer]
                    + head[:, 62 + layer : 63 + layer]
                )
                rows = pl.ds(pl.multiple_of(block * LOCAL + HALF * h, 16), HALF)
                raw = gst[layer, block, h, :, 0:LENGTH].astype(F32) * g
                x = raw * scale[:, 0:LENGTH]
                xx = x * x
                t = jnp.tanh(GELU_C * (x + GELU_A * (xx * x)))
                upper = 0.5 * (1.0 + t)
                hid[layer, rows, 0:LENGTH] = (x * upper).astype(BF16)
                slope = upper + (0.5 * x) * (1.0 - t * t) * (GELU_C + (3.0 * GELU_A * GELU_C) * xx)
                mm[layer, rows, :] = (raw * slope).astype(BF16)
                x = gst[layer, block, h, :, LENGTH:WIN].astype(F32) * scale[:, LENGTH:WIN] * g
                t = jnp.tanh(GELU_C * (x + GELU_A * (x * x * x)))
                hid[layer, rows, LENGTH:WIN] = (0.5 * x * (1.0 + t)).astype(BF16)
            return carry

        for d in (0,) + NEAR:
            group = lax.rem(mx + d, SIDE)
            for e in (0,) + NEAR:
                if d + e > 0:
                    wait_block(0, d, e)
                    wait_block(1, e, d)
                if d == NEAR[-1]:
                    hide(group * SIDE + lax.rem(my + e, SIDE), 0)
            if d != NEAR[-1]:
                lax.fori_loop(group * SIDE, group * SIDE + SIDE, hide, 0)
            span = pl.ds(pl.multiple_of(group * 384, 128), 384)
            part = dot(w_ref[layer, :, span], hid[layer, span, :])
            if d == 0:
                ysum[...] = part
                second_axis(2)
                transpose_weights(layer)
                if layer == 0:
                    prepare_tissues()
                if layer == 1:
                    wait_meta()
                    prepare_picks(range(0, 4))
                if layer == 2:
                    prepare_picks(range(4, 8))
            elif d != NEAR[-1]:
                ysum[...] += part
            else:
                y = ysum[...] + part

        mixed = pltpu.roll(y[0:96], reach, 1) + y[96:192] + pltpu.roll(y[192:288], WIN - reach, 1)
        own = jnp.concatenate([gst[layer, me, 0], gst[layer, me, 1]], axis=0)
        state = own.astype(F32) + mixed
        if layer < LAYERS - 1:
            state = jnp.where(outside, 0.0, state).astype(BF16)
            for h in range(2):
                gst[layer + 1, me, h] = state[HALF * h : HALF * h + HALF, :]
        else:
            state3[...] = state[:, 0:LENGTH].astype(BF16)

    def acc_copy(d):
        return remote(
            acc_tx.at[:, CAP * d : CAP * d + CAP],
            acc_rx.at[:, CAP * (SEQ - d) : CAP * (SEQ - d) + CAP],
            acc_send.at[d - 1],
            acc_recv.at[d - 1],
            {"seq": speer(d)},
        )

    def ab_copy(d):
        return remote(
            ab_tx.at[:, CAP * d : CAP * d + CAP],
            ab_rx.at[:, CAP * (SEQ - d) : CAP * (SEQ - d) + CAP],
            ab_send.at[d - 1],
            ab_recv.at[d - 1],
            {"seq": speer(d)},
        )

    acc_tx[...] = dot(state3[...], pick[...]).astype(BF16)
    for d in range(1, SEQ):
        begin(acc_copy(d))
    acc_rx[:, 0:CAP] = acc_tx[:, 0:CAP]
    donor = dot(state3[...], donor_hot[...])
    load_tower.wait()
    weight_j = sgrad_ref[...] / ROOT
    rows_q = tissue_rows[...]
    accept_back = (weight_j * donor * rows_q).astype(BF16)
    ab_tx[...] = dot_rows(accept_back, slots[...]).astype(BF16)
    for d in range(1, SEQ):
        begin(ab_copy(d))
    ab_rx[:, 0:CAP] = ab_tx[:, 0:CAP]
    vv[LAYERS - 1] = dot(w_ref[LAYERS - 1], mm[LAYERS - 1])
    for d in range(1, SEQ):
        acc_copy(d).wait_recv()
    accept = dot(acc_rx[...], slots[...])
    donor_back = weight_j * accept * rows_q
    d_high = donor_back.astype(BF16)
    d_low = (donor_back - d_high.astype(F32)).astype(BF16)
    up[...] = tower_ref[...] + dot_rows(d_high, donor_hot[...]) + dot_rows(d_low, donor_hot[...])
    sc_all[me] = jnp.sum(donor * accept * rows_q, axis=0, keepdims=True) / ROOT
    for d in range(1, SEQ):
        ab_copy(d).wait_recv()
    up[...] += dot_rows(ab_rx[...], pick[...])
    for d in range(1, SIDE * SIDE):
        begin(
            remote(sc_all.at[me], sc_all.at[me], sc_send.at[d - 1], sc_recv.at[d - 1], {"tp": tpeer(d)})
        )

    def w_cores(layer):
        return remote(
            wg.at[layer, 1 - core], wrx.at[layer], w_send.at[layer, 0], w_recv.at[layer, 0], {"seq": partner}
        )

    def w_slices(layer, d):
        return remote(
            wz_tx.at[layer, lax.rem(mz + d, SIDE)],
            wz_rx.at[layer, d - 1],
            w_send.at[layer, d],
            w_recv.at[layer, d],
            {"seq": zpeer(d)},
        )

    def w_result(layer, d):
        return remote(
            wres.at[layer, core, mz],
            wres.at[layer, core, mz],
            w_send.at[layer, 3 + d],
            w_recv.at[layer, 3 + d],
            {"seq": zpeer(d)},
        )

    def w_share(layer, d):
        part = wres.at[layer, core, lax.rem(mz + SIDE - d, SIDE)]
        return remote(part, part, w_send.at[layer, 7 + d], w_recv.at[layer, 7 + d], {"seq": partner})

    def w_step2(layer):
        w_cores(layer).wait_recv()
        summed = wg[layer, core].astype(F32) + wrx[layer].astype(F32)
        for q in range(SIDE):
            wz_tx[layer, q] = summed[:, 384 * q : 384 * q + 384].astype(BF16)
        for d in NEAR:
            begin(w_slices(layer, d))

    def w_step3(layer):
        result = wz_tx[layer, mz].astype(F32)
        for d in NEAR:
            w_slices(layer, d).wait_recv()
            result = result + wz_rx[layer, d - 1].astype(F32)
        wres[layer, core, mz] = result.astype(BF16)
        for d in NEAR:
            begin(w_result(layer, d))
        begin(w_share(layer, 0))

    def w_step4(layer):
        for d in NEAR:
            src = wres.at[layer, core, lax.rem(mz + SIDE - d, SIDE)]
            remote(
                src, src, w_send.at[layer, 3 + d], w_recv.at[layer, 3 + d], {"seq": zpeer(d)}
            ).wait_recv()
            begin(w_share(layer, d))

    def store_w(layer):
        return pltpu.make_async_copy(wres.at[layer], wgrad_ref.at[layer], load_sem.at[3 + layer])

    def w_step5(layer):
        for d in range(SIDE):
            part = wres.at[layer, 1 - core, lax.rem(mz + SIDE - d, SIDE)]
            remote(
                part, part, w_send.at[layer, 7 + d], w_recv.at[layer, 7 + d], {"seq": partner}
            ).wait_recv()
        store_w(layer).start()

    gg[...] = jnp.zeros((128, 128), F32)
    for layer in reversed(range(LAYERS)):
        reach = 2 ** (layer + 3)
        shifts = (WIN - reach, 0, reach)
        gbuf[layer] = up[...].astype(BF16)
        halo_start(gbuf.at[layer], halo_b.at[layer], layer + 1)
        g = gbuf[layer].astype(F32)

        def shifted(window, shifts=shifts):
            rolled = [pltpu.roll(window, k, 1) if k else window for k in shifts]
            return jnp.concatenate(rolled, axis=0)

        inner_g = shifted(jnp.concatenate([g, jnp.zeros((LOCAL, 128), F32)], axis=1)).astype(BF16)

        def chunk(h, index, window, layer=layer):
            rows = pl.ds(pl.multiple_of(768 * h + 192 * index, 16), 192)
            return dot(wt[layer, rows, :], window)

        def rs_one(h, c, d, layer=layer):
            return remote(
                pab.at[layer, h, c, d - 1],
                rx.at[layer, h, c, d - 1],
                rs_send.at[layer, h, c, d - 1],
                rs_recv.at[layer, h, c, d - 1],
                {"tp": xpeer(d) if h == 0 else ypeer(d)},
            )

        def rs_two(h, c, d, layer=layer):
            index = lax.rem((my if h == 0 else mx) + d, SIDE)
            return remote(
                sab.at[layer, h, c, index],
                ry.at[layer, h, c, d - 1],
                rs_send.at[layer, h, c, 2 + d],
                rs_recv.at[layer, h, c, 2 + d],
                {"tp": ypeer(d) if h == 0 else xpeer(d)},
            )

        def partials(c, window, layer=layer, chunk=chunk, rs_one=rs_one):
            for d in (2, 1, 3):
                for h in range(2):
                    base = mx if h == 0 else my
                    pab[layer, h, c, d - 1] = chunk(h, lax.rem(base + d, SIDE), window).astype(BF16)
                    begin(rs_one(h, c, d))
            for h in range(2):
                own = chunk(h, mx if h == 0 else my, window)
                sf[h, c] = own.reshape(SIDE, HALF, 256)

        partials(0, inner_g[:, 128:384])
        for q in range(3):
            part = dot_rows(inner_g, hid[layer, 512 * q : 512 * q + 512, :]).astype(BF16)
            for h in range(2):
                wg[layer, h, :, 512 * q : 512 * q + 512] = part[144 * h : 144 * h + 144]
        begin(w_cores(layer))
        halo_wait(gbuf.at[layer], halo_b.at[layer], layer + 1)
        full_g = shifted(jnp.concatenate([g, halo_tile(halo_b.at[layer])], axis=1))
        full_g = full_g[:, 0:LENGTH]
        partials(1, jnp.concatenate([full_g[:, 0:128], full_g[:, 384:512]], axis=1).astype(BF16))
        inn[layer, me] = jnp.sum(full_g * vv[layer], axis=0, keepdims=True)
        for d in range(1, SIDE * SIDE):
            begin(
                remote(
                    inn.at[layer, me],
                    inn.at[layer, me],
                    inn_send.at[layer, d - 1],
                    inn_recv.at[layer, d - 1],
                    {"tp": tpeer(d)},
                )
            )
        if layer < LAYERS - 1:
            w_step4(layer + 1)
        w_step2(layer)
        for c in range(2):
            for h in range(2):
                for d in NEAR:
                    rs_one(h, c, d).wait_recv()
                    sf[h, c] += rx[layer, h, c, d - 1].astype(F32).reshape(SIDE, HALF, 256)
                sab[layer, h, c] = sf[h, c].astype(BF16)
                for d in NEAR:
                    begin(rs_two(h, c, d))
            if c == 0 and layer == 0:
                w_step3(layer)
        if layer > 0:
            w_step3(layer)
        if layer < LAYERS - 1:
            w_step5(layer + 1)

        x = (seq_ref[...] if layer == 0 else jnp.concatenate(
            [gst[layer, me, 0, :, 0:LENGTH], gst[layer, me, 1, :, 0:LENGTH]], axis=0
        )).astype(F32)
        scale = inv[layer, 0:1, 0:LENGTH]
        g_col = gain_ref[:, 56 + layer : 57 + layer]
        norm = x * scale
        pre = norm * g_col
        t = jnp.tanh(GELU_C * (pre + GELU_A * (pre * pre * pre)))
        slope = 0.5 * (1.0 + t) + 0.5 * pre * (1.0 - t * t) * (
            GELU_C * (1.0 + 3.0 * GELU_A * (pre * pre))
        )
        halves = []
        for h in range(2):
            sides = []
            for c in range(2):
                back = sf[h, c, my if h == 0 else mx]
                for d in NEAR:
                    rs_two(h, c, d).wait_recv()
                    back = back + ry[layer, h, c, d - 1].astype(F32)
                sides.append(back)
            middle, edges = sides
            halves.append(jnp.concatenate([edges[:, 0:128], middle, edges[:, 128:256]], axis=1))
        back_pre = jnp.concatenate(halves, axis=0) * slope
        back_norm = back_pre * g_col
        gain_col = jnp.sum(back_pre * norm, axis=1, keepdims=True)
        gg[0:LOCAL, :] = jnp.where(lane == layer, gain_col, gg[0:LOCAL, :])
        if layer == 0:
            gg_all[s] = gg[...].T[0:8]
            for d in range(1, SEQ):
                begin(
                    remote(
                        gg_all.at[s], gg_all.at[s], gg_send.at[d - 1], gg_recv.at[d - 1], {"seq": speer(d)}
                    )
                )
        for d in range(1, SIDE * SIDE):
            src = inn.at[layer, tpeer(SIDE * SIDE - d)]
            remote(
                src, src, inn_send.at[layer, d - 1], inn_recv.at[layer, d - 1], {"tp": tpeer(d)}
            ).wait_recv()
        inner = jnp.sum(inn[layer], axis=0)
        up[...] = up[...] + scale * back_norm - x * (scale * scale * scale) * (inner / CHANNELS)

    grad_ref[...] = up[...]
    w_step4(0)
    for d in range(1, SIDE * SIDE):
        src = sc_all.at[tpeer(SIDE * SIDE - d)]
        remote(src, src, sc_send.at[d - 1], sc_recv.at[d - 1], {"tp": tpeer(d)}).wait_recv()
    scores_ref[...] = jnp.sum(sc_all[...], axis=0)
    for d in range(1, SEQ):
        src = gg_all.at[speer(SEQ - d)]
        remote(src, src, gg_send.at[d - 1], gg_recv.at[d - 1], {"seq": speer(d)}).wait_recv()
    gains_ref[...] = jnp.sum(gg_all[...], axis=0)[0:LAYERS, 0:LOCAL]
    w_step5(0)
    for layer in range(LAYERS):
        store_w(layer).wait()
    for copy in pending:
        copy.wait_send()


def dma(*shape):
    return pltpu.SemaphoreType.DMA(shape)


def section(*operands):
    vmem = pl.BlockSpec(memory_space=pltpu.VMEM)
    hbm = pl.BlockSpec(memory_space=pl.ANY)
    return pl.pallas_call(
        section_kernel,
        out_shape=(
            jax.ShapeDtypeStruct((1, JUNC), F32),
            jax.ShapeDtypeStruct((LOCAL, LENGTH), F32),
            jax.ShapeDtypeStruct((LAYERS, 2, SIDE, 144, 384), BF16),
            jax.ShapeDtypeStruct((LAYERS, LOCAL), F32),
        ),
        in_specs=[vmem, hbm, vmem, hbm, hbm] + [vmem] * 5,
        out_specs=(vmem, vmem, hbm, vmem),
        scratch_shapes=[
            pltpu.VMEM((LAYERS, 3 * LOCAL, CHANNELS), BF16),
            pltpu.VMEM((LOCAL, LENGTH), F32),
            pltpu.VMEM((LOCAL, 128), F32),
            pltpu.VMEM((367, 256), F32),
            pltpu.VMEM((128, 128), F32),
            pltpu.VMEM((384, 128), F32),
            pltpu.VMEM((LAYERS, 16, 2, HALF, WIN), BF16),
            pltpu.VMEM((LAYERS, CHANNELS, WIN), BF16),
            pltpu.VMEM((LAYERS, CHANNELS, LENGTH), BF16),
            pltpu.VMEM((LAYERS, 3 * LOCAL, LENGTH), F32),
            pltpu.VMEM((3 * LOCAL, WIN), F32),
            pltpu.VMEM((LAYERS, 16, 1, WIN), F32),
            pltpu.VMEM((LAYERS, 8, WIN), F32),
            pltpu.VMEM((LAYERS, CHANNELS, 3 * LOCAL), BF16),
            pltpu.VMEM((SEQ, 1, JUNC), jnp.int32),
            pltpu.VMEM((LENGTH, SEQ * CAP), BF16),
            pltpu.VMEM((SEQ * CAP, JUNC), BF16),
            pltpu.VMEM((LENGTH, JUNC), BF16),
            pltpu.VMEM((LOCAL, JUNC), F32),
            pltpu.VMEM((LOCAL, LENGTH), BF16),
            pltpu.VMEM((LOCAL, SEQ * CAP), BF16),
            pltpu.VMEM((LOCAL, SEQ * CAP), BF16),
            pltpu.VMEM((LOCAL, SEQ * CAP), BF16),
            pltpu.VMEM((LOCAL, SEQ * CAP), BF16),
            pltpu.VMEM((16, 1, JUNC), F32),
            pltpu.VMEM((LOCAL, LENGTH), F32),
            pltpu.VMEM((LAYERS, LOCAL, LENGTH), BF16),
            pltpu.VMEM((2, LOCAL, 128), BF16),
            pltpu.VMEM((LAYERS, 2, LOCAL, 128), BF16),
            pltpu.VMEM((LAYERS, 2, 2, 3, 192, 256), BF16),
            pltpu.VMEM((LAYERS, 2, 2, 3, 192, 256), BF16),
            pltpu.VMEM((2, 2, SIDE, HALF, 256), F32),
            pltpu.VMEM((LAYERS, 2, 2, SIDE, HALF, 256), BF16),
            pltpu.VMEM((LAYERS, 2, 2, 3, HALF, 256), BF16),
            pltpu.VMEM((LAYERS, 16, 1, LENGTH), F32),
            pltpu.VMEM((LAYERS, 2, 144, CHANNELS), BF16),
            pltpu.VMEM((LAYERS, 144, CHANNELS), BF16),
            pltpu.VMEM((LAYERS, SIDE, 144, 384), BF16),
            pltpu.VMEM((LAYERS, 3, 144, 384), BF16),
            pltpu.VMEM((LAYERS, 2, SIDE, 144, 384), BF16),
            pltpu.VMEM((128, 128), F32),
            pltpu.VMEM((SEQ, 8, 128), F32),
            dma(4, 2),
            dma(4, 2),
            dma(LAYERS, 30),
            dma(LAYERS, 16, 2),
            dma(7),
            dma(7),
            dma(7),
            dma(7),
            dma(7),
            dma(7),
            dma(15),
            dma(15),
            dma(LAYERS, 2, 2, 6),
            dma(LAYERS, 2, 2, 6),
            dma(LAYERS, 15),
            dma(LAYERS, 15),
            dma(LAYERS, 11),
            dma(LAYERS, 11),
            dma(7),
            dma(7),
            dma(LAYERS, 15),
            dma(LAYERS, 15),
            dma(6),
        ],
        compiler_params=pltpu.CompilerParams(
            collective_id=0, has_side_effects=True, vmem_limit_bytes=62 * 1024 * 1024
        ),
        name="conv_section",
    )(*operands)


def finish_kernel(
    w_in, scores_in, grad_in, gains_in, w_out, scores_out, grad_out, gains_out, wb, wf, sb, gb, nb, sem
):
    small = ((scores_in, sb, scores_out), (grad_in, gb, grad_out), (gains_in, nb, gains_out))
    loads = [pltpu.make_async_copy(w_in.at[k], wb.at[k], sem.at[k]) for k in range(LAYERS)]
    for k, (source, buffer, _) in enumerate(small):
        loads.append(pltpu.make_async_copy(source, buffer, sem.at[LAYERS + k]))
    for load in loads:
        load.start()
    stores = []
    for k in range(LAYERS):
        loads[k].wait()
        for h in range(2):
            for q in range(SIDE):
                wf[k, 144 * h : 144 * h + 144, 384 * q : 384 * q + 384] = wb[k, h, q].astype(F32)
            rows = pl.ds(144 * h, 144)
            store = pltpu.make_async_copy(wf.at[k, rows], w_out.at[k, rows], sem.at[6 + 2 * k + h])
            store.start()
            stores.append(store)
    for k, (_, buffer, target) in enumerate(small):
        loads[LAYERS + k].wait()
        store = pltpu.make_async_copy(buffer, target, sem.at[12 + k])
        store.start()
        stores.append(store)
    for store in stores:
        store.wait()


def finish(weights, scores, grad, gains):
    hbm = pl.BlockSpec(memory_space=pl.ANY)
    return pl.pallas_call(
        finish_kernel,
        out_shape=(
            jax.ShapeDtypeStruct((LAYERS, 3 * LOCAL, CHANNELS), F32),
            jax.ShapeDtypeStruct(scores.shape, F32),
            jax.ShapeDtypeStruct(grad.shape, F32),
            jax.ShapeDtypeStruct(gains.shape, F32),
        ),
        in_specs=[hbm] * 4,
        out_specs=(hbm,) * 4,
        scratch_shapes=[
            pltpu.VMEM(weights.shape, BF16),
            pltpu.VMEM((LAYERS, 3 * LOCAL, CHANNELS), F32),
            pltpu.VMEM(scores.shape, F32),
            pltpu.VMEM(grad.shape, F32),
            pltpu.VMEM(gains.shape, F32),
            dma(15),
        ],
        name="finish",
    )(weights, scores, grad, gains)


def local(
    sequence_in,
    conv_weight,
    norm_gain,
    tissue_scale,
    donor_offset,
    acceptor_owner,
    acceptor_offset,
    tissue,
    tower_grad,
    score_grad,
):
    stacked = conv_weight.transpose(0, 2, 1, 3).reshape(LAYERS, 3 * LOCAL, CHANNELS)
    scores, grad, weights, gains = section(
        sequence_in,
        stacked,
        norm_gain,
        tower_grad,
        tissue_scale,
        acceptor_owner.T,
        acceptor_offset[None, :],
        donor_offset[None, :],
        tissue[None, :],
        score_grad[None, :],
    )
    weights, scores, grad, gains = finish(weights, scores, grad, gains)
    weights = weights.reshape(LAYERS, 3, LOCAL, CHANNELS).transpose(0, 2, 1, 3)
    return (scores[0], grad, weights, gains)


def solution(mesh):
    return jax.shard_map(
        local,
        mesh=mesh,
        in_specs=(
            P("tp", "seq"),
            P(None, "tp", None, None),
            P(None, "tp"),
            P(),
            P("seq"),
            P("seq", None),
            P("seq"),
            P("seq"),
            P("tp", "seq"),
            P("seq"),
        ),
        out_specs=(P("seq"), P("tp", "seq"), P(None, "tp", None, None), P(None, "tp")),
        check_vma=False,
    )
```
